256 devices in a mesh: samp: 64 (over z, x, core), snp: 4 (over y).
Axes of the slice: x: 4, y: 4, z: 8, core: 2. Of those that a mesh axis runs over, the one named last changes fastest.
Arguments:
- genotype: int32 [40960, 4096], P('samp', 'snp'), may hold values from 0 to 2
- freqs: float32 [4096], P('snp'), may hold values from 0.35 to 0.65
- left_factors: float32 [40960, 20], P('samp'), may hold values from -6 to 6
- singular: float32 [20], replicated, may hold values from 0.5 to 2
- right_factors: float32 [4096, 20], P(('snp', 'samp')), may hold values from -1.25 to 1.25
- sketch: bfloat16 [4096, 64], P('snp'), may hold values from -6 to 6
- batch_sizes: int32 [12], replicated, may hold values from 1 to 6826, 40960 in all
- missing_batch: int32 [48], replicated, may hold values from 0 to 11, as said below
- missing_block: int32 [48], replicated, may hold values from 0 to 15, as said below
Outputs:
- basis: float32 [40960, 64], P('samp')
- projection: float32 [4096, 64], P('snp')
- snp_basis: float32 [4096, 64], P('snp')
The draws below stay inside these ranges and needn't reach their ends.
Inputs may be any that keep to these rules, and one draw needn't show every extreme that they name: The pairs (missing_batch, missing_block) are distinct; every block id appears exactly 3 times and every batch id exactly 48 // 12 times. `missing_block`: paired entry by entry with missing_batch.
All inputs are finite; a program needn't handle non-finite values.
Results may differ from the reference program's by a relative error of at most 0.012.
Values may be sent and summed in bfloat16 or wider, within the bound.
No kernel may reach another device: no remote copies, remote signals or barrier semaphores. Data moves between devices by JAX's collectives and lax.ppermute only.
A program may use at most 64 MiB of HBM per device.

```python
import math
import jax
import jax.numpy as jnp
import numpy as np
from jax import lax

SNPS = 4096
RANK = 20
SKETCH = 64
BATCHES = 12
BLOCK = 256
ITERS = 2
ROWS_DEV = 640
BLOCKS = 16
MISS = 48
NSAMP = 40960


def missing_tiles(key):
    offset = jax.random.randint(jax.random.fold_in(key, 11), (), 0, BATCHES)
    order = jax.random.permutation(jax.random.fold_in(key, 12), MISS).astype(jnp.int32)
    block_ids = order // 3
    turn = order % 3
    batch_ids = (offset + block_ids + BATCHES // 3 * turn) % BATCHES
    return (batch_ids.astype(jnp.int32), block_ids.astype(jnp.int32))


def draw_missing_batch(key, part):
    return missing_tiles(key)[0]


def draw_missing_block(key, part):
    return missing_tiles(key)[1]


def draw_genotype(key, part):
    populations = jax.random.randint(jax.random.fold_in(key, 21), (NSAMP,), 0, 4).astype(jnp.int32)
    base_rate = jax.random.randint(jax.random.fold_in(key, 22), (SNPS,), 350, 651).astype(jnp.int32)
    shifts = jax.random.randint(jax.random.fold_in(key, 23), (4, SNPS), -150, 151).astype(jnp.int32)
    permille = base_rate[None, :] + shifts[populations]
    pairs = jax.random.randint(jax.random.fold_in(key, 24), (NSAMP, SNPS), 0, 1000000).astype(jnp.int32)
    first = (pairs // 1000 < permille).astype(jnp.int32)
    second = (pairs % 1000 < permille).astype(jnp.int32)
    return (first + second).astype(jnp.int32)


def block_scale(rng, extent, split, least, top_value):
    factor_of, own = 1.0, jax.random.fold_in(rng, 6)
    for axis_at, blocks in split:
        draws = jnp.exp(jax.random.uniform(jax.random.fold_in(own, axis_at), (blocks,), jnp.float32, least / len(split), top_value / len(split)))
        factor_of = factor_of * jnp.repeat(draws, extent[axis_at] // blocks).reshape([-1 if axis == axis_at else 1 for axis in range(len(extent))])
    return factor_of


def length_profile(count, total, most, skew):
    loads = [(1 << 20) // math.isqrt(grade ** skew) + 1 for grade in range(2, count + 1)]
    spare, given = total - most - (count - 1), [1] * (count - 1)
    while spare > 0:
        movable = [i for i in range(count - 1) if given[i] < most]
        whole, budget = sum([loads[i] for i in movable]), spare
        for i in movable:
            more = min(most - given[i], max(1, budget * loads[i] // whole), spare)
            given[i] = given[i] + more
            spare = spare - more
    return np.array([most] + given)


def uneven(key, amount, total, reach, lean):
    if amount == 2:
        one = jax.random.randint(key, (), max(1, total - reach), min(reach, total - 1) + 1)
        return jnp.stack([one, total - one])
    sizes = jnp.asarray(length_profile(amount, total, reach, lean), jnp.int32)
    pairs = (amount - 1) // 2
    source_of, receiver = sizes[1:1 + 2 * pairs:2], sizes[2:2 + 2 * pairs:2]
    room = jnp.minimum(source_of - 1, reach - receiver)
    moved = jax.random.randint(jax.random.fold_in(key, 1), (pairs,), 0, 1 << 20) % (room + 1)
    sizes = sizes.at[1:1 + 2 * pairs:2].set(source_of - moved).at[2:2 + 2 * pairs:2].set(receiver + moved)
    return sizes[jax.random.permutation(jax.random.fold_in(key, 2), amount)]


def normal_values(stream_key, extent, width, bound, cuts=(), held_as=jnp.bfloat16):
    entries = jax.random.normal(stream_key, extent, jnp.float32) * width
    if len(cuts) > 0:
        entries = block_scale(stream_key, extent, cuts, -0.22, 0.18) * entries
    return jnp.clip(entries, min=-bound, max=bound).astype(held_as)


def setup_inputs(seed: int = 0) -> dict:
    splits = jax.random.split(jax.random.key(seed), 10)
    return {
        "genotype": draw_genotype(jax.random.fold_in(splits[9], 71), 0),
        "freqs": jnp.clip(0.35 + 0.29999998 * jax.random.uniform(splits[1], (SNPS,), jnp.float32) ** block_scale(splits[1], (SNPS,), ((0, 4),), -0.2, 0.2), 0.35, 0.65),
        "left_factors": normal_values(splits[2], (NSAMP, RANK), 1.0, 6.0, ((0, 64),), jnp.float32),
        "singular": jnp.clip(jnp.exp(jax.random.uniform(splits[3], (RANK,), jnp.float32, math.log(0.5), math.log(2.0))), 0.5, 2.0),
        "right_factors": normal_values(splits[4], (SNPS, RANK), RANK ** -0.5, 1.25, ((0, 256),), jnp.float32),
        "sketch": normal_values(splits[5], (SNPS, SKETCH), 1.0, 6.0, ((0, 4),)),
        "batch_sizes": uneven(splits[6], BATCHES, NSAMP, NSAMP // 6, 2).astype(jnp.int32),
        "missing_batch": draw_missing_batch(jax.random.fold_in(splits[9], 71), 0),
        "missing_block": draw_missing_block(jax.random.fold_in(splits[9], 71), 0),
    }


def orthonormal(values, total):
    gram = jnp.dot(values.T, values, precision=lax.Precision.HIGHEST) / total
    lower = jnp.linalg.cholesky(gram)
    return jax.scipy.linalg.solve_triangular(lower, values.T, lower=True).T

def orthonormal_reversed(values, total):
    return orthonormal(values[:, ::-1], total)[:, ::-1]

def reference(genotype, freqs, left_factors, singular, right_factors, sketch, batch_sizes, missing_batch, missing_block):
    batch_range = jnp.arange(BATCHES, dtype=jnp.int32)
    block_range = jnp.arange(BLOCKS, dtype=jnp.int32)
    hot_batch = (missing_batch[:, None] == batch_range[None, :]).astype(jnp.float32)
    hot_block = (missing_block[:, None] == block_range[None, :]).astype(jnp.float32)
    table = jnp.dot(hot_batch.T.astype(jnp.float32), hot_block.astype(jnp.float32), preferred_element_type=jnp.float32)
    ends = jnp.cumsum(batch_sizes).astype(jnp.int32)
    col_block = (jnp.arange(SNPS, dtype=jnp.int32) // BLOCK).astype(jnp.int32)
    col_hot = (col_block[None, :] == block_range[:, None]).astype(jnp.float32)
    weighted = left_factors * singular[None, :]

    def build(index):
        start = (index * ROWS_DEV).astype(jnp.int32)
        geno_rows = lax.dynamic_slice_in_dim(genotype, start, ROWS_DEV, 0)
        weight_rows = lax.dynamic_slice_in_dim(weighted, start, ROWS_DEV, 0)
        row_ids = start + jnp.arange(ROWS_DEV, dtype=jnp.int32)
        batch_of = lax.optimization_barrier(jnp.sum((row_ids[:, None] >= ends[None, :]).astype(jnp.int32), axis=1)).astype(jnp.int32)
        row_hot = (batch_of[:, None] == batch_range[None, :]).astype(jnp.float32)
        missing = jnp.dot(jnp.dot(row_hot.astype(jnp.float32), table.astype(jnp.float32), preferred_element_type=jnp.float32).astype(jnp.float32), col_hot.astype(jnp.float32), preferred_element_type=jnp.float32) > 0.5
        lowrank = jnp.dot(weight_rows, right_factors.T, precision=lax.Precision.HIGHEST)
        observed = geno_rows.astype(jnp.float32) - 2.0 * freqs[None, :]
        return jnp.where(missing, lowrank, observed).astype(jnp.bfloat16)
    pieces = lax.map(build, jnp.arange(NSAMP // ROWS_DEV, dtype=jnp.int32))
    matrix = pieces.reshape(NSAMP, SNPS)
    basis = orthonormal(jnp.dot(matrix.astype(jnp.float32), sketch.astype(jnp.float32), preferred_element_type=jnp.float32), NSAMP)
    column_basis = jnp.zeros((SNPS, SKETCH), jnp.float32)
    for sweep_index in range(ITERS):
        columns = jnp.dot(matrix.T.astype(jnp.float32), basis.astype(jnp.bfloat16).astype(jnp.float32), preferred_element_type=jnp.float32)
        column_basis = orthonormal_reversed(columns, SNPS)
        basis = orthonormal(jnp.dot(matrix.astype(jnp.float32), column_basis.astype(jnp.bfloat16).astype(jnp.float32), preferred_element_type=jnp.float32), NSAMP)
    projection = jnp.dot(matrix.T.astype(jnp.float32), basis.astype(jnp.bfloat16).astype(jnp.float32), preferred_element_type=jnp.float32) / math.sqrt(NSAMP)
    return (basis, projection, column_basis)
```

```python
import math

import jax
import jax.numpy as jnp
from jax import lax
from jax.sharding import PartitionSpec as P

BATCHES = 12
BLOCK = 256
ITERS = 2
BLOCKS = 16
TILE = (8, 128)
HIGH = lax.Precision.HIGHEST


def exact_dot(a, b, contract):
    return lax.dot_general(a, b, (contract, ((), ())), precision=HIGH)


def split_dot(values, matrix, dim):
    high = values.astype(jnp.bfloat16)
    low = (values - high.astype(jnp.float32)).astype(jnp.bfloat16)
    both = jnp.concatenate([high, low], axis=0)
    out = lax.dot_general(
        both, matrix, (((1,), (dim,)), ((), ())), preferred_element_type=jnp.float32
    )
    rows = values.shape[0]
    return out[:rows] + out[rows:]


def lower_inverse(gram):
    lower = jnp.linalg.cholesky(gram)
    eye = jnp.eye(gram.shape[0], dtype=gram.dtype)
    return jax.scipy.linalg.solve_triangular(lower, eye, lower=True)


def upper_inverse(gram):
    return lower_inverse(gram[::-1, ::-1])[::-1, ::-1]


def snp_sum(value):
    size = lax.axis_size("snp")
    others = [
        lax.ppermute(value, "snp", [(i, (i + k) % size) for i in range(size)])
        for k in range(1, size)
    ]
    for other in others:
        value = value + other
    return value


def samp_sum(columns, gram):
    count = lax.axis_size("samp")
    rows, width = columns.shape
    across = width // TILE[1]
    tiles = columns.reshape(rows // 8, 8, across, 128).transpose(0, 2, 1, 3)
    wide = jnp.pad(gram, ((0, 0), (0, 128 - gram.shape[1])))
    gram_tiles = jnp.broadcast_to(wide.reshape(rows // 8, 1, 8, 128), tiles.shape)
    send = jnp.concatenate([tiles, gram_tiles], axis=2).reshape(count, -1, 16, 128)
    parts = send.shape[1]
    send = send.reshape(count, parts * 16, 128)
    got = lax.all_to_all(send, "samp", 0, 0)
    total = jnp.sum(got, axis=0)
    spread = lax.all_to_all(jnp.broadcast_to(total[None], got.shape), "samp", 0, 0)
    spread = spread.reshape(rows // 8, across, 16, 128)
    columns = spread[:, :, :8].transpose(0, 2, 1, 3).reshape(rows, width)
    gram = spread[:, 0, 8:, : gram.shape[1]].reshape(rows, gram.shape[1])
    return columns, gram


def on_device(
    genotype,
    freqs,
    left_factors,
    singular,
    right_factors,
    sketch,
    batch_sizes,
    missing_batch,
    missing_block,
):
    row_count, col_width = genotype.shape
    samp_size = lax.axis_size("samp")
    sample_count = row_count * samp_size
    snp_count = col_width * lax.axis_size("snp")
    right_local = lax.all_to_all(
        jnp.broadcast_to(right_factors[None], (samp_size, *right_factors.shape)), "samp", 0, 0
    ).reshape(col_width, -1)
    batch_range = jnp.arange(BATCHES, dtype=jnp.int32)
    block_range = jnp.arange(BLOCKS, dtype=jnp.int32)
    hot_batch = (missing_batch[:, None] == batch_range[None, :]).astype(jnp.float32)
    hot_block = (missing_block[:, None] == block_range[None, :]).astype(jnp.float32)
    table = jnp.dot(hot_batch.T, hot_block, preferred_element_type=jnp.float32)
    ends = jnp.cumsum(batch_sizes)
    row_ids = lax.axis_index("samp") * row_count + jnp.arange(row_count, dtype=jnp.int32)
    batch_of = jnp.sum((row_ids[:, None] >= ends[None, :]).astype(jnp.int32), axis=1)
    row_hot = (batch_of[:, None] == batch_range[None, :]).astype(jnp.float32)
    col_ids = lax.axis_index("snp") * col_width + jnp.arange(col_width, dtype=jnp.int32)
    col_hot = ((col_ids // BLOCK)[None, :] == block_range[:, None]).astype(jnp.float32)
    missing = (
        jnp.dot(
            jnp.dot(row_hot, table, preferred_element_type=jnp.float32),
            col_hot,
            preferred_element_type=jnp.float32,
        )
        > 0.5
    )
    lowrank = jnp.dot(left_factors * singular[None, :], right_local.T, precision=HIGH)
    observed = genotype.astype(jnp.float32) - 2.0 * freqs[None, :]
    matrix = jnp.where(missing, lowrank, observed).astype(jnp.bfloat16)

    start = lax.dot_general(
        sketch, matrix, (((0,), (1,)), ((), ())), preferred_element_type=jnp.float32
    )
    samples = snp_sum(start)
    columns = None
    for sweep_index in range(ITERS + 1):
        partial_columns = split_dot(samples, matrix, 0)
        partial_gram = exact_dot(samples, samples, ((1,), (1,)))
        raw, gram = samp_sum(partial_columns, partial_gram)
        factor = lower_inverse(gram / sample_count)
        if sweep_index == ITERS:
            break
        raw = exact_dot(factor, raw, ((1,), (0,)))
        product = split_dot(raw, matrix, 1)
        own = exact_dot(raw, raw, ((1,), (1,)))
        summed = snp_sum(jnp.concatenate([product, own], axis=1))
        factor = upper_inverse(summed[:, row_count:] / snp_count)
        samples = exact_dot(factor, summed[:, :row_count], ((1,), (0,)))
        columns = exact_dot(factor, raw, ((1,), (0,)))
    basis = exact_dot(samples, factor, ((0,), (1,)))
    projection = exact_dot(raw, factor / math.sqrt(sample_count), ((0,), (1,)))
    return (basis, projection, columns.T)


def solution(mesh):
    in_specs = (
        P("samp", "snp"),
        P("snp"),
        P("samp", None),
        P(),
        P(("snp", "samp"), None),
        P("snp", None),
        P(),
        P(),
        P(),
    )
    out_specs = (P("samp", None), P("snp", None), P("snp", None))
    return jax.shard_map(
        on_device, mesh=mesh, in_specs=in_specs, out_specs=out_specs, check_vma=False
    )
```

```python
import math

import jax
import jax.numpy as jnp
from jax import lax
from jax.experimental import pallas as pl
from jax.experimental.pallas import tpu as pltpu
from jax.sharding import Mesh, PartitionSpec as P

BATCHES = 12
BLOCK = 256
ITERS = 2
BLOCKS = 16
LANES = 128
SUB = 8
F32 = jnp.float32
BF16 = jnp.bfloat16
HIGH = lax.Precision.HIGHEST


def exact_dot(a, b, a_dim, b_dim):
    return lax.dot_general(
        a, b, (((a_dim,), (b_dim,)), ((), ())), precision=HIGH, preferred_element_type=F32
    )


def split_dot(values, matrix, dim):
    high = values.astype(BF16)
    low = (values - high.astype(F32)).astype(BF16)
    both = jnp.concatenate([high, low], axis=0)
    out = lax.dot_general(
        both, matrix, (((1,), (dim,)), ((), ())), preferred_element_type=F32
    )
    rows = values.shape[0]
    return out[:rows] + out[rows:]


def inverse_factor(gram, lower):
    size = gram.shape[0]
    across = lax.broadcasted_iota(jnp.int32, (size, size), 1)
    down = lax.broadcasted_iota(jnp.int32, (size, size), 0)
    wide = jnp.concatenate([gram, (across == down).astype(F32)], axis=1)
    count = size // SUB
    shape = (SUB, 2 * size)
    tiles = [wide[SUB * t : SUB * (t + 1)] for t in range(count)]
    sub = lax.broadcasted_iota(jnp.int32, shape, 0)
    step = 1 if lower else -1
    for a in range(count)[::step]:
        active = range(a, count) if lower else range(a + 1)
        cols = {
            t: [
                jnp.broadcast_to(tiles[t][:, SUB * a + k : SUB * a + k + 1], shape)
                for k in range(SUB)
            ]
            for t in active
        }
        scale = jnp.zeros(shape, F32)
        for k in range(SUB)[::step]:
            pivot = jnp.broadcast_to(cols[a][k][k : k + 1], shape)
            inverse = 1.0 / pivot
            scale = jnp.where(sub == k, pivot, scale)
            keep = (sub > k) if lower else (sub < k)
            rest = range(k + 1, SUB) if lower else range(k)
            row = jnp.broadcast_to(tiles[a][k : k + 1], shape) * inverse
            heads = {j: jnp.broadcast_to(cols[a][j][k : k + 1], shape) * inverse for j in rest}
            for t in active:
                column = cols[t][k]
                if t == a:
                    column = jnp.where(keep, column, 0.0)
                tiles[t] = tiles[t] - column * row
                for j in rest:
                    cols[t][j] = cols[t][j] - column * heads[j]
        tiles[a] = tiles[a] * lax.rsqrt(scale)
    return jnp.concatenate(tiles, axis=0)[:, size:]


def kernel_call(body, out_shapes, *operands):
    return pl.pallas_call(
        body,
        out_shape=out_shapes,
        compiler_params=pltpu.CompilerParams(vmem_limit_bytes=48 * 1024 * 1024),
    )(*operands)


def shape_of(shape, dtype=F32):
    return jax.ShapeDtypeStruct(shape, dtype)


def write_send(columns, gram, core, mine, other):
    rows, width = columns.shape
    half = rows // 2
    first = core == 0
    wide = jnp.concatenate([gram, jnp.zeros((rows, LANES - gram.shape[1]), F32)], axis=1)
    for value, low in ((columns, 0), (wide, SUB)):
        top, bottom = value[:half], value[half:]
        kept = jnp.where(first, top, bottom)
        sent = jnp.where(first, bottom, top)
        for ref, part in ((mine, kept), (other, sent)):
            for a in range(half // SUB):
                for b in range(width // LANES):
                    at = LANES * b if low == 0 else 0
                    ref[a * (width // LANES) + b, low : low + SUB, :] = part[
                        SUB * a : SUB * (a + 1), at : at + LANES
                    ]


def read_sum(mine, other, core, width):
    across = width // LANES
    half = mine.shape[0] // across
    halves = []
    for ref in (mine, other):
        value = jnp.concatenate(
            [
                jnp.concatenate([ref[a * across + b, :SUB, :] for b in range(across)], axis=1)
                for a in range(half)
            ],
            axis=0,
        )
        gram = jnp.concatenate([ref[a * across, SUB:, :] for a in range(half)], axis=0)
        halves.append((value, gram))
    first = core == 0
    columns, gram = (
        jnp.concatenate([jnp.where(first, m, o), jnp.where(first, o, m)], axis=0)
        for m, o in zip(*halves)
    )
    return columns, gram[:, : gram.shape[0]]


def spread_kernel(parts, out):
    out[...] = jnp.broadcast_to(jnp.sum(parts[...], axis=0, keepdims=True), out.shape)


def three_parts(value):
    high = value.astype(BF16)
    rest = value - high.astype(F32)
    middle = rest.astype(BF16)
    return [high, middle, (rest - middle.astype(F32)).astype(BF16)]


def solution(mesh):
    samp, snp = mesh.shape["samp"], mesh.shape["snp"]
    chips = samp // 2
    fine = Mesh(mesh.devices.reshape(chips, 2, snp), ("chip", "core", "snp"))

    def swap(value):
        return lax.ppermute(value, "core", [(0, 1), (1, 0)])

    def snp_others(value):
        return [
            lax.ppermute(value, "snp", [(i, (i + k) % snp) for i in range(snp)])
            for k in range(1, snp)
        ]

    def samp_sum(mine, other):
        send = mine + swap(other)
        got = lax.all_to_all(send, "chip", 0, 0)
        spread = kernel_call(spread_kernel, shape_of(got.shape), got)
        whole = lax.all_to_all(spread, "chip", 0, 0)
        return whole, swap(whole)

    def on_device(
        genotype,
        freqs,
        left_factors,
        singular,
        right_factors,
        sketch,
        batch_sizes,
        missing_batch,
        missing_block,
    ):
        row_count, col_width = genotype.shape
        rank = left_factors.shape[1]
        width = sketch.shape[1]
        sample_count = row_count * samp
        snp_count = col_width * snp
        core = lax.axis_index("core")
        place = core.reshape(1).astype(jnp.int32)
        samp_index = lax.axis_index("chip") * 2 + core

        right_mine = lax.all_to_all(
            jnp.broadcast_to(right_factors[None], (chips, *right_factors.shape)), "chip", 0, 0
        )
        right_other = swap(right_mine)

        batch_range = jnp.arange(BATCHES, dtype=jnp.int32)
        local_blocks = col_width // BLOCK
        block_range = lax.axis_index("snp") * local_blocks + jnp.arange(
            local_blocks, dtype=jnp.int32
        )
        ends = jnp.sum(
            jnp.where(batch_range[:, None] <= batch_range[None, :], batch_sizes[:, None], 0), axis=0
        )
        row_ids = samp_index * row_count + jnp.arange(row_count, dtype=jnp.int32)
        batch_of = jnp.sum((row_ids[:, None] >= ends[None, :]).astype(jnp.int32), axis=1)
        missing = jnp.sum(
            (
                (batch_of[:, None, None] == missing_batch[None, None, :])
                & (block_range[None, :, None] == missing_block[None, None, :])
            ).astype(F32),
            axis=2,
        )
        observed = (genotype.astype(F32) - 2.0 * freqs[None, :]).astype(BF16)
        weighted = left_factors * singular[None, :]

        def build_kernel(place, obs, miss, weight, mine, other, omega, x_out, start):
            first = place[0] == 0
            r_mine, r_other = mine[...], other[...]
            low = jnp.where(first, r_mine, r_other)
            high = jnp.where(first, r_other, r_mine)
            right = jnp.stack([low, high], axis=1).reshape(col_width, rank)
            lowrank = exact_dot(weight[...], right, 1, 1)
            pieces = []
            for j in range(local_blocks):
                at = slice(BLOCK * j, BLOCK * (j + 1))
                gone = jnp.broadcast_to(miss[:, j : j + 1], (row_count, BLOCK)) > 0.5
                pieces.append(jnp.where(gone, lowrank[:, at], obs[:, at].astype(F32)))
            x = jnp.concatenate(pieces, axis=1).astype(BF16)
            x_out[...] = x
            start[...] = lax.dot_general(
                omega[...], x, (((1,), (1,)), ((), ())), preferred_element_type=F32
            )

        def call_with_place(body, outs, *operands):
            specs = [pl.BlockSpec(memory_space=pltpu.SMEM)] + [
                pl.BlockSpec(memory_space=pltpu.VMEM) for _ in operands
            ]
            return pl.pallas_call(
                body,
                out_shape=outs,
                in_specs=specs,
                compiler_params=pltpu.CompilerParams(vmem_limit_bytes=48 * 1024 * 1024),
            )(place, *operands)

        matrix, start = call_with_place(
            build_kernel,
            (shape_of((row_count, col_width), BF16), shape_of((width, row_count))),
            observed,
            missing,
            weighted,
            right_mine,
            right_other,
            sketch.T,
        )

        part_shape = shape_of((chips, 2 * SUB, LANES))
        packed = row_count + 3 * width

        def first_kernel(place, own, a, b, c, x, samples_out, mine, other):
            samples = own[...] + a[...] + b[...] + c[...]
            samples_out[...] = samples
            write_send(
                split_dot(samples, x[...], 0),
                exact_dot(samples, samples, 1, 1),
                place[0],
                mine,
                other,
            )

        def forward_kernel(place, mine, other, x, raw_out, product_out, gram_out, wire):
            columns, gram = read_sum(mine, other, place[0], col_width)
            raw = exact_dot(inverse_factor(gram / sample_count, True), columns, 1, 0)
            raw_out[...] = raw
            product = split_dot(raw, x[...], 1)
            own = exact_dot(raw, raw, 1, 1)
            product_out[...] = product
            gram_out[...] = own
            wire[...] = jnp.concatenate([product.astype(BF16), *three_parts(own)], axis=1)

        def backward_kernel(
            place, product, gram, a, b, c, raw, x, samples_out, columns_out, mine, other
        ):
            total, own = product[...], gram[...]
            for ref in (a, b, c):
                total = total + ref[:, :row_count].astype(F32)
                parts = [
                    ref[:, row_count + width * i : row_count + width * (i + 1)].astype(F32)
                    for i in range(3)
                ]
                own = own + (parts[0] + (parts[1] + parts[2]))
            factor = inverse_factor(own / snp_count, False)
            samples = exact_dot(factor, total, 1, 0)
            samples_out[...] = samples
            columns_out[...] = exact_dot(factor, raw[...], 1, 0)
            write_send(
                split_dot(samples, x[...], 0),
                exact_dot(samples, samples, 1, 1),
                place[0],
                mine,
                other,
            )

        def last_kernel(place, mine, other, samples, basis, projection):
            columns, gram = read_sum(mine, other, place[0], col_width)
            factor = inverse_factor(gram / sample_count, True)
            basis[...] = exact_dot(factor, samples[...], 1, 0)
            projection[...] = exact_dot(factor / math.sqrt(sample_count), columns, 1, 0)

        samples_shape = shape_of((width, row_count))
        columns_shape = shape_of((width, col_width))
        samples, mine, other = call_with_place(
            first_kernel,
            (samples_shape, part_shape, part_shape),
            start,
            *snp_others(start),
            matrix,
        )
        columns = None
        for _ in range(ITERS):
            raw, product, gram, wire = call_with_place(
                forward_kernel,
                (
                    columns_shape,
                    samples_shape,
                    shape_of((width, width)),
                    shape_of((width, packed), BF16),
                ),
                *samp_sum(mine, other),
                matrix,
            )
            samples, columns, mine, other = call_with_place(
                backward_kernel,
                (samples_shape, columns_shape, part_shape, part_shape),
                product,
                gram,
                *snp_others(wire),
                raw,
                matrix,
            )
        basis, projection = call_with_place(
            last_kernel, (samples_shape, columns_shape), *samp_sum(mine, other), samples
        )
        return (basis.T, projection.T, columns.T)

    samp_axes = ("chip", "core")
    in_specs = (
        P(samp_axes, "snp"),
        P("snp"),
        P(samp_axes, None),
        P(),
        P(("snp", *samp_axes), None),
        P("snp", None),
        P(),
        P(),
        P(),
    )
    out_specs = (P(samp_axes, None), P("snp", None), P("snp", None))
    return jax.shard_map(
        on_device, mesh=fine, in_specs=in_specs, out_specs=out_specs, check_vma=False
    )
```

```python
import math

import jax
import jax.numpy as jnp
from jax import lax
from jax.experimental import pallas as pl
from jax.experimental.pallas import tpu as pltpu
from jax.sharding import Mesh, PartitionSpec as P

BATCHES = 12
BLOCK = 256
ITERS = 2
BLOCKS = 16
LANES = 128
SUB = 8
GROUP = 32
F32 = jnp.float32
BF16 = jnp.bfloat16
HIGH = lax.Precision.HIGHEST


def exact_dot(a, b, a_dim, b_dim):
    return lax.dot_general(
        a, b, (((a_dim,), (b_dim,)), ((), ())), precision=HIGH, preferred_element_type=F32
    )


def split_dot(values, matrix, dim):
    high = values.astype(BF16)
    low = (values - high.astype(F32)).astype(BF16)
    both = jnp.concatenate([high, low], axis=0)
    out = lax.dot_general(
        both, matrix, (((1,), (dim,)), ((), ())), preferred_element_type=F32
    )
    rows = values.shape[0]
    return out[:rows] + out[rows:]


def inverse_factor(gram, lower):
    size = gram.shape[0]
    across = lax.broadcasted_iota(jnp.int32, (size, size), 1)
    down = lax.broadcasted_iota(jnp.int32, (size, size), 0)
    wide = jnp.concatenate([gram, (across == down).astype(F32)], axis=1)
    count = size // SUB
    shape = (SUB, 2 * size)
    tiles = [wide[SUB * t : SUB * (t + 1)] for t in range(count)]
    sub = lax.broadcasted_iota(jnp.int32, shape, 0)
    step = 1 if lower else -1
    for a in range(count)[::step]:
        active = range(a, count) if lower else range(a + 1)
        cols = {
            t: [
                jnp.broadcast_to(tiles[t][:, SUB * a + k : SUB * a + k + 1], shape)
                for k in range(SUB)
            ]
            for t in active
        }
        scale = jnp.zeros(shape, F32)
        for k in range(SUB)[::step]:
            pivot = jnp.broadcast_to(cols[a][k][k : k + 1], shape)
            inverse = 1.0 / pivot
            scale = jnp.where(sub == k, pivot, scale)
            keep = (sub > k) if lower else (sub < k)
            rest = range(k + 1, SUB) if lower else range(k)
            row = jnp.broadcast_to(tiles[a][k : k + 1], shape) * inverse
            heads = {j: jnp.broadcast_to(cols[a][j][k : k + 1], shape) * inverse for j in rest}
            for t in active:
                column = cols[t][k]
                if t == a:
                    column = jnp.where(keep, column, 0.0)
                tiles[t] = tiles[t] - column * row
                for j in rest:
                    cols[t][j] = cols[t][j] - column * heads[j]
        tiles[a] = tiles[a] * lax.rsqrt(scale)
    return jnp.concatenate(tiles, axis=0)[:, size:]


def kernel_call(body, out_shapes, *operands):
    return pl.pallas_call(
        body,
        out_shape=out_shapes,
        compiler_params=pltpu.CompilerParams(vmem_limit_bytes=48 * 1024 * 1024),
    )(*operands)


def shape_of(shape, dtype=F32):
    return jax.ShapeDtypeStruct(shape, dtype)


def write_send(columns, gram, core, mine, other):
    rows, width = columns.shape
    half = rows // 2
    first = core == 0
    wide = jnp.concatenate([gram, jnp.zeros((rows, LANES - gram.shape[1]), F32)], axis=1)
    for value, low in ((columns, 0), (wide, SUB)):
        top, bottom = value[:half], value[half:]
        kept = jnp.where(first, top, bottom)
        sent = jnp.where(first, bottom, top)
        for ref, part in ((mine, kept), (other, sent)):
            for a in range(half // SUB):
                for b in range(width // LANES):
                    at = LANES * b if low == 0 else 0
                    ref[a * (width // LANES) + b, low : low + SUB, :] = part[
                        SUB * a : SUB * (a + 1), at : at + LANES
                    ]


def read_sum(mine, other, core, width):
    across = width // LANES
    half = mine.shape[0] // across
    halves = []
    for ref in (mine, other):
        value = jnp.concatenate(
            [
                jnp.concatenate([ref[a * across + b, :SUB, :] for b in range(across)], axis=1)
                for a in range(half)
            ],
            axis=0,
        )
        gram = jnp.concatenate([ref[a * across, SUB:, :] for a in range(half)], axis=0)
        halves.append((value, gram))
    first = core == 0
    columns, gram = (
        jnp.concatenate([jnp.where(first, m, o), jnp.where(first, o, m)], axis=0)
        for m, o in zip(*halves)
    )
    return columns, gram[:, : gram.shape[0]]


def spread_kernel(parts, out):
    out[...] = jnp.broadcast_to(jnp.sum(parts[...], axis=0, keepdims=True), out.shape)


def three_parts(value):
    high = value.astype(BF16)
    rest = value - high.astype(F32)
    middle = rest.astype(BF16)
    return [high, middle, (rest - middle.astype(F32)).astype(BF16)]


def solution(mesh):
    samp, snp = mesh.shape["samp"], mesh.shape["snp"]
    chips = samp // 2
    fine = Mesh(mesh.devices.reshape(chips, 2, snp), ("chip", "core", "snp"))

    def swap(value):
        return lax.ppermute(value, "core", [(0, 1), (1, 0)])

    def snp_others(value):
        return [
            lax.ppermute(value, "snp", [(i, (i + k) % snp) for i in range(snp)])
            for k in range(1, snp)
        ]

    def samp_sum(mine, other):
        send = mine + swap(other)
        got = lax.all_to_all(send, "chip", 0, 0)
        spread = kernel_call(spread_kernel, shape_of(got.shape), got)
        whole = lax.all_to_all(spread, "chip", 0, 0)
        return whole, swap(whole)

    def on_device(
        genotype,
        freqs,
        left_factors,
        singular,
        right_factors,
        sketch,
        batch_sizes,
        missing_batch,
        missing_block,
    ):
        row_count, col_width = genotype.shape
        rank = left_factors.shape[1]
        width = sketch.shape[1]
        sample_count = row_count * samp
        snp_count = col_width * snp
        core = lax.axis_index("core")
        place = core.reshape(1).astype(jnp.int32)
        samp_index = lax.axis_index("chip") * 2 + core

        right_mine = lax.all_to_all(
            jnp.broadcast_to(
                jnp.pad(right_factors, ((0, 0), (0, LANES - rank)))[None],
                (chips, right_factors.shape[0], LANES),
            ),
            "chip",
            0,
            0,
        )
        right_other = swap(right_mine)

        batch_range = jnp.arange(BATCHES, dtype=jnp.int32)
        local_blocks = col_width // BLOCK
        snp_index = lax.axis_index("snp")
        ends = jnp.sum(
            jnp.where(batch_range[:, None] <= batch_range[None, :], batch_sizes[:, None], 0), axis=0
        )
        row_ids = samp_index * row_count + jnp.arange(row_count, dtype=jnp.int32)
        batch_of = jnp.sum((row_ids[:, None] >= ends[None, :]).astype(jnp.int32), axis=1)
        away = jnp.arange(BLOCKS, dtype=jnp.int32)
        block_ids = (snp_index - away // local_blocks) % snp * local_blocks + away % local_blocks
        missing_rows = jnp.sum(
            (
                (batch_of[None, :, None] == missing_batch[None, None, :])
                & (block_ids[:, None, None] == missing_block[None, None, :])
            ).astype(F32),
            axis=2,
        )
        missing = missing_rows[:local_blocks].T
        weighted = left_factors * singular[None, :]
        weight_rows = jnp.pad(weighted.T, ((0, GROUP - rank), (0, 0)))
        weight_lanes = jnp.pad(weighted, ((0, 0), (0, LANES - rank)))
        omega = sketch.T

        def gone_blocks(miss, rows):
            return [
                jnp.broadcast_to(miss[:, j : j + 1], (rows, BLOCK)) > 0.5
                for j in range(local_blocks)
            ]

        def observe_kernel(geno, freq, miss, om, obs, start):
            rows = geno.shape[0]
            values = geno[...].astype(F32) - 2.0 * freq[...]
            gone = jnp.concatenate(gone_blocks(miss, rows), axis=1)
            kept = jnp.where(gone, 0.0, values).astype(BF16)
            obs[...] = kept
            start[...] = lax.dot_general(
                om[...], kept, (((1,), (1,)), ((), ())), preferred_element_type=F32
            )

        observed, start = pl.pallas_call(
            observe_kernel,
            grid=(row_count // LANES,),
            out_shape=(shape_of((row_count, col_width), BF16), shape_of((width, row_count))),
            in_specs=[
                pl.BlockSpec((LANES, col_width), lambda i: (i, 0)),
                pl.BlockSpec((1, col_width), lambda i: (0, 0)),
                pl.BlockSpec((LANES, local_blocks), lambda i: (i, 0)),
                pl.BlockSpec((width, col_width), lambda i: (0, 0)),
            ],
            out_specs=(
                pl.BlockSpec((LANES, col_width), lambda i: (i, 0)),
                pl.BlockSpec((width, LANES), lambda i: (0, i)),
            ),
        )(genotype, freqs.reshape(1, col_width), missing, omega)
        start_others = snp_others(start)

        def call_with_place(body, outs, *operands):
            specs = [pl.BlockSpec(memory_space=pltpu.SMEM)] + [
                pl.BlockSpec(memory_space=pltpu.VMEM) for _ in operands
            ]
            return pl.pallas_call(
                body,
                out_shape=outs,
                in_specs=specs,
                compiler_params=pltpu.CompilerParams(vmem_limit_bytes=48 * 1024 * 1024),
            )(place, *operands)

        def right_rows(place, mine, other):
            first = place[0] == 0
            r_mine, r_other = mine[...], other[...]
            low = jnp.where(first, r_mine, r_other)
            high = jnp.where(first, r_other, r_mine)
            return jnp.stack([low, high], axis=1).reshape(col_width, LANES)

        def mix_kernel(place, mine, other, om, mixed):
            right = right_rows(place, mine, other)
            pieces = [
                exact_dot(
                    om[:, BLOCK * j : BLOCK * (j + 1)].astype(F32),
                    right[BLOCK * j : BLOCK * (j + 1)],
                    1,
                    0,
                )[:, :GROUP]
                for j in range(local_blocks)
            ]
            mixed[...] = jnp.concatenate(pieces, axis=1)

        def build_kernel(place, obs, miss, weight, mine, other, x_out):
            right = right_rows(place, mine, other)
            for j, gone in enumerate(gone_blocks(miss, row_count)):
                at = slice(BLOCK * j, BLOCK * (j + 1))
                lowrank = exact_dot(weight[...], right[at], 1, 1)
                x_out[:, at] = jnp.where(gone, lowrank.astype(BF16), obs[:, at])

        mixed = call_with_place(
            mix_kernel,
            shape_of((width, local_blocks * GROUP)),
            right_mine,
            right_other,
            omega,
        )
        mixed_others = snp_others(mixed)
        matrix = call_with_place(
            build_kernel,
            shape_of((row_count, col_width), BF16),
            observed,
            missing,
            weight_lanes,
            right_mine,
            right_other,
        )

        part_shape = shape_of((chips, 2 * SUB, LANES))
        packed = row_count + 3 * width

        def first_kernel(
            place, own, a, b, c, q0, q1, q2, q3, miss, weight, x, samples_out, mine, other
        ):
            samples = own[...] + a[...] + b[...] + c[...]
            for k, q in enumerate((q0, q1, q2, q3)):
                masked = [
                    weight[...] * miss[local_blocks * k + j : local_blocks * k + j + 1, :]
                    for j in range(local_blocks)
                ]
                samples = samples + exact_dot(q[...], jnp.concatenate(masked, axis=0), 1, 0)
            samples_out[...] = samples
            write_send(
                split_dot(samples, x[...], 0),
                exact_dot(samples, samples, 1, 1),
                place[0],
                mine,
                other,
            )

        def forward_kernel(place, mine, other, x, raw_out, product_out, gram_out, wire):
            columns, gram = read_sum(mine, other, place[0], col_width)
            raw = exact_dot(inverse_factor(gram / sample_count, True), columns, 1, 0)
            raw_out[...] = raw
            product = split_dot(raw, x[...], 1)
            own = exact_dot(raw, raw, 1, 1)
            product_out[...] = product
            gram_out[...] = own
            wire[...] = jnp.concatenate([product.astype(BF16), *three_parts(own)], axis=1)

        def backward_kernel(
            place, product, gram, a, b, c, raw, x, samples_out, columns_out, mine, other
        ):
            total, own = product[...], gram[...]
            for ref in (a, b, c):
                total = total + ref[:, :row_count].astype(F32)
                parts = [
                    ref[:, row_count + width * i : row_count + width * (i + 1)].astype(F32)
                    for i in range(3)
                ]
                own = own + (parts[0] + (parts[1] + parts[2]))
            factor = inverse_factor(own / snp_count, False)
            samples = exact_dot(factor, total, 1, 0)
            samples_out[...] = samples
            columns_out[...] = exact_dot(factor, raw[...], 1, 0)
            write_send(
                split_dot(samples, x[...], 0),
                exact_dot(samples, samples, 1, 1),
                place[0],
                mine,
                other,
            )

        def last_kernel(place, mine, other, samples, basis, projection):
            columns, gram = read_sum(mine, other, place[0], col_width)
            factor = inverse_factor(gram / sample_count, True)
            basis[...] = exact_dot(factor, samples[...], 1, 0)
            projection[...] = exact_dot(factor / math.sqrt(sample_count), columns, 1, 0)

        samples_shape = shape_of((width, row_count))
        columns_shape = shape_of((width, col_width))
        samples, mine, other = call_with_place(
            first_kernel,
            (samples_shape, part_shape, part_shape),
            start,
            *start_others,
            mixed,
            *mixed_others,
            missing_rows,
            weight_rows,
            matrix,
        )
        columns = None
        for _ in range(ITERS):
            raw, product, gram, wire = call_with_place(
                forward_kernel,
                (
                    columns_shape,
                    samples_shape,
                    shape_of((width, width)),
                    shape_of((width, packed), BF16),
                ),
                *samp_sum(mine, other),
                matrix,
            )
            samples, columns, mine, other = call_with_place(
                backward_kernel,
                (samples_shape, columns_shape, part_shape, part_shape),
                product,
                gram,
                *snp_others(wire),
                raw,
                matrix,
            )
        basis, projection = call_with_place(
            last_kernel, (samples_shape, columns_shape), *samp_sum(mine, other), samples
        )
        return (basis.T, projection.T, columns.T)

    samp_axes = ("chip", "core")
    in_specs = (
        P(samp_axes, "snp"),
        P("snp"),
        P(samp_axes, None),
        P(),
        P(("snp", *samp_axes), None),
        P("snp", None),
        P(),
        P(),
        P(),
    )
    out_specs = (P(samp_axes, None), P("snp", None), P("snp", None))
    return jax.shard_map(
        on_device, mesh=fine, in_specs=in_specs, out_specs=out_specs, check_vma=False
    )
```

```python
import math

import jax
import jax.numpy as jnp
from jax import lax
from jax.experimental import pallas as pl
from jax.experimental.pallas import tpu as pltpu
from jax.sharding import Mesh, PartitionSpec as P

BATCHES = 12
BLOCK = 256
ITERS = 2
BLOCKS = 16
LANES = 128
SUB = 8
GROUP = 32
F32 = jnp.float32
BF16 = jnp.bfloat16
HIGH = lax.Precision.HIGHEST


def exact_dot(a, b, a_dim, b_dim):
    return lax.dot_general(
        a, b, (((a_dim,), (b_dim,)), ((), ())), precision=HIGH, preferred_element_type=F32
    )


def split_dot(values, matrix, dim):
    high = values.astype(BF16)
    low = (values - high.astype(F32)).astype(BF16)
    both = jnp.concatenate([high, low], axis=0)
    out = lax.dot_general(
        both, matrix, (((1,), (dim,)), ((), ())), preferred_element_type=F32
    )
    rows = values.shape[0]
    return out[:rows] + out[rows:]


def inverse_factor(gram, lower):
    size = gram.shape[0]
    across = lax.broadcasted_iota(jnp.int32, (size, size), 1)
    down = lax.broadcasted_iota(jnp.int32, (size, size), 0)
    wide = jnp.concatenate([gram, (across == down).astype(F32)], axis=1)
    count = size // SUB
    shape = (SUB, 2 * size)
    tiles = [wide[SUB * t : SUB * (t + 1)] for t in range(count)]
    sub = lax.broadcasted_iota(jnp.int32, shape, 0)
    step = 1 if lower else -1
    for a in range(count)[::step]:
        active = range(a, count) if lower else range(a + 1)
        cols = {
            t: [
                jnp.broadcast_to(tiles[t][:, SUB * a + k : SUB * a + k + 1], shape)
                for k in range(SUB)
            ]
            for t in active
        }
        scale = jnp.zeros(shape, F32)
        for k in range(SUB)[::step]:
            pivot = jnp.broadcast_to(cols[a][k][k : k + 1], shape)
            inverse = 1.0 / pivot
            scale = jnp.where(sub == k, pivot, scale)
            keep = (sub > k) if lower else (sub < k)
            rest = range(k + 1, SUB) if lower else range(k)
            row = jnp.broadcast_to(tiles[a][k : k + 1], shape) * inverse
            heads = {j: jnp.broadcast_to(cols[a][j][k : k + 1], shape) * inverse for j in rest}
            for t in active:
                column = cols[t][k]
                if t == a:
                    column = jnp.where(keep, column, 0.0)
                tiles[t] = tiles[t] - column * row
                for j in rest:
                    cols[t][j] = cols[t][j] - column * heads[j]
        tiles[a] = tiles[a] * lax.rsqrt(scale)
    return jnp.concatenate(tiles, axis=0)[:, size:]


def kernel_call(body, out_shapes, *operands):
    return pl.pallas_call(
        body,
        out_shape=out_shapes,
        compiler_params=pltpu.CompilerParams(vmem_limit_bytes=48 * 1024 * 1024),
    )(*operands)


def shape_of(shape, dtype=F32):
    return jax.ShapeDtypeStruct(shape, dtype)


def write_send(columns, gram, core, mine, other):
    rows, width = columns.shape
    half = rows // 2
    first = core == 0
    wide = jnp.concatenate([gram, jnp.zeros((rows, LANES - gram.shape[1]), F32)], axis=1)
    for value, low in ((columns, 0), (wide, SUB)):
        top, bottom = value[:half], value[half:]
        kept = jnp.where(first, top, bottom)
        sent = jnp.where(first, bottom, top)
        for ref, part in ((mine, kept), (other, sent)):
            for a in range(half // SUB):
                for b in range(width // LANES):
                    at = LANES * b if low == 0 else 0
                    ref[a * (width // LANES) + b, low : low + SUB, :] = part[
                        SUB * a : SUB * (a + 1), at : at + LANES
                    ]


def read_sum(mine, other, core, width):
    across = width // LANES
    half = mine.shape[0] // across
    halves = []
    for ref in (mine, other):
        value = jnp.concatenate(
            [
                jnp.concatenate([ref[a * across + b, :SUB, :] for b in range(across)], axis=1)
                for a in range(half)
            ],
            axis=0,
        )
        gram = jnp.concatenate([ref[a * across, SUB:, :] for a in range(half)], axis=0)
        halves.append((value, gram))
    first = core == 0
    columns, gram = (
        jnp.concatenate([jnp.where(first, m, o), jnp.where(first, o, m)], axis=0)
        for m, o in zip(*halves)
    )
    return columns, gram[:, : gram.shape[0]]


def spread_kernel(parts, out):
    out[...] = jnp.broadcast_to(jnp.sum(parts[...], axis=0, keepdims=True), out.shape)


def three_parts(value):
    high = value.astype(BF16)
    rest = value - high.astype(F32)
    middle = rest.astype(BF16)
    return [high, middle, (rest - middle.astype(F32)).astype(BF16)]


def solution(mesh):
    samp, snp = mesh.shape["samp"], mesh.shape["snp"]
    chips = samp // 2
    fine = Mesh(mesh.devices.reshape(chips, 2, snp), ("chip", "core", "snp"))

    def swap(value):
        return lax.ppermute(value, "core", [(0, 1), (1, 0)])

    def snp_others(value):
        return [
            lax.ppermute(value, "snp", [(i, (i + k) % snp) for i in range(snp)])
            for k in range(1, snp)
        ]

    def samp_sum(mine, other):
        send = mine + swap(other)
        got = lax.all_to_all(send, "chip", 0, 0)
        spread = kernel_call(spread_kernel, shape_of(got.shape), got)
        whole = lax.all_to_all(spread, "chip", 0, 0)
        return whole, swap(whole)

    def on_device(
        genotype,
        freqs,
        left_factors,
        singular,
        right_factors,
        sketch,
        batch_sizes,
        missing_batch,
        missing_block,
    ):
        row_count, col_width = genotype.shape
        rank = left_factors.shape[1]
        width = sketch.shape[1]
        sample_count = row_count * samp
        snp_count = col_width * snp
        place = lax.axis_index(("chip", "core", "snp")).reshape(1).astype(jnp.int32)
        local_blocks = col_width // BLOCK
        omega = sketch.T

        def core_of(place):
            return place[0] // snp % 2

        def call_with_place(body, outs, *operands, scalars=(), out_specs=None, cost=None):
            smem = pl.BlockSpec(memory_space=pltpu.SMEM)
            specs = [smem] * (1 + len(scalars)) + [
                pl.BlockSpec(memory_space=pltpu.VMEM) for _ in operands
            ]
            more = {} if out_specs is None else {"out_specs": out_specs}
            return pl.pallas_call(
                body,
                out_shape=outs,
                in_specs=specs,
                cost_estimate=cost,
                compiler_params=pltpu.CompilerParams(vmem_limit_bytes=48 * 1024 * 1024),
                **more,
            )(place, *scalars, *operands)

        def batch_ids(place, sizes, shape, axis):
            ids = lax.broadcasted_iota(jnp.int32, shape, axis) + place[0] // snp * row_count
            batch = jnp.zeros(shape, jnp.int32)
            end = jnp.int32(0)
            for b in range(BATCHES - 1):
                end = end + sizes[b]
                batch = batch + (ids >= end).astype(jnp.int32)
            return batch

        def gone_in(bits, batch):
            return ((jnp.broadcast_to(bits, batch.shape) >> batch) & 1) == 1

        chunk = LANES

        def observe_kernel(
            place, sizes_in, batch_in, block_in, geno_in, freq_in, om_in,
            obs, start, bits,
            sizes, tile_batch, tile_block, geno, freq, om, sems,
        ):
            copies = [
                pltpu.make_async_copy(source, target, sems.at[i])
                for i, (source, target) in enumerate(
                    [
                        (batch_in, tile_batch),
                        (block_in, tile_block),
                        (sizes_in, sizes),
                        (freq_in, freq),
                    ]
                    + [
                        (geno_in.at[pl.ds(low, chunk)], geno.at[pl.ds(low, chunk)])
                        for low in range(0, row_count, chunk)
                    ]
                    + [(om_in, om)]
                )
            ]
            for copy in copies:
                copy.start()
            for block in range(BLOCKS):
                bits[block] = 0
            copies[0].wait()
            copies[1].wait()
            for i in range(tile_batch.shape[0]):
                block = tile_block[i]
                bits[block] = bits[block] | (1 << tile_batch[i])
            copies[2].wait()
            copies[3].wait()
            batch = batch_ids(place, sizes, (row_count, LANES), 0)
            own_bits = [bits[place[0] % snp * local_blocks + j] for j in range(local_blocks)]
            for n, top in enumerate(range(0, row_count, chunk)):
                copies[4 + n].wait()
                rows = slice(top, top + chunk)
                for j in range(local_blocks):
                    gone = gone_in(own_bits[j], batch[rows])
                    for low in range(BLOCK * j, BLOCK * (j + 1), LANES):
                        at = slice(low, low + LANES)
                        values = geno[rows, at].astype(F32) - 2.0 * freq[:, at]
                        obs[rows, at] = jnp.where(gone, 0.0, values).astype(BF16)
            copies[-1].wait()
            start[...] = lax.dot_general(
                om[...], obs[...], (((1,), (1,)), ((), ())), preferred_element_type=F32
            )

        vmem = pl.BlockSpec(memory_space=pltpu.VMEM)
        smem = pl.BlockSpec(memory_space=pltpu.SMEM)
        tiles = missing_batch.shape
        observed, start, bits = pl.pallas_call(
            observe_kernel,
            out_shape=(
                shape_of((row_count, col_width), BF16),
                shape_of((width, row_count)),
                shape_of((BLOCKS,), jnp.int32),
            ),
            in_specs=[smem] + [pl.BlockSpec(memory_space=pltpu.HBM)] * 6,
            out_specs=(vmem, vmem, smem),
            scratch_shapes=[
                pltpu.SMEM(batch_sizes.shape, jnp.int32),
                pltpu.SMEM(tiles, jnp.int32),
                pltpu.SMEM(tiles, jnp.int32),
                pltpu.VMEM((row_count, col_width), jnp.int32),
                pltpu.VMEM((1, col_width), F32),
                pltpu.VMEM((width, col_width), BF16),
                pltpu.SemaphoreType.DMA((5 + row_count // chunk,)),
            ],
            compiler_params=pltpu.CompilerParams(vmem_limit_bytes=63 * 1024 * 1024),
        )(
            place,
            batch_sizes,
            missing_batch,
            missing_block,
            genotype,
            freqs.reshape(1, col_width),
            omega,
        )

        def pack_kernel(place, bits, mine, other, spread):
            del bits
            first = core_of(place) == 0
            low = jnp.where(first, mine[...], other[...])
            high = jnp.where(first, other[...], mine[...])
            fill = jnp.zeros((SUB, GROUP - rank), F32)
            pieces = []
            for part in (low, high):
                for top in range(0, part.shape[0], SUB):
                    pieces += [part[top : top + SUB], fill]
            tile = jnp.concatenate(pieces, axis=1)
            spread[...] = jnp.broadcast_to(tile[None], spread.shape)

        right_tiles = lax.all_to_all(
            call_with_place(
                pack_kernel,
                shape_of((chips, SUB, LANES)),
                right_factors,
                swap(right_factors),
                scalars=(bits,),
            ),
            "chip",
            0,
            0,
        )
        start_others = snp_others(start)

        def right_rows(tiles):
            value = tiles[...]
            parts = [value[:, :, g : g + GROUP] for g in range(0, LANES, GROUP)]
            return jnp.stack(parts, axis=1).reshape(col_width, GROUP)

        def weight_rows(scale, left):
            rows = [left[r : r + 1, :] * scale[r] for r in range(rank)]
            return jnp.concatenate(
                [*rows, jnp.zeros((GROUP - rank, row_count), F32)], axis=0
            )

        def mix_kernel(place, tiles, om, mixed):
            right = right_rows(tiles)
            pieces = [
                exact_dot(
                    om[:, BLOCK * j : BLOCK * (j + 1)].astype(F32),
                    right[BLOCK * j : BLOCK * (j + 1)],
                    1,
                    0,
                )
                for j in range(local_blocks)
            ]
            mixed[...] = jnp.concatenate(pieces, axis=1)

        def build_kernel(place, sizes, bits, scale, obs, left, tiles, x_out):
            right = right_rows(tiles)
            weight = weight_rows(scale, left).T
            batch = batch_ids(place, sizes, (row_count, BLOCK), 0)
            for j in range(local_blocks):
                at = slice(BLOCK * j, BLOCK * (j + 1))
                lowrank = exact_dot(weight, right[at], 1, 1)
                gone = gone_in(bits[place[0] % snp * local_blocks + j], batch)
                x_out[:, at] = jnp.where(gone, lowrank, obs[:, at].astype(F32)).astype(BF16)

        mixed = call_with_place(
            mix_kernel,
            shape_of((width, local_blocks * GROUP)),
            right_tiles,
            omega,
        )
        mixed_others = snp_others(mixed)
        left_rows = left_factors.T
        matrix = call_with_place(
            build_kernel,
            shape_of((row_count, col_width), BF16),
            observed,
            left_rows,
            right_tiles,
            scalars=(batch_sizes, bits, singular),
        )

        part_shape = shape_of((chips, 2 * SUB, LANES))
        packed = row_count + 3 * width

        def first_kernel(
            place, sizes, bits, scale, own, a, b, c, q0, q1, q2, q3, left, x,
            samples_out, mine, other,
        ):
            samples = own[...] + a[...] + b[...] + c[...]
            batch = batch_ids(place, sizes, (1, row_count), 1)
            weight = weight_rows(scale, left)
            for k, q in enumerate((q0, q1, q2, q3)):
                source = (place[0] + (snp - k)) % snp
                masked = [
                    jnp.where(gone_in(bits[source * local_blocks + j], batch), weight, 0.0)
                    for j in range(local_blocks)
                ]
                samples = samples + exact_dot(q[...], jnp.concatenate(masked, axis=0), 1, 0)
            samples_out[...] = samples
            write_send(
                split_dot(samples, x[...], 0),
                exact_dot(samples, samples, 1, 1),
                core_of(place),
                mine,
                other,
            )

        def forward_kernel(place, mine, other, x, raw_out, product_out, gram_out, wire):
            columns, gram = read_sum(mine, other, core_of(place), col_width)
            raw = exact_dot(inverse_factor(gram / sample_count, True), columns, 1, 0)
            raw_out[...] = raw
            product = split_dot(raw, x[...], 1)
            own = exact_dot(raw, raw, 1, 1)
            product_out[...] = product
            gram_out[...] = own
            wire[...] = jnp.concatenate([product.astype(BF16), *three_parts(own)], axis=1)

        def backward_kernel(
            place, product, gram, a, b, c, raw, x, samples_out, columns_out, mine, other
        ):
            total, own = product[...], gram[...]
            for ref in (a, b, c):
                total = total + ref[:, :row_count].astype(F32)
                parts = [
                    ref[:, row_count + width * i : row_count + width * (i + 1)].astype(F32)
                    for i in range(3)
                ]
                own = own + (parts[0] + (parts[1] + parts[2]))
            factor = inverse_factor(own / snp_count, False)
            samples = exact_dot(factor, total, 1, 0)
            samples_out[...] = samples
            columns_out[...] = exact_dot(factor, raw[...], 1, 0)
            write_send(
                split_dot(samples, x[...], 0),
                exact_dot(samples, samples, 1, 1),
                core_of(place),
                mine,
                other,
            )

        def last_kernel(place, mine, other, samples, basis, projection):
            columns, gram = read_sum(mine, other, core_of(place), col_width)
            factor = inverse_factor(gram / sample_count, True)
            basis[...] = exact_dot(factor, samples[...], 1, 0)
            projection[...] = exact_dot(factor / math.sqrt(sample_count), columns, 1, 0)

        samples_shape = shape_of((width, row_count))
        columns_shape = shape_of((width, col_width))
        samples, mine, other = call_with_place(
            first_kernel,
            (samples_shape, part_shape, part_shape),
            start,
            *start_others,
            mixed,
            *mixed_others,
            left_rows,
            matrix,
            scalars=(batch_sizes, bits, singular),
        )
        columns = None
        for _ in range(ITERS):
            raw, product, gram, wire = call_with_place(
                forward_kernel,
                (
                    columns_shape,
                    samples_shape,
                    shape_of((width, width)),
                    shape_of((width, packed), BF16),
                ),
                *samp_sum(mine, other),
                matrix,
            )
            samples, columns, mine, other = call_with_place(
                backward_kernel,
                (samples_shape, columns_shape, part_shape, part_shape),
                product,
                gram,
                *snp_others(wire),
                raw,
                matrix,
            )
        basis, projection = call_with_place(
            last_kernel, (samples_shape, columns_shape), *samp_sum(mine, other), samples
        )
        return (basis.T, projection.T, columns.T)

    samp_axes = ("chip", "core")
    in_specs = (
        P(samp_axes, "snp"),
        P("snp"),
        P(samp_axes, None),
        P(),
        P(("snp", *samp_axes), None),
        P("snp", None),
        P(),
        P(),
        P(),
    )
    out_specs = (P(samp_axes, None), P("snp", None), P("snp", None))
    return jax.shard_map(
        on_device, mesh=fine, in_specs=in_specs, out_specs=out_specs, check_vma=False
    )
```

```python
import math

import jax
import jax.numpy as jnp
from jax import lax
from jax.experimental import pallas as pl
from jax.experimental.pallas import tpu as pltpu
from jax.sharding import Mesh, PartitionSpec as P

BATCHES = 12
BLOCK = 256
ITERS = 2
BLOCKS = 16
LANES = 128
SUB = 8
GROUP = 32
F32 = jnp.float32
BF16 = jnp.bfloat16
HIGH = lax.Precision.HIGHEST


def exact_dot(a, b, a_dim, b_dim):
    return lax.dot_general(
        a, b, (((a_dim,), (b_dim,)), ((), ())), precision=HIGH, preferred_element_type=F32
    )


def split_dot(values, matrix, dim):
    high = values.astype(BF16)
    low = (values - high.astype(F32)).astype(BF16)
    both = jnp.concatenate([high, low], axis=0)
    out = lax.dot_general(
        both, matrix, (((1,), (dim,)), ((), ())), preferred_element_type=F32
    )
    rows = values.shape[0]
    return out[:rows] + out[rows:]


def inverse_factor(gram, lower):
    size = gram.shape[0]
    across = lax.broadcasted_iota(jnp.int32, (size, size), 1)
    down = lax.broadcasted_iota(jnp.int32, (size, size), 0)
    wide = jnp.concatenate([gram, (across == down).astype(F32)], axis=1)
    count = size // SUB
    shape = (SUB, 2 * size)
    tiles = [wide[SUB * t : SUB * (t + 1)] for t in range(count)]
    sub = lax.broadcasted_iota(jnp.int32, shape, 0)
    step = 1 if lower else -1
    for a in range(count)[::step]:
        active = range(a, count) if lower else range(a + 1)
        cols = {
            t: [
                jnp.broadcast_to(tiles[t][:, SUB * a + k : SUB * a + k + 1], shape)
                for k in range(SUB)
            ]
            for t in active
        }
        scale = jnp.zeros(shape, F32)
        for k in range(SUB)[::step]:
            pivot = jnp.broadcast_to(cols[a][k][k : k + 1], shape)
            inverse = 1.0 / pivot
            scale = jnp.where(sub == k, pivot, scale)
            keep = (sub > k) if lower else (sub < k)
            rest = range(k + 1, SUB) if lower else range(k)
            row = jnp.broadcast_to(tiles[a][k : k + 1], shape) * inverse
            heads = {j: jnp.broadcast_to(cols[a][j][k : k + 1], shape) * inverse for j in rest}
            for t in active:
                column = cols[t][k]
                if t == a:
                    column = jnp.where(keep, column, 0.0)
                tiles[t] = tiles[t] - column * row
                for j in rest:
                    cols[t][j] = cols[t][j] - column * heads[j]
        tiles[a] = tiles[a] * lax.rsqrt(scale)
    return jnp.concatenate(tiles, axis=0)[:, size:]


def kernel_call(body, out_shapes, *operands):
    return pl.pallas_call(
        body,
        out_shape=out_shapes,
        compiler_params=pltpu.CompilerParams(vmem_limit_bytes=48 * 1024 * 1024),
    )(*operands)


def shape_of(shape, dtype=F32):
    return jax.ShapeDtypeStruct(shape, dtype)


def write_send(columns, gram, core, mine, other):
    rows = columns.shape[0]
    blank = jnp.zeros((rows, LANES - gram.shape[1]), F32)
    value = jnp.concatenate([columns, gram, blank], axis=1)
    top, bottom = value[: rows // 2], value[rows // 2 :]
    mine[...] = jnp.where(core == 0, top, bottom)
    other[...] = jnp.where(core == 0, bottom, top)


def three_parts(value):
    high = value.astype(BF16)
    rest = value - high.astype(F32)
    middle = rest.astype(BF16)
    return [high, middle, (rest - middle.astype(F32)).astype(BF16)]


def solution(mesh):
    samp, snp = mesh.shape["samp"], mesh.shape["snp"]
    chips, ring = samp // 2, 4
    depth = chips // ring
    fine = Mesh(mesh.devices.reshape(depth, ring, 2, snp), ("z", "x", "core", "snp"))
    samp_axes = ("z", "x", "core")

    def swap(value):
        return lax.ppermute(value, "core", [(0, 1), (1, 0)])

    def snp_others(value):
        return [
            lax.ppermute(value, "snp", [(i, (i + k) % snp) for i in range(snp)])
            for k in range(1, snp)
        ]

    def x_shift(value, k):
        return lax.ppermute(value, "x", [(i, (i + k) % ring) for i in range(ring)])

    def on_device(
        genotype,
        freqs,
        left_factors,
        singular,
        right_factors,
        sketch,
        batch_sizes,
        missing_batch,
        missing_block,
    ):
        row_count, col_width = genotype.shape
        rank = left_factors.shape[1]
        width = sketch.shape[1]
        sample_count = row_count * samp
        snp_count = col_width * snp
        place = lax.axis_index((*samp_axes, "snp")).reshape(1).astype(jnp.int32)
        local_blocks = col_width // BLOCK
        omega = sketch.T

        def core_of(place):
            return place[0] // snp % 2

        def x_of(place):
            return place[0] // (snp * 2) % ring

        def call_with_place(body, outs, *operands, scalars=(), scratch=()):
            smem = pl.BlockSpec(memory_space=pltpu.SMEM)
            specs = [smem] * (1 + len(scalars)) + [
                pl.BlockSpec(memory_space=pltpu.VMEM) for _ in operands
            ]
            return pl.pallas_call(
                body,
                out_shape=outs,
                in_specs=specs,
                scratch_shapes=scratch,
                compiler_params=pltpu.CompilerParams(vmem_limit_bytes=48 * 1024 * 1024),
            )(place, *scalars, *operands)

        def batch_ids(place, sizes, shape, axis):
            ids = lax.broadcasted_iota(jnp.int32, shape, axis) + place[0] // snp * row_count
            batch = jnp.zeros(shape, jnp.int32)
            end = jnp.int32(0)
            for b in range(BATCHES - 1):
                end = end + sizes[b]
                batch = batch + (ids >= end).astype(jnp.int32)
            return batch

        def gone_in(bits, batch):
            return ((jnp.broadcast_to(bits, batch.shape) >> batch) & 1) == 1

        chunk = LANES

        def observe_kernel(
            place, sizes_in, batch_in, block_in, geno_in, freq_in, om_in,
            obs, start, bits,
            sizes, tile_batch, tile_block, geno, freq, om, sems,
        ):
            copies = [
                pltpu.make_async_copy(source, target, sems.at[i])
                for i, (source, target) in enumerate(
                    [
                        (batch_in, tile_batch),
                        (block_in, tile_block),
                        (sizes_in, sizes),
                        (freq_in, freq),
                    ]
                    + [
                        (geno_in.at[pl.ds(low, chunk)], geno.at[pl.ds(low, chunk)])
                        for low in range(0, row_count, chunk)
                    ]
                    + [(om_in, om)]
                )
            ]
            for copy in copies:
                copy.start()
            for block in range(BLOCKS):
                bits[block] = 0
            copies[0].wait()
            copies[1].wait()
            for i in range(tile_batch.shape[0]):
                block = tile_block[i]
                bits[block] = bits[block] | (1 << tile_batch[i])
            copies[2].wait()
            copies[3].wait()
            batch = batch_ids(place, sizes, (row_count, LANES), 0)
            own_bits = [bits[place[0] % snp * local_blocks + j] for j in range(local_blocks)]
            for n, top in enumerate(range(0, row_count, chunk)):
                copies[4 + n].wait()
                rows = slice(top, top + chunk)
                for j in range(local_blocks):
                    gone = gone_in(own_bits[j], batch[rows])
                    for low in range(BLOCK * j, BLOCK * (j + 1), LANES):
                        at = slice(low, low + LANES)
                        values = geno[rows, at].astype(F32) - 2.0 * freq[:, at]
                        obs[rows, at] = jnp.where(gone, 0.0, values).astype(BF16)
            copies[-1].wait()
            start[...] = lax.dot_general(
                om[...], obs[...], (((1,), (1,)), ((), ())), preferred_element_type=F32
            )

        vmem = pl.BlockSpec(memory_space=pltpu.VMEM)
        smem = pl.BlockSpec(memory_space=pltpu.SMEM)
        tiles = missing_batch.shape
        observed, start, bits = pl.pallas_call(
            observe_kernel,
            out_shape=(
                shape_of((row_count, col_width), BF16),
                shape_of((width, row_count)),
                shape_of((BLOCKS,), jnp.int32),
            ),
            in_specs=[smem] + [pl.BlockSpec(memory_space=pltpu.HBM)] * 6,
            out_specs=(vmem, vmem, smem),
            scratch_shapes=[
                pltpu.SMEM(batch_sizes.shape, jnp.int32),
                pltpu.SMEM(tiles, jnp.int32),
                pltpu.SMEM(tiles, jnp.int32),
                pltpu.VMEM((row_count, col_width), jnp.int32),
                pltpu.VMEM((1, col_width), F32),
                pltpu.VMEM((width, col_width), BF16),
                pltpu.SemaphoreType.DMA((5 + row_count // chunk,)),
            ],
            compiler_params=pltpu.CompilerParams(vmem_limit_bytes=63 * 1024 * 1024),
        )(
            place,
            batch_sizes,
            missing_batch,
            missing_block,
            genotype,
            freqs.reshape(1, col_width),
            omega,
        )

        def pack_kernel(place, bits, mine, other, spread):
            del bits
            first = core_of(place) == 0
            low = jnp.where(first, mine[...], other[...])
            high = jnp.where(first, other[...], mine[...])
            fill = jnp.zeros((SUB, GROUP - rank), F32)
            pieces = []
            for part in (low, high):
                for top in range(0, part.shape[0], SUB):
                    pieces += [part[top : top + SUB], fill]
            tile = jnp.concatenate(pieces, axis=1)
            spread[...] = jnp.broadcast_to(tile[None], spread.shape)

        right_tiles = lax.all_to_all(
            call_with_place(
                pack_kernel,
                shape_of((chips, SUB, LANES)),
                right_factors,
                swap(right_factors),
                scalars=(bits,),
            ),
            ("z", "x"),
            0,
            0,
        )
        start_others = snp_others(start)

        def right_rows(tiles):
            value = tiles[...]
            parts = [value[:, :, g : g + GROUP] for g in range(0, LANES, GROUP)]
            return jnp.stack(parts, axis=1).reshape(col_width, GROUP)

        def weight_rows(scale, left):
            rows = [left[r : r + 1, :] * scale[r] for r in range(rank)]
            return jnp.concatenate(
                [*rows, jnp.zeros((GROUP - rank, row_count), F32)], axis=0
            )

        def mix_kernel(place, tiles, om, mixed):
            right = right_rows(tiles)
            pieces = [
                exact_dot(
                    om[:, BLOCK * j : BLOCK * (j + 1)].astype(F32),
                    right[BLOCK * j : BLOCK * (j + 1)],
                    1,
                    0,
                )
                for j in range(local_blocks)
            ]
            mixed[...] = jnp.concatenate(pieces, axis=1)

        def build_kernel(place, sizes, bits, scale, obs, left, tiles, x_out):
            right = right_rows(tiles)
            weight = weight_rows(scale, left).T
            batch = batch_ids(place, sizes, (row_count, BLOCK), 0)
            for j in range(local_blocks):
                at = slice(BLOCK * j, BLOCK * (j + 1))
                lowrank = exact_dot(weight, right[at], 1, 1)
                gone = gone_in(bits[place[0] % snp * local_blocks + j], batch)
                x_out[:, at] = jnp.where(gone, lowrank, obs[:, at].astype(F32)).astype(BF16)

        mixed = call_with_place(
            mix_kernel,
            shape_of((width, local_blocks * GROUP)),
            right_tiles,
            omega,
        )
        mixed_others = snp_others(mixed)
        left_rows = left_factors.T
        matrix = call_with_place(
            build_kernel,
            shape_of((row_count, col_width), BF16),
            observed,
            left_rows,
            right_tiles,
            scalars=(batch_sizes, bits, singular),
        )

        packed = row_count + 3 * width
        sum_width = col_width + LANES
        part_shape = shape_of((width // 2, sum_width))
        tile_shape = shape_of((SUB, sum_width))

        def split_kernel(place, mine, got, own, *sends):
            for k, ref in enumerate((own, *sends)):
                rows = pl.ds(pl.multiple_of((x_of(place) + k) % ring * SUB, SUB), SUB)
                ref[...] = mine[rows, :] + got[rows, :]

        def spread_kernel(place, own, a, b, c, out):
            total = own[...] + a[...] + b[...] + c[...]
            if out.dtype == BF16:
                columns, gram = total[:, :col_width], total[:, col_width : col_width + width]
                total = jnp.concatenate(
                    [
                        columns.astype(BF16),
                        *three_parts(gram),
                        jnp.zeros((SUB, out.shape[2] - col_width - 3 * width), BF16),
                    ],
                    axis=1,
                )
            out[...] = jnp.broadcast_to(total[None], out.shape)

        def gather_kernel(place, parts, out):
            total = jnp.sum(parts[...].astype(F32), axis=0)
            if parts.dtype == BF16:
                grams = [
                    total[:, col_width + width * i : col_width + width * (i + 1)]
                    for i in range(3)
                ]
                total = jnp.concatenate(
                    [
                        total[:, :col_width],
                        grams[0] + (grams[1] + grams[2]),
                        jnp.zeros((SUB, LANES - width), F32),
                    ],
                    axis=1,
                )
            out[...] = total

        def samp_sum(mine, other, dtype):
            own, *sends = call_with_place(
                split_kernel, (tile_shape,) * ring, mine, swap(other)
            )
            gots = [x_shift(send, k) for k, send in enumerate(sends, 1)]
            wide = sum_width if dtype == F32 else col_width + 2 * LANES
            spread = call_with_place(
                spread_kernel, shape_of((depth, SUB, wide), dtype), own, *gots
            )
            tile = call_with_place(
                gather_kernel, tile_shape, lax.all_to_all(spread, "z", 0, 0)
            )
            near = [tile] + [x_shift(tile, k) for k in range(1, ring)]
            return [*near, *[swap(value) for value in near]]

        def read_sum(place, tiles, whole):
            for n, ref in enumerate(tiles):
                side = core_of(place) if n < ring else 1 - core_of(place)
                tile = side * ring + (x_of(place) + (ring - n % ring)) % ring
                whole[pl.ds(pl.multiple_of(tile * SUB, SUB), SUB), :] = ref[...]
            return whole[:, :col_width], whole[:, col_width : col_width + width]

        whole_scratch = [pltpu.VMEM((width, sum_width), F32)]

        def first_kernel(
            place, sizes, bits, scale, own, a, b, c, q0, q1, q2, q3, left, x,
            samples_out, mine, other,
        ):
            samples = own[...] + a[...] + b[...] + c[...]
            batch = batch_ids(place, sizes, (1, row_count), 1)
            weight = weight_rows(scale, left)
            for k, q in enumerate((q0, q1, q2, q3)):
                source = (place[0] + (snp - k)) % snp
                masked = [
                    jnp.where(gone_in(bits[source * local_blocks + j], batch), weight, 0.0)
                    for j in range(local_blocks)
                ]
                samples = samples + exact_dot(q[...], jnp.concatenate(masked, axis=0), 1, 0)
            samples_out[...] = samples
            write_send(
                split_dot(samples, x[...], 0),
                exact_dot(samples, samples, 1, 1),
                core_of(place),
                mine,
                other,
            )

        def forward_kernel(place, *refs):
            tiles, (x, raw_out, product_out, gram_out, wire, whole) = refs[:8], refs[8:]
            columns, gram = read_sum(place, tiles, whole)
            raw = exact_dot(inverse_factor(gram / sample_count, True), columns, 1, 0)
            raw_out[...] = raw
            product = split_dot(raw, x[...], 1)
            own = exact_dot(raw, raw, 1, 1)
            product_out[...] = product
            gram_out[...] = own
            wire[...] = jnp.concatenate([product.astype(BF16), *three_parts(own)], axis=1)

        def backward_kernel(
            place, product, gram, a, b, c, raw, x, samples_out, columns_out, mine, other
        ):
            total, own = product[...], gram[...]
            for ref in (a, b, c):
                total = total + ref[:, :row_count].astype(F32)
                parts = [
                    ref[:, row_count + width * i : row_count + width * (i + 1)].astype(F32)
                    for i in range(3)
                ]
                own = own + (parts[0] + (parts[1] + parts[2]))
            factor = inverse_factor(own / snp_count, False)
            samples = exact_dot(factor, total, 1, 0)
            samples_out[...] = samples
            columns_out[...] = exact_dot(factor, raw[...], 1, 0)
            write_send(
                split_dot(samples, x[...], 0),
                exact_dot(samples, samples, 1, 1),
                core_of(place),
                mine,
                other,
            )

        def last_kernel(place, *refs):
            tiles, (samples, basis, projection, whole) = refs[:8], refs[8:]
            columns, gram = read_sum(place, tiles, whole)
            factor = inverse_factor(gram / sample_count, True)
            basis[...] = exact_dot(factor, samples[...], 1, 0)
            projection[...] = exact_dot(factor / math.sqrt(sample_count), columns, 1, 0)

        samples_shape = shape_of((width, row_count))
        columns_shape = shape_of((width, col_width))
        samples, mine, other = call_with_place(
            first_kernel,
            (samples_shape, part_shape, part_shape),
            start,
            *start_others,
            mixed,
            *mixed_others,
            left_rows,
            matrix,
            scalars=(batch_sizes, bits, singular),
        )
        columns, dtype = None, F32
        for _ in range(ITERS):
            raw, product, gram, wire = call_with_place(
                forward_kernel,
                (
                    columns_shape,
                    samples_shape,
                    shape_of((width, width)),
                    shape_of((width, packed), BF16),
                ),
                *samp_sum(mine, other, dtype),
                matrix,
                scratch=whole_scratch,
            )
            dtype = BF16
            samples, columns, mine, other = call_with_place(
                backward_kernel,
                (samples_shape, columns_shape, part_shape, part_shape),
                product,
                gram,
                *snp_others(wire),
                raw,
                matrix,
            )
        basis, projection = call_with_place(
            last_kernel,
            (samples_shape, columns_shape),
            *samp_sum(mine, other, dtype),
            samples,
            scratch=whole_scratch,
        )
        return (basis.T, projection.T, columns.T)

    in_specs = (
        P(samp_axes, "snp"),
        P("snp"),
        P(samp_axes, None),
        P(),
        P(("snp", *samp_axes), None),
        P("snp", None),
        P(),
        P(),
        P(),
    )
    out_specs = (P(samp_axes, None), P("snp", None), P("snp", None))
    return jax.shard_map(
        on_device, mesh=fine, in_specs=in_specs, out_specs=out_specs, check_vma=False
    )
```

```python
import math

import jax
import jax.numpy as jnp
from jax import lax
from jax.experimental import pallas as pl
from jax.experimental.pallas import tpu as pltpu
from jax.sharding import Mesh, PartitionSpec as P

BATCHES = 12
BLOCK = 256
ITERS = 2
BLOCKS = 16
LANES = 128
SUB = 8
GROUP = 32
F32 = jnp.float32
BF16 = jnp.bfloat16
HIGH = lax.Precision.HIGHEST


def exact_dot(a, b, a_dim, b_dim):
    return lax.dot_general(
        a, b, (((a_dim,), (b_dim,)), ((), ())), precision=HIGH, preferred_element_type=F32
    )


def split_dot(values, matrix, dim):
    high = values.astype(BF16)
    low = (values - high.astype(F32)).astype(BF16)
    both = jnp.concatenate([high, low], axis=0)
    out = lax.dot_general(
        both, matrix, (((1,), (dim,)), ((), ())), preferred_element_type=F32
    )
    rows = values.shape[0]
    return out[:rows] + out[rows:]


def inverse_factor(gram, lower):
    size = gram.shape[0]
    across = lax.broadcasted_iota(jnp.int32, (size, size), 1)
    down = lax.broadcasted_iota(jnp.int32, (size, size), 0)
    wide = jnp.concatenate([gram, (across == down).astype(F32)], axis=1)
    count = size // SUB
    shape = (SUB, 2 * size)
    tiles = [wide[SUB * t : SUB * (t + 1)] for t in range(count)]
    sub = lax.broadcasted_iota(jnp.int32, shape, 0)
    step = 1 if lower else -1
    for a in range(count)[::step]:
        active = range(a, count) if lower else range(a + 1)
        cols = {
            t: [
                jnp.broadcast_to(tiles[t][:, SUB * a + k : SUB * a + k + 1], shape)
                for k in range(SUB)
            ]
            for t in active
        }
        scale = jnp.zeros(shape, F32)
        for k in range(SUB)[::step]:
            pivot = jnp.broadcast_to(cols[a][k][k : k + 1], shape)
            inverse = 1.0 / pivot
            scale = jnp.where(sub == k, pivot, scale)
            keep = (sub > k) if lower else (sub < k)
            rest = range(k + 1, SUB) if lower else range(k)
            row = jnp.broadcast_to(tiles[a][k : k + 1], shape) * inverse
            heads = {j: jnp.broadcast_to(cols[a][j][k : k + 1], shape) * inverse for j in rest}
            for t in active:
                column = cols[t][k]
                if t == a:
                    column = jnp.where(keep, column, 0.0)
                tiles[t] = tiles[t] - column * row
                for j in rest:
                    cols[t][j] = cols[t][j] - column * heads[j]
        tiles[a] = tiles[a] * lax.rsqrt(scale)
    return jnp.concatenate(tiles, axis=0)[:, size:]


def kernel_call(body, out_shapes, *operands):
    return pl.pallas_call(
        body,
        out_shape=out_shapes,
        compiler_params=pltpu.CompilerParams(vmem_limit_bytes=48 * 1024 * 1024),
    )(*operands)


def shape_of(shape, dtype=F32):
    return jax.ShapeDtypeStruct(shape, dtype)


def write_send(columns, gram, core, mine, other):
    rows = columns.shape[0]
    blank = jnp.zeros((rows, LANES - gram.shape[1]), F32)
    value = jnp.concatenate([columns, gram, blank], axis=1)
    top, bottom = value[: rows // 2], value[rows // 2 :]
    mine[...] = jnp.where(core == 0, top, bottom)
    other[...] = jnp.where(core == 0, bottom, top)


def three_parts(value):
    high = value.astype(BF16)
    rest = value - high.astype(F32)
    middle = rest.astype(BF16)
    return [high, middle, (rest - middle.astype(F32)).astype(BF16)]


def solution(mesh):
    samp, snp = mesh.shape["samp"], mesh.shape["snp"]
    chips, ring = samp // 2, 4
    depth = chips // ring
    fine = Mesh(mesh.devices.reshape(depth, ring, 2, snp), ("z", "x", "core", "snp"))
    samp_axes = ("z", "x", "core")

    def swap(value):
        return lax.ppermute(value, "core", [(0, 1), (1, 0)])

    def snp_others(value):
        return [
            lax.ppermute(value, "snp", [(i, (i + k) % snp) for i in range(snp)])
            for k in range(1, snp)
        ]

    def x_shift(value, k):
        return lax.ppermute(value, "x", [(i, (i + k) % ring) for i in range(ring)])

    def on_device(
        genotype,
        freqs,
        left_factors,
        singular,
        right_factors,
        sketch,
        batch_sizes,
        missing_batch,
        missing_block,
    ):
        row_count, col_width = genotype.shape
        rank = left_factors.shape[1]
        width = sketch.shape[1]
        sample_count = row_count * samp
        snp_count = col_width * snp
        place = lax.axis_index((*samp_axes, "snp")).reshape(1).astype(jnp.int32)
        local_blocks = col_width // BLOCK
        omega = sketch.T

        def core_of(place):
            return place[0] // snp % 2

        def x_of(place):
            return place[0] // (snp * 2) % ring

        def call_with_place(body, outs, *operands, scalars=(), scratch=()):
            smem = pl.BlockSpec(memory_space=pltpu.SMEM)
            specs = [smem] * (1 + len(scalars)) + [
                pl.BlockSpec(memory_space=pltpu.VMEM) for _ in operands
            ]
            return pl.pallas_call(
                body,
                out_shape=outs,
                in_specs=specs,
                scratch_shapes=scratch,
                compiler_params=pltpu.CompilerParams(vmem_limit_bytes=48 * 1024 * 1024),
            )(place, *scalars, *operands)

        def batch_ids(place, sizes, shape, axis):
            ids = lax.broadcasted_iota(jnp.int32, shape, axis) + place[0] // snp * row_count
            batch = jnp.zeros(shape, jnp.int32)
            end = jnp.int32(0)
            for b in range(BATCHES - 1):
                end = end + sizes[b]
                batch = batch + (ids >= end).astype(jnp.int32)
            return batch

        def gone_in(bits, batch):
            return ((jnp.broadcast_to(bits, batch.shape) >> batch) & 1) == 1

        chunk = LANES

        def observe_kernel(
            place, sizes_in, batch_in, block_in, geno_in, freq_in, om_in,
            obs, start, bits,
            sizes, tile_batch, tile_block, geno, freq, om, sems,
        ):
            copies = [
                pltpu.make_async_copy(source, target, sems.at[i])
                for i, (source, target) in enumerate(
                    [
                        (batch_in, tile_batch),
                        (block_in, tile_block),
                        (sizes_in, sizes),
                        (freq_in, freq),
                    ]
                    + [
                        (geno_in.at[pl.ds(low, chunk)], geno.at[pl.ds(low, chunk)])
                        for low in range(0, row_count, chunk)
                    ]
                    + [(om_in, om)]
                )
            ]
            for copy in copies:
                copy.start()
            for block in range(BLOCKS):
                bits[block] = 0
            copies[0].wait()
            copies[1].wait()
            for i in range(tile_batch.shape[0]):
                block = tile_block[i]
                bits[block] = bits[block] | (1 << tile_batch[i])
            copies[2].wait()
            copies[3].wait()
            batch = batch_ids(place, sizes, (row_count, LANES), 0)
            own_bits = [bits[place[0] % snp * local_blocks + j] for j in range(local_blocks)]
            for n, top in enumerate(range(0, row_count, chunk)):
                copies[4 + n].wait()
                rows = slice(top, top + chunk)
                for j in range(local_blocks):
                    gone = gone_in(own_bits[j], batch[rows])
                    for low in range(BLOCK * j, BLOCK * (j + 1), LANES):
                        at = slice(low, low + LANES)
                        values = geno[rows, at].astype(F32) - 2.0 * freq[:, at]
                        obs[rows, at] = jnp.where(gone, 0.0, values).astype(BF16)
            copies[-1].wait()
            start[...] = lax.dot_general(
                om[...], obs[...], (((1,), (1,)), ((), ())), preferred_element_type=F32
            )

        vmem = pl.BlockSpec(memory_space=pltpu.VMEM)
        smem = pl.BlockSpec(memory_space=pltpu.SMEM)
        tiles = missing_batch.shape
        observed, start, bits = pl.pallas_call(
            observe_kernel,
            out_shape=(
                shape_of((row_count, col_width), BF16),
                shape_of((width, row_count)),
                shape_of((BLOCKS,), jnp.int32),
            ),
            in_specs=[smem] + [pl.BlockSpec(memory_space=pltpu.HBM)] * 6,
            out_specs=(vmem, vmem, smem),
            scratch_shapes=[
                pltpu.SMEM(batch_sizes.shape, jnp.int32),
                pltpu.SMEM(tiles, jnp.int32),
                pltpu.SMEM(tiles, jnp.int32),
                pltpu.VMEM((row_count, col_width), jnp.int32),
                pltpu.VMEM((1, col_width), F32),
                pltpu.VMEM((width, col_width), BF16),
                pltpu.SemaphoreType.DMA((5 + row_count // chunk,)),
            ],
            compiler_params=pltpu.CompilerParams(vmem_limit_bytes=63 * 1024 * 1024),
        )(
            place,
            batch_sizes,
            missing_batch,
            missing_block,
            genotype,
            freqs.reshape(1, col_width),
            omega,
        )

        def pack_kernel(place, bits, mine, other, spread):
            del bits
            first = core_of(place) == 0
            low = jnp.where(first, mine[...], other[...])
            high = jnp.where(first, other[...], mine[...])
            fill = jnp.zeros((SUB, GROUP - rank), F32)
            pieces = []
            for part in (low, high):
                for top in range(0, part.shape[0], SUB):
                    pieces += [part[top : top + SUB], fill]
            tile = jnp.concatenate(pieces, axis=1)
            spread[...] = jnp.broadcast_to(tile[None], spread.shape)

        right_tiles = lax.all_to_all(
            call_with_place(
                pack_kernel,
                shape_of((chips, SUB, LANES)),
                right_factors,
                swap(right_factors),
                scalars=(bits,),
            ),
            ("z", "x"),
            0,
            0,
        )
        start_others = snp_others(start)

        def right_rows(tiles):
            value = tiles[...]
            parts = [value[:, :, g : g + GROUP] for g in range(0, LANES, GROUP)]
            return jnp.stack(parts, axis=1).reshape(col_width, GROUP)

        def weight_rows(scale, left):
            rows = [left[r : r + 1, :] * scale[r] for r in range(rank)]
            return jnp.concatenate(
                [*rows, jnp.zeros((GROUP - rank, row_count), F32)], axis=0
            )

        def mix_kernel(place, tiles, om, mixed):
            right = right_rows(tiles)
            pieces = [
                exact_dot(
                    om[:, BLOCK * j : BLOCK * (j + 1)].astype(F32),
                    right[BLOCK * j : BLOCK * (j + 1)],
                    1,
                    0,
                )
                for j in range(local_blocks)
            ]
            mixed[...] = jnp.concatenate(pieces, axis=1)

        def build_kernel(place, sizes, bits, scale, obs, left, tiles, x_out):
            right = right_rows(tiles)
            weight = weight_rows(scale, left).T
            batch = batch_ids(place, sizes, (row_count, BLOCK), 0)
            for j in range(local_blocks):
                at = slice(BLOCK * j, BLOCK * (j + 1))
                lowrank = exact_dot(weight, right[at], 1, 1)
                gone = gone_in(bits[place[0] % snp * local_blocks + j], batch)
                x_out[:, at] = jnp.where(gone, lowrank, obs[:, at].astype(F32)).astype(BF16)

        mixed = call_with_place(
            mix_kernel,
            shape_of((width, local_blocks * GROUP)),
            right_tiles,
            omega,
        )
        mixed_others = snp_others(mixed)
        left_rows = left_factors.T
        matrix = call_with_place(
            build_kernel,
            shape_of((row_count, col_width), BF16),
            observed,
            left_rows,
            right_tiles,
            scalars=(batch_sizes, bits, singular),
        )

        packed = row_count + 3 * width
        sum_width = col_width + LANES
        part_shape = shape_of((width // 2, sum_width))
        tile_shape = shape_of((SUB, sum_width))

        def split_kernel(place, mine, got, own, *sends):
            for k, ref in enumerate((own, *sends)):
                rows = pl.ds(pl.multiple_of((x_of(place) + k) % ring * SUB, SUB), SUB)
                ref[...] = mine[rows, :] + got[rows, :]

        def spread_kernel(place, own, a, b, c, out):
            total = own[...] + a[...] + b[...] + c[...]
            if out.dtype == BF16:
                columns, gram = total[:, :col_width], total[:, col_width : col_width + width]
                total = jnp.concatenate(
                    [
                        columns.astype(BF16),
                        *three_parts(gram),
                        jnp.zeros((SUB, out.shape[2] - col_width - 3 * width), BF16),
                    ],
                    axis=1,
                )
            out[...] = jnp.broadcast_to(total[None], out.shape)

        def gather_kernel(place, parts, out):
            total = jnp.sum(parts[...].astype(F32), axis=0)
            if parts.dtype == BF16:
                grams = [
                    total[:, col_width + width * i : col_width + width * (i + 1)]
                    for i in range(3)
                ]
                total = jnp.concatenate(
                    [
                        total[:, :col_width],
                        grams[0] + (grams[1] + grams[2]),
                        jnp.zeros((SUB, LANES - width), F32),
                    ],
                    axis=1,
                )
            out[...] = jnp.broadcast_to(total[None], out.shape)

        def samp_sum(mine, other, dtype):
            own, *sends = call_with_place(
                split_kernel, (tile_shape,) * ring, mine, swap(other)
            )
            gots = [x_shift(send, k) for k, send in enumerate(sends, 1)]
            wide = sum_width if dtype == F32 else col_width + 2 * LANES
            spread = call_with_place(
                spread_kernel, shape_of((depth, SUB, wide), dtype), own, *gots
            )
            tiles = call_with_place(
                gather_kernel,
                shape_of((ring, *tile_shape.shape)),
                lax.all_to_all(spread, "z", 0, 0),
            )
            near = lax.all_to_all(tiles, "x", 0, 0)
            return [near, swap(near)]

        def read_sum(place, tiles, whole):
            half = width // 2
            for side, ref in zip((core_of(place), 1 - core_of(place)), tiles):
                whole[pl.ds(pl.multiple_of(side * half, half), half), :] = ref[...].reshape(
                    half, sum_width
                )
            return whole[:, :col_width], whole[:, col_width : col_width + width]

        whole_scratch = [pltpu.VMEM((width, sum_width), F32)]

        def first_kernel(
            place, sizes, bits, scale, own, a, b, c, q0, q1, q2, q3, left, x,
            samples_out, mine, other,
        ):
            samples = own[...] + a[...] + b[...] + c[...]
            batch = batch_ids(place, sizes, (1, row_count), 1)
            weight = weight_rows(scale, left)
            for k, q in enumerate((q0, q1, q2, q3)):
                source = (place[0] + (snp - k)) % snp
                masked = [
                    jnp.where(gone_in(bits[source * local_blocks + j], batch), weight, 0.0)
                    for j in range(local_blocks)
                ]
                samples = samples + exact_dot(q[...], jnp.concatenate(masked, axis=0), 1, 0)
            samples_out[...] = samples
            write_send(
                split_dot(samples, x[...], 0),
                exact_dot(samples, samples, 1, 1),
                core_of(place),
                mine,
                other,
            )

        def forward_kernel(place, *refs):
            tiles, (x, raw_out, product_out, gram_out, wire, whole) = refs[:2], refs[2:]
            columns, gram = read_sum(place, tiles, whole)
            raw = exact_dot(inverse_factor(gram / sample_count, True), columns, 1, 0)
            raw_out[...] = raw
            product = split_dot(raw, x[...], 1)
            own = exact_dot(raw, raw, 1, 1)
            product_out[...] = product
            gram_out[...] = own
            wire[...] = jnp.concatenate([product.astype(BF16), *three_parts(own)], axis=1)

        def backward_kernel(
            place, product, gram, a, b, c, raw, x, samples_out, columns_out, mine, other
        ):
            total, own = product[...], gram[...]
            for ref in (a, b, c):
                total = total + ref[:, :row_count].astype(F32)
                parts = [
                    ref[:, row_count + width * i : row_count + width * (i + 1)].astype(F32)
                    for i in range(3)
                ]
                own = own + (parts[0] + (parts[1] + parts[2]))
            factor = inverse_factor(own / snp_count, False)
            samples = exact_dot(factor, total, 1, 0)
            samples_out[...] = samples
            columns_out[...] = exact_dot(factor, raw[...], 1, 0)
            write_send(
                split_dot(samples, x[...], 0),
                exact_dot(samples, samples, 1, 1),
                core_of(place),
                mine,
                other,
            )

        def last_kernel(place, *refs):
            tiles, (samples, basis, projection, whole) = refs[:2], refs[2:]
            columns, gram = read_sum(place, tiles, whole)
            factor = inverse_factor(gram / sample_count, True)
            basis[...] = exact_dot(factor, samples[...], 1, 0)
            projection[...] = exact_dot(factor / math.sqrt(sample_count), columns, 1, 0)

        samples_shape = shape_of((width, row_count))
        columns_shape = shape_of((width, col_width))
        samples, mine, other = call_with_place(
            first_kernel,
            (samples_shape, part_shape, part_shape),
            start,
            *start_others,
            mixed,
            *mixed_others,
            left_rows,
            matrix,
            scalars=(batch_sizes, bits, singular),
        )
        columns, dtype = None, F32
        for _ in range(ITERS):
            raw, product, gram, wire = call_with_place(
                forward_kernel,
                (
                    columns_shape,
                    samples_shape,
                    shape_of((width, width)),
                    shape_of((width, packed), BF16),
                ),
                *samp_sum(mine, other, dtype),
                matrix,
                scratch=whole_scratch,
            )
            dtype = BF16
            samples, columns, mine, other = call_with_place(
                backward_kernel,
                (samples_shape, columns_shape, part_shape, part_shape),
                product,
                gram,
                *snp_others(wire),
                raw,
                matrix,
            )
        basis, projection = call_with_place(
            last_kernel,
            (samples_shape, columns_shape),
            *samp_sum(mine, other, dtype),
            samples,
            scratch=whole_scratch,
        )
        return (basis.T, projection.T, columns.T)

    in_specs = (
        P(samp_axes, "snp"),
        P("snp"),
        P(samp_axes, None),
        P(),
        P(("snp", *samp_axes), None),
        P("snp", None),
        P(),
        P(),
        P(),
    )
    out_specs = (P(samp_axes, None), P("snp", None), P("snp", None))
    return jax.shard_map(
        on_device, mesh=fine, in_specs=in_specs, out_specs=out_specs, check_vma=False
    )
```

```python
import math

import jax
import jax.numpy as jnp
from jax import lax
from jax.experimental import pallas as pl
from jax.experimental.pallas import tpu as pltpu
from jax.sharding import Mesh, PartitionSpec as P

BATCHES = 12
BLOCK = 256
ITERS = 2
BLOCKS = 16
LANES = 128
SUB = 8
GROUP = 32
F32 = jnp.float32
BF16 = jnp.bfloat16
HIGH = lax.Precision.HIGHEST


def exact_dot(a, b, a_dim, b_dim):
    return lax.dot_general(
        a, b, (((a_dim,), (b_dim,)), ((), ())), precision=HIGH, preferred_element_type=F32
    )


def split_dot(values, matrix, dim):
    high = values.astype(BF16)
    low = (values - high.astype(F32)).astype(BF16)
    both = jnp.concatenate([high, low], axis=0)
    out = lax.dot_general(
        both, matrix, (((1,), (dim,)), ((), ())), preferred_element_type=F32
    )
    rows = values.shape[0]
    return out[:rows] + out[rows:]


def inverse_factor(gram, lower):
    size = gram.shape[0]
    across = lax.broadcasted_iota(jnp.int32, (size, size), 1)
    down = lax.broadcasted_iota(jnp.int32, (size, size), 0)
    wide = jnp.concatenate([gram, (across == down).astype(F32)], axis=1)
    count = size // SUB
    shape = (SUB, 2 * size)
    tiles = [wide[SUB * t : SUB * (t + 1)] for t in range(count)]
    sub = lax.broadcasted_iota(jnp.int32, shape, 0)
    step = 1 if lower else -1

    def spread_row(value, k):
        return jnp.broadcast_to(value[k : k + 1], shape)

    for a in range(count)[::step]:
        active = range(a, count) if lower else range(a + 1)
        cols = {
            t: [
                jnp.broadcast_to(tiles[t][:, SUB * a + k : SUB * a + k + 1], shape)
                for k in range(SUB)
            ]
            for t in active
        }
        scale = jnp.zeros(shape, F32)
        order = range(SUB)[::step]
        for p, q in zip(order[::2], order[1::2]):
            aa, bb = spread_row(cols[a][p], p), spread_row(cols[a][p], q)
            cc = spread_row(cols[a][q], q)
            det = aa * cc - bb * bb
            inverse, first = 1.0 / det, 1.0 / aa
            ia, ib, ic = cc * inverse, bb * inverse, aa * inverse
            scale = jnp.where(sub == p, aa, jnp.where(sub == q, det * first, scale))
            keep = (sub > q) if lower else (sub < q)
            rest = [j for j in order if (j > q if lower else j < q)]

            def solved(value):
                vp, vq = spread_row(value, p), spread_row(value, q)
                return ia * vp - ib * vq, ic * vq - ib * vp

            row_p = spread_row(tiles[a], p)
            up, uq = solved(tiles[a])
            heads = {j: solved(cols[a][j]) for j in rest}
            for t in active:
                cp, cq = cols[t][p], cols[t][q]
                for j in rest:
                    cols[t][j] = cols[t][j] - (cp * heads[j][0] + cq * heads[j][1])
                if t == a:
                    inner = jnp.where(sub == q, bb * first, 0.0) * row_p
                    cp, cq = jnp.where(keep, cp, 0.0), jnp.where(keep, cq, 0.0)
                    tiles[t] = tiles[t] - (cp * up + cq * uq) - inner
                else:
                    tiles[t] = tiles[t] - (cp * up + cq * uq)
        tiles[a] = tiles[a] * lax.rsqrt(scale)
    return jnp.concatenate(tiles, axis=0)[:, size:]


def shape_of(shape, dtype=F32):
    return jax.ShapeDtypeStruct(shape, dtype)


def write_send(columns, gram, core, mine, other):
    rows = columns.shape[0]
    blank = jnp.zeros((rows, LANES - gram.shape[1]), F32)
    value = jnp.concatenate([columns, gram, blank], axis=1)
    top, bottom = value[: rows // 2], value[rows // 2 :]
    mine[...] = jnp.where(core == 0, top, bottom)
    other[...] = jnp.where(core == 0, bottom, top)


def three_parts(value):
    high = value.astype(BF16)
    rest = value - high.astype(F32)
    middle = rest.astype(BF16)
    return [high, middle, (rest - middle.astype(F32)).astype(BF16)]


def solution(mesh):
    samp, snp = mesh.shape["samp"], mesh.shape["snp"]
    chips, ring = samp // 2, 4
    depth = chips // ring
    fine = Mesh(mesh.devices.reshape(depth, ring, 2, snp), ("z", "x", "core", "snp"))
    samp_axes = ("z", "x", "core")

    def swap(value):
        return lax.ppermute(value, "core", [(0, 1), (1, 0)])

    def snp_others(value):
        return [
            lax.ppermute(value, "snp", [(i, (i + k) % snp) for i in range(snp)])
            for k in range(1, snp)
        ]

    def x_shift(value, k):
        return lax.ppermute(value, "x", [(i, (i + k) % ring) for i in range(ring)])

    def on_device(
        genotype,
        freqs,
        left_factors,
        singular,
        right_factors,
        sketch,
        batch_sizes,
        missing_batch,
        missing_block,
    ):
        row_count, col_width = genotype.shape
        rank = left_factors.shape[1]
        width = sketch.shape[1]
        sample_count = row_count * samp
        snp_count = col_width * snp
        place = lax.axis_index((*samp_axes, "snp")).reshape(1).astype(jnp.int32)
        local_blocks = col_width // BLOCK
        omega = sketch.T

        def core_of(place):
            return place[0] // snp % 2

        def x_of(place):
            return place[0] // (snp * 2) % ring

        def call_with_place(body, outs, *operands, scalars=(), scratch=()):
            smem = pl.BlockSpec(memory_space=pltpu.SMEM)
            specs = [smem] * (1 + len(scalars)) + [
                pl.BlockSpec(memory_space=pltpu.VMEM) for _ in operands
            ]
            return pl.pallas_call(
                body,
                out_shape=outs,
                in_specs=specs,
                scratch_shapes=scratch,
                compiler_params=pltpu.CompilerParams(vmem_limit_bytes=48 * 1024 * 1024),
            )(place, *scalars, *operands)

        def batch_ids(place, sizes, shape, axis):
            ids = lax.broadcasted_iota(jnp.int32, shape, axis) + place[0] // snp * row_count
            batch = jnp.zeros(shape, jnp.int32)
            end = jnp.int32(0)
            for b in range(BATCHES - 1):
                end = end + sizes[b]
                batch = batch + (ids >= end).astype(jnp.int32)
            return batch

        def gone_in(bits, batch):
            return ((jnp.broadcast_to(bits, batch.shape) >> batch) & 1) == 1

        chunk = LANES

        def observe_kernel(
            place, sizes_in, batch_in, block_in, geno_in, freq_in, om_in,
            obs, start, bits,
            sizes, tile_batch, tile_block, geno, freq, om, sems,
        ):
            copies = [
                pltpu.make_async_copy(source, target, sems.at[i])
                for i, (source, target) in enumerate(
                    [
                        (batch_in, tile_batch),
                        (block_in, tile_block),
                        (sizes_in, sizes),
                        (freq_in, freq),
                    ]
                    + [
                        (geno_in.at[pl.ds(low, chunk)], geno.at[pl.ds(low, chunk)])
                        for low in range(0, row_count, chunk)
                    ]
                    + [(om_in, om)]
                )
            ]
            for copy in copies:
                copy.start()
            for block in range(BLOCKS):
                bits[block] = 0
            copies[0].wait()
            copies[1].wait()
            for i in range(tile_batch.shape[0]):
                block = tile_block[i]
                bits[block] = bits[block] | (1 << tile_batch[i])
            copies[2].wait()
            copies[3].wait()
            batch = batch_ids(place, sizes, (row_count, LANES), 0)
            own_bits = [bits[place[0] % snp * local_blocks + j] for j in range(local_blocks)]
            for n, top in enumerate(range(0, row_count, chunk)):
                copies[4 + n].wait()
                rows = slice(top, top + chunk)
                for j in range(local_blocks):
                    gone = gone_in(own_bits[j], batch[rows])
                    for low in range(BLOCK * j, BLOCK * (j + 1), LANES):
                        at = slice(low, low + LANES)
                        values = geno[rows, at].astype(F32) - 2.0 * freq[:, at]
                        obs[rows, at] = jnp.where(gone, 0.0, values).astype(BF16)
            copies[-1].wait()
            start[...] = lax.dot_general(
                om[...], obs[...], (((1,), (1,)), ((), ())), preferred_element_type=F32
            )

        vmem = pl.BlockSpec(memory_space=pltpu.VMEM)
        smem = pl.BlockSpec(memory_space=pltpu.SMEM)
        tiles = missing_batch.shape
        observed, start, bits = pl.pallas_call(
            observe_kernel,
            out_shape=(
                shape_of((row_count, col_width), BF16),
                shape_of((width, row_count)),
                shape_of((BLOCKS,), jnp.int32),
            ),
            in_specs=[smem] + [pl.BlockSpec(memory_space=pltpu.HBM)] * 6,
            out_specs=(vmem, vmem, smem),
            scratch_shapes=[
                pltpu.SMEM(batch_sizes.shape, jnp.int32),
                pltpu.SMEM(tiles, jnp.int32),
                pltpu.SMEM(tiles, jnp.int32),
                pltpu.VMEM((row_count, col_width), jnp.int32),
                pltpu.VMEM((1, col_width), F32),
                pltpu.VMEM((width, col_width), BF16),
                pltpu.SemaphoreType.DMA((5 + row_count // chunk,)),
            ],
            compiler_params=pltpu.CompilerParams(vmem_limit_bytes=63 * 1024 * 1024),
        )(
            place,
            batch_sizes,
            missing_batch,
            missing_block,
            genotype,
            freqs.reshape(1, col_width),
            omega,
        )

        def pack_kernel(place, mine, other, spread):
            first = core_of(place) == 0
            low = jnp.where(first, mine[...], other[...])
            high = jnp.where(first, other[...], mine[...])
            fill = jnp.zeros((SUB, GROUP - rank), F32)
            pieces = []
            for part in (low, high):
                for top in range(0, part.shape[0], SUB):
                    pieces += [part[top : top + SUB], fill]
            tile = jnp.concatenate(pieces, axis=1)
            spread[...] = jnp.broadcast_to(tile[None], spread.shape)

        right_tiles = lax.all_to_all(
            call_with_place(
                pack_kernel,
                shape_of((chips, SUB, LANES)),
                right_factors,
                swap(right_factors),
            ),
            ("z", "x"),
            0,
            0,
        )
        start_others = snp_others(start)

        def right_rows(tiles):
            value = tiles[...]
            parts = [value[:, :, g : g + GROUP] for g in range(0, LANES, GROUP)]
            return jnp.stack(parts, axis=1).reshape(col_width, GROUP)

        def weight_rows(scale, left):
            rows = [left[r : r + 1, :] * scale[r] for r in range(rank)]
            return jnp.concatenate(
                [*rows, jnp.zeros((GROUP - rank, row_count), F32)], axis=0
            )

        def mix_kernel(place, tiles, om, mixed):
            right = right_rows(tiles)
            pieces = [
                exact_dot(
                    om[:, BLOCK * j : BLOCK * (j + 1)].astype(F32),
                    right[BLOCK * j : BLOCK * (j + 1)],
                    1,
                    0,
                )
                for j in range(local_blocks)
            ]
            mixed[...] = jnp.concatenate(pieces, axis=1)

        def build_kernel(place, sizes, bits, scale, obs, left, tiles, x_out):
            right = right_rows(tiles)
            weight = weight_rows(scale, left).T
            batch = batch_ids(place, sizes, (row_count, BLOCK), 0)
            for j in range(local_blocks):
                at = slice(BLOCK * j, BLOCK * (j + 1))
                lowrank = exact_dot(weight, right[at], 1, 1)
                gone = gone_in(bits[place[0] % snp * local_blocks + j], batch)
                x_out[:, at] = jnp.where(gone, lowrank, obs[:, at].astype(F32)).astype(BF16)

        mixed = call_with_place(
            mix_kernel,
            shape_of((width, local_blocks * GROUP)),
            right_tiles,
            omega,
        )
        mixed_others = snp_others(mixed)
        left_rows = left_factors.T
        matrix = call_with_place(
            build_kernel,
            shape_of((row_count, col_width), BF16),
            observed,
            left_rows,
            right_tiles,
            scalars=(batch_sizes, bits, singular),
        )

        packed = row_count + 3 * width
        sum_width = col_width + LANES
        part_shape = shape_of((width // 2, sum_width))
        tile_shape = shape_of((SUB, sum_width))

        def split_kernel(place, mine, got, own, *sends):
            for k, ref in enumerate((own, *sends)):
                rows = pl.ds(pl.multiple_of((x_of(place) + k) % ring * SUB, SUB), SUB)
                ref[...] = mine[rows, :] + got[rows, :]

        def spread_kernel(place, own, a, b, c, out):
            total = own[...] + a[...] + b[...] + c[...]
            if out.dtype == BF16:
                columns, gram = total[:, :col_width], total[:, col_width : col_width + width]
                total = jnp.concatenate(
                    [
                        columns.astype(BF16),
                        *three_parts(gram),
                        jnp.zeros((SUB, out.shape[2] - col_width - 3 * width), BF16),
                    ],
                    axis=1,
                )
            out[...] = jnp.broadcast_to(total[None], out.shape)

        def gather_kernel(place, parts, out):
            total = jnp.sum(parts[...].astype(F32), axis=0)
            if parts.dtype == BF16:
                grams = [
                    total[:, col_width + width * i : col_width + width * (i + 1)]
                    for i in range(3)
                ]
                total = jnp.concatenate(
                    [
                        total[:, :col_width],
                        grams[0] + (grams[1] + grams[2]),
                        jnp.zeros((SUB, LANES - width), F32),
                    ],
                    axis=1,
                )
            out[...] = jnp.broadcast_to(total[None], out.shape)

        def samp_sum(mine, other, dtype):
            own, *sends = call_with_place(
                split_kernel, (tile_shape,) * ring, mine, swap(other)
            )
            gots = [x_shift(send, k) for k, send in enumerate(sends, 1)]
            wide = sum_width if dtype == F32 else col_width + 2 * LANES
            spread = call_with_place(
                spread_kernel, shape_of((depth, SUB, wide), dtype), own, *gots
            )
            tiles = call_with_place(
                gather_kernel,
                shape_of((ring, *tile_shape.shape)),
                lax.all_to_all(spread, "z", 0, 0),
            )
            near = lax.all_to_all(tiles, "x", 0, 0)
            return [near, swap(near)]

        def read_sum(place, tiles, whole):
            half = width // 2
            for side, ref in zip((core_of(place), 1 - core_of(place)), tiles):
                whole[pl.ds(pl.multiple_of(side * half, half), half), :] = ref[...].reshape(
                    half, sum_width
                )
            return whole[:, :col_width], whole[:, col_width : col_width + width]

        whole_scratch = [pltpu.VMEM((width, sum_width), F32)]

        def first_kernel(
            place, sizes, bits, scale, own, a, b, c, q0, q1, q2, q3, left, x,
            samples_out, mine, other,
        ):
            samples = own[...] + a[...] + b[...] + c[...]
            batch = batch_ids(place, sizes, (1, row_count), 1)
            weight = weight_rows(scale, left)
            for k, q in enumerate((q0, q1, q2, q3)):
                source = (place[0] + (snp - k)) % snp
                masked = [
                    jnp.where(gone_in(bits[source * local_blocks + j], batch), weight, 0.0)
                    for j in range(local_blocks)
                ]
                samples = samples + exact_dot(q[...], jnp.concatenate(masked, axis=0), 1, 0)
            samples_out[...] = samples
            write_send(
                split_dot(samples, x[...], 0),
                exact_dot(samples, samples, 1, 1),
                core_of(place),
                mine,
                other,
            )

        def forward_kernel(place, *refs):
            tiles, (x, raw_out, product_out, gram_out, wire, whole) = refs[:2], refs[2:]
            columns, gram = read_sum(place, tiles, whole)
            raw = exact_dot(inverse_factor(gram / sample_count, True), columns, 1, 0)
            raw_out[...] = raw
            product = split_dot(raw, x[...], 1)
            own = exact_dot(raw, raw, 1, 1)
            product_out[...] = product
            gram_out[...] = own
            wire[...] = jnp.concatenate([product.astype(BF16), *three_parts(own)], axis=1)

        def backward_kernel(
            place, product, gram, a, b, c, raw, x, samples_out, columns_out, mine, other
        ):
            total, own = product[...], gram[...]
            for ref in (a, b, c):
                total = total + ref[:, :row_count].astype(F32)
                parts = [
                    ref[:, row_count + width * i : row_count + width * (i + 1)].astype(F32)
                    for i in range(3)
                ]
                own = own + (parts[0] + (parts[1] + parts[2]))
            factor = inverse_factor(own / snp_count, False)
            samples = exact_dot(factor, total, 1, 0)
            samples_out[...] = samples
            columns_out[...] = exact_dot(factor, raw[...], 1, 0)
            write_send(
                split_dot(samples, x[...], 0),
                exact_dot(samples, samples, 1, 1),
                core_of(place),
                mine,
                other,
            )

        def last_kernel(place, *refs):
            tiles, (samples, basis, projection, whole) = refs[:2], refs[2:]
            columns, gram = read_sum(place, tiles, whole)
            factor = inverse_factor(gram / sample_count, True)
            basis[...] = exact_dot(factor, samples[...], 1, 0)
            projection[...] = exact_dot(factor / math.sqrt(sample_count), columns, 1, 0)

        samples_shape = shape_of((width, row_count))
        columns_shape = shape_of((width, col_width))
        samples, mine, other = call_with_place(
            first_kernel,
            (samples_shape, part_shape, part_shape),
            start,
            *start_others,
            mixed,
            *mixed_others,
            left_rows,
            matrix,
            scalars=(batch_sizes, bits, singular),
        )
        columns, dtype = None, F32
        for _ in range(ITERS):
            raw, product, gram, wire = call_with_place(
                forward_kernel,
                (
                    columns_shape,
                    samples_shape,
                    shape_of((width, width)),
                    shape_of((width, packed), BF16),
                ),
                *samp_sum(mine, other, dtype),
                matrix,
                scratch=whole_scratch,
            )
            dtype = BF16
            samples, columns, mine, other = call_with_place(
                backward_kernel,
                (samples_shape, columns_shape, part_shape, part_shape),
                product,
                gram,
                *snp_others(wire),
                raw,
                matrix,
            )
        basis, projection = call_with_place(
            last_kernel,
            (samples_shape, columns_shape),
            *samp_sum(mine, other, dtype),
            samples,
            scratch=whole_scratch,
        )
        return (basis.T, projection.T, columns.T)

    in_specs = (
        P(samp_axes, "snp"),
        P("snp"),
        P(samp_axes, None),
        P(),
        P(("snp", *samp_axes), None),
        P("snp", None),
        P(),
        P(),
        P(),
    )
    out_specs = (P(samp_axes, None), P("snp", None), P("snp", None))
    return jax.shard_map(
        on_device, mesh=fine, in_specs=in_specs, out_specs=out_specs, check_vma=False
    )
```

```python
import math

import jax
import jax.numpy as jnp
from jax import lax
from jax.experimental import pallas as pl
from jax.experimental.pallas import tpu as pltpu
from jax.sharding import Mesh, PartitionSpec as P

BATCHES = 12
BLOCK = 256
ITERS = 2
BLOCKS = 16
LANES = 128
SUB = 8
GROUP = 32
SHIFTS = (2, 1, 3)
F32 = jnp.float32
BF16 = jnp.bfloat16
HIGH = lax.Precision.HIGHEST


def exact_dot(a, b, a_dim, b_dim):
    return lax.dot_general(
        a, b, (((a_dim,), (b_dim,)), ((), ())), precision=HIGH, preferred_element_type=F32
    )


def split_dot(values, matrix, dim):
    high = values.astype(BF16)
    low = (values - high.astype(F32)).astype(BF16)
    both = jnp.concatenate([high, low], axis=0)
    out = lax.dot_general(
        both, matrix, (((1,), (dim,)), ((), ())), preferred_element_type=F32
    )
    rows = values.shape[0]
    return out[:rows] + out[rows:]


def inverse_factor(gram, lower):
    size = gram.shape[0]
    across = lax.broadcasted_iota(jnp.int32, (size, size), 1)
    down = lax.broadcasted_iota(jnp.int32, (size, size), 0)
    wide = jnp.concatenate([gram, (across == down).astype(F32)], axis=1)
    count = size // SUB
    shape = (SUB, 2 * size)
    tiles = [wide[SUB * t : SUB * (t + 1)] for t in range(count)]
    sub = lax.broadcasted_iota(jnp.int32, shape, 0)
    step = 1 if lower else -1

    def spread_row(value, k):
        return jnp.broadcast_to(value[k : k + 1], shape)

    for a in range(count)[::step]:
        active = range(a, count) if lower else range(a + 1)
        cols = {
            t: [
                jnp.broadcast_to(tiles[t][:, SUB * a + k : SUB * a + k + 1], shape)
                for k in range(SUB)
            ]
            for t in active
        }
        scale = jnp.zeros(shape, F32)
        order = range(SUB)[::step]
        for p, q in zip(order[::2], order[1::2]):
            aa, bb = spread_row(cols[a][p], p), spread_row(cols[a][p], q)
            cc = spread_row(cols[a][q], q)
            det = aa * cc - bb * bb
            inverse, first = 1.0 / det, 1.0 / aa
            ia, ib, ic = cc * inverse, bb * inverse, aa * inverse
            scale = jnp.where(sub == p, aa, jnp.where(sub == q, det * first, scale))
            keep = (sub > q) if lower else (sub < q)
            rest = [j for j in order if (j > q if lower else j < q)]

            def solved(value):
                vp, vq = spread_row(value, p), spread_row(value, q)
                return ia * vp - ib * vq, ic * vq - ib * vp

            row_p = spread_row(tiles[a], p)
            up, uq = solved(tiles[a])
            heads = {j: solved(cols[a][j]) for j in rest}
            for t in active:
                cp, cq = cols[t][p], cols[t][q]
                for j in rest:
                    cols[t][j] = cols[t][j] - (cp * heads[j][0] + cq * heads[j][1])
                if t == a:
                    inner = jnp.where(sub == q, bb * first, 0.0) * row_p
                    cp, cq = jnp.where(keep, cp, 0.0), jnp.where(keep, cq, 0.0)
                    tiles[t] = tiles[t] - (cp * up + cq * uq) - inner
                else:
                    tiles[t] = tiles[t] - (cp * up + cq * uq)
        tiles[a] = tiles[a] * lax.rsqrt(scale)
    return jnp.concatenate(tiles, axis=0)[:, size:]


def shape_of(shape, dtype=F32):
    return jax.ShapeDtypeStruct(shape, dtype)


def write_send(columns, gram, core, mine, other):
    rows = columns.shape[0]
    blank = jnp.zeros((rows, LANES - gram.shape[1]), F32)
    value = jnp.concatenate([columns, gram, blank], axis=1)
    top, bottom = value[: rows // 2], value[rows // 2 :]
    mine[...] = jnp.where(core == 0, top, bottom)
    other[...] = jnp.where(core == 0, bottom, top)


def three_parts(value):
    high = value.astype(BF16)
    rest = value - high.astype(F32)
    middle = rest.astype(BF16)
    return [high, middle, (rest - middle.astype(F32)).astype(BF16)]


def solution(mesh):
    samp, snp = mesh.shape["samp"], mesh.shape["snp"]
    chips, ring = samp // 2, 4
    depth = chips // ring
    fine = Mesh(mesh.devices.reshape(depth, ring, 2, snp), ("z", "x", "core", "snp"))
    samp_axes = ("z", "x", "core")

    def swap(value):
        return lax.ppermute(value, "core", [(0, 1), (1, 0)])

    def snp_others(value):
        return [
            lax.ppermute(value, "snp", [(i, (i + k) % snp) for i in range(snp)])
            for k in SHIFTS
        ]

    def x_shift(value, k):
        return lax.ppermute(value, "x", [(i, (i + k) % ring) for i in range(ring)])

    def on_device(
        genotype,
        freqs,
        left_factors,
        singular,
        right_factors,
        sketch,
        batch_sizes,
        missing_batch,
        missing_block,
    ):
        row_count, col_width = genotype.shape
        rank = left_factors.shape[1]
        width = sketch.shape[1]
        sample_count = row_count * samp
        snp_count = col_width * snp
        place = lax.axis_index((*samp_axes, "snp")).reshape(1).astype(jnp.int32)
        local_blocks = col_width // BLOCK
        omega = sketch.T

        def core_of(place):
            return place[0] // snp % 2

        def x_of(place):
            return place[0] // (snp * 2) % ring

        def call_with_place(body, outs, *operands, scalars=(), scratch=()):
            smem = pl.BlockSpec(memory_space=pltpu.SMEM)
            specs = [smem] * (1 + len(scalars)) + [
                pl.BlockSpec(memory_space=pltpu.VMEM) for _ in operands
            ]
            return pl.pallas_call(
                body,
                out_shape=outs,
                in_specs=specs,
                scratch_shapes=scratch,
                compiler_params=pltpu.CompilerParams(vmem_limit_bytes=48 * 1024 * 1024),
            )(place, *scalars, *operands)

        def batch_ids(place, sizes, shape, axis):
            ids = lax.broadcasted_iota(jnp.int32, shape, axis) + place[0] // snp * row_count
            batch = jnp.zeros(shape, jnp.int32)
            end = jnp.int32(0)
            for b in range(BATCHES - 1):
                end = end + sizes[b]
                batch = batch + (ids >= end).astype(jnp.int32)
            return batch

        def gone_in(bits, batch):
            return ((jnp.broadcast_to(bits, batch.shape) >> batch) & 1) == 1

        chunk = LANES

        def observe_kernel(
            place, sizes_in, batch_in, block_in, geno_in, freq_in, om_in,
            obs, start, bits,
            sizes, tile_batch, tile_block, geno, freq, om, sems,
        ):
            copies = [
                pltpu.make_async_copy(source, target, sems.at[i])
                for i, (source, target) in enumerate(
                    [
                        (batch_in, tile_batch),
                        (block_in, tile_block),
                        (sizes_in, sizes),
                        (freq_in, freq),
                    ]
                    + [
                        (geno_in.at[pl.ds(low, chunk)], geno.at[pl.ds(low, chunk)])
                        for low in range(0, row_count, chunk)
                    ]
                    + [(om_in, om)]
                )
            ]
            for copy in copies:
                copy.start()
            for block in range(BLOCKS):
                bits[block] = 0
            copies[0].wait()
            copies[1].wait()
            for i in range(tile_batch.shape[0]):
                block = tile_block[i]
                bits[block] = bits[block] | (1 << tile_batch[i])
            copies[2].wait()
            copies[3].wait()
            batch = batch_ids(place, sizes, (row_count, LANES), 0)
            own_bits = [bits[place[0] % snp * local_blocks + j] for j in range(local_blocks)]
            for n, top in enumerate(range(0, row_count, chunk)):
                copies[4 + n].wait()
                rows = slice(top, top + chunk)
                for j in range(local_blocks):
                    gone = gone_in(own_bits[j], batch[rows])
                    for low in range(BLOCK * j, BLOCK * (j + 1), LANES):
                        at = slice(low, low + LANES)
                        values = geno[rows, at].astype(F32) - 2.0 * freq[:, at]
                        obs[rows, at] = jnp.where(gone, 0.0, values).astype(BF16)
            copies[-1].wait()
            start[...] = lax.dot_general(
                om[...], obs[...], (((1,), (1,)), ((), ())), preferred_element_type=F32
            )

        vmem = pl.BlockSpec(memory_space=pltpu.VMEM)
        smem = pl.BlockSpec(memory_space=pltpu.SMEM)
        tiles = missing_batch.shape
        observed, start, bits = pl.pallas_call(
            observe_kernel,
            out_shape=(
                shape_of((row_count, col_width), BF16),
                shape_of((width, row_count)),
                shape_of((BLOCKS,), jnp.int32),
            ),
            in_specs=[smem] + [pl.BlockSpec(memory_space=pltpu.HBM)] * 6,
            out_specs=(vmem, vmem, smem),
            scratch_shapes=[
                pltpu.SMEM(batch_sizes.shape, jnp.int32),
                pltpu.SMEM(tiles, jnp.int32),
                pltpu.SMEM(tiles, jnp.int32),
                pltpu.VMEM((row_count, col_width), jnp.int32),
                pltpu.VMEM((1, col_width), F32),
                pltpu.VMEM((width, col_width), BF16),
                pltpu.SemaphoreType.DMA((5 + row_count // chunk,)),
            ],
            compiler_params=pltpu.CompilerParams(vmem_limit_bytes=63 * 1024 * 1024),
        )(
            place,
            batch_sizes,
            missing_batch,
            missing_block,
            genotype,
            freqs.reshape(1, col_width),
            omega,
        )

        def pack_kernel(place, mine, other, spread):
            first = core_of(place) == 0
            low = jnp.where(first, mine[...], other[...])
            high = jnp.where(first, other[...], mine[...])
            fill = jnp.zeros((SUB, GROUP - rank), F32)
            pieces = []
            for part in (low, high):
                for top in range(0, part.shape[0], SUB):
                    pieces += [part[top : top + SUB], fill]
            tile = jnp.concatenate(pieces, axis=1)
            spread[...] = jnp.broadcast_to(tile[None], spread.shape)

        right_tiles = lax.all_to_all(
            call_with_place(
                pack_kernel,
                shape_of((chips, SUB, LANES)),
                right_factors,
                swap(right_factors),
            ),
            ("z", "x"),
            0,
            0,
        )
        start_others = snp_others(start)

        def right_rows(tiles):
            value = tiles[...]
            parts = [value[:, :, g : g + GROUP] for g in range(0, LANES, GROUP)]
            return jnp.stack(parts, axis=1).reshape(col_width, GROUP)

        def weight_rows(scale, left):
            rows = [left[r : r + 1, :] * scale[r] for r in range(rank)]
            return jnp.concatenate(
                [*rows, jnp.zeros((GROUP - rank, row_count), F32)], axis=0
            )

        def mix_kernel(place, tiles, om, mixed):
            right = right_rows(tiles)
            pieces = [
                exact_dot(
                    om[:, BLOCK * j : BLOCK * (j + 1)].astype(F32),
                    right[BLOCK * j : BLOCK * (j + 1)],
                    1,
                    0,
                )
                for j in range(local_blocks)
            ]
            mixed[...] = jnp.concatenate(pieces, axis=1)

        def build_kernel(place, sizes, bits, scale, obs, left, tiles, x_out):
            right = right_rows(tiles)
            weight = weight_rows(scale, left).T
            batch = batch_ids(place, sizes, (row_count, BLOCK), 0)
            for j in range(local_blocks):
                at = slice(BLOCK * j, BLOCK * (j + 1))
                lowrank = exact_dot(weight, right[at], 1, 1)
                gone = gone_in(bits[place[0] % snp * local_blocks + j], batch)
                x_out[:, at] = jnp.where(gone, lowrank, obs[:, at].astype(F32)).astype(BF16)

        mixed = call_with_place(
            mix_kernel,
            shape_of((width, local_blocks * GROUP)),
            right_tiles,
            omega,
        )
        mixed_others = snp_others(mixed)
        left_rows = left_factors.T
        matrix = call_with_place(
            build_kernel,
            shape_of((row_count, col_width), BF16),
            observed,
            left_rows,
            right_tiles,
            scalars=(batch_sizes, bits, singular),
        )

        packed = row_count + 3 * width
        sum_width = col_width + LANES
        part_shape = shape_of((width // 2, sum_width))
        tile_shape = shape_of((SUB, sum_width))

        def split_kernel(place, mine, got, own, *sends):
            for k, ref in enumerate((own, *sends)):
                rows = pl.ds(pl.multiple_of((x_of(place) + k) % ring * SUB, SUB), SUB)
                ref[...] = mine[rows, :] + got[rows, :]

        def spread_kernel(place, own, a, b, c, out):
            total = own[...] + a[...] + b[...] + c[...]
            if out.dtype == BF16:
                columns, gram = total[:, :col_width], total[:, col_width : col_width + width]
                total = jnp.concatenate(
                    [
                        columns.astype(BF16),
                        *three_parts(gram),
                        jnp.zeros((SUB, out.shape[2] - col_width - 3 * width), BF16),
                    ],
                    axis=1,
                )
            out[...] = jnp.broadcast_to(total[None], out.shape)

        def gather_kernel(place, parts, out):
            total = jnp.sum(parts[...].astype(F32), axis=0)
            if parts.dtype == BF16:
                grams = [
                    total[:, col_width + width * i : col_width + width * (i + 1)]
                    for i in range(3)
                ]
                total = jnp.concatenate(
                    [
                        total[:, :col_width],
                        grams[0] + (grams[1] + grams[2]),
                        jnp.zeros((SUB, LANES - width), F32),
                    ],
                    axis=1,
                )
            out[...] = jnp.broadcast_to(total[None], out.shape)

        def samp_sum(mine, other, dtype):
            own, *sends = call_with_place(
                split_kernel, (tile_shape,) * ring, mine, swap(other)
            )
            gots = [x_shift(sends[k - 1], k) for k in ((1, 3, 2) if dtype == F32 else SHIFTS)]
            wide = sum_width if dtype == F32 else col_width + 2 * LANES
            spread = call_with_place(
                spread_kernel, shape_of((depth, SUB, wide), dtype), own, *gots
            )
            tiles = call_with_place(
                gather_kernel,
                shape_of((ring, *tile_shape.shape)),
                lax.all_to_all(spread, "z", 0, 0),
            )
            near = lax.all_to_all(tiles, "x", 0, 0)
            return [near, swap(near)]

        def read_sum(place, tiles, whole):
            half = width // 2
            for side, ref in zip((core_of(place), 1 - core_of(place)), tiles):
                whole[pl.ds(pl.multiple_of(side * half, half), half), :] = ref[...].reshape(
                    half, sum_width
                )
            return whole[:, :col_width], whole[:, col_width : col_width + width]

        whole_scratch = [pltpu.VMEM((width, sum_width), F32)]

        def first_kernel(
            place, sizes, bits, scale, own, a, b, c, q0, q1, q2, q3, left, x,
            samples_out, mine, other,
        ):
            samples = own[...] + a[...] + b[...] + c[...]
            batch = batch_ids(place, sizes, (1, row_count), 1)
            weight = weight_rows(scale, left)
            for k, q in zip((0, *SHIFTS), (q0, q1, q2, q3)):
                source = (place[0] + (snp - k)) % snp
                masked = [
                    jnp.where(gone_in(bits[source * local_blocks + j], batch), weight, 0.0)
                    for j in range(local_blocks)
                ]
                samples = samples + exact_dot(q[...], jnp.concatenate(masked, axis=0), 1, 0)
            samples_out[...] = samples
            write_send(
                split_dot(samples, x[...], 0),
                exact_dot(samples, samples, 1, 1),
                core_of(place),
                mine,
                other,
            )

        def forward_kernel(place, *refs):
            tiles, (x, raw_out, product_out, gram_out, wire, whole) = refs[:2], refs[2:]
            columns, gram = read_sum(place, tiles, whole)
            raw = exact_dot(inverse_factor(gram / sample_count, True), columns, 1, 0)
            raw_out[...] = raw
            product = split_dot(raw, x[...], 1)
            own = exact_dot(raw, raw, 1, 1)
            product_out[...] = product
            gram_out[...] = own
            wire[...] = jnp.concatenate([product.astype(BF16), *three_parts(own)], axis=1)

        def backward_kernel(
            place, product, gram, a, b, c, raw, x, samples_out, columns_out, mine, other
        ):
            total, own = product[...], gram[...]
            for ref in (a, b, c):
                total = total + ref[:, :row_count].astype(F32)
                parts = [
                    ref[:, row_count + width * i : row_count + width * (i + 1)].astype(F32)
                    for i in range(3)
                ]
                own = own + (parts[0] + (parts[1] + parts[2]))
            factor = inverse_factor(own / snp_count, False)
            samples = exact_dot(factor, total, 1, 0)
            samples_out[...] = samples
            columns_out[...] = exact_dot(factor, raw[...], 1, 0)
            write_send(
                split_dot(samples, x[...], 0),
                exact_dot(samples, samples, 1, 1),
                core_of(place),
                mine,
                other,
            )

        def last_kernel(place, *refs):
            tiles, (samples, basis, projection, whole) = refs[:2], refs[2:]
            columns, gram = read_sum(place, tiles, whole)
            factor = inverse_factor(gram / sample_count, True)
            basis[...] = exact_dot(factor, samples[...], 1, 0)
            projection[...] = exact_dot(factor / math.sqrt(sample_count), columns, 1, 0)

        samples_shape = shape_of((width, row_count))
        columns_shape = shape_of((width, col_width))
        samples, mine, other = call_with_place(
            first_kernel,
            (samples_shape, part_shape, part_shape),
            start,
            *start_others,
            mixed,
            *mixed_others,
            left_rows,
            matrix,
            scalars=(batch_sizes, bits, singular),
        )
        columns, dtype = None, F32
        for _ in range(ITERS):
            raw, product, gram, wire = call_with_place(
                forward_kernel,
                (
                    columns_shape,
                    samples_shape,
                    shape_of((width, width)),
                    shape_of((width, packed), BF16),
                ),
                *samp_sum(mine, other, dtype),
                matrix,
                scratch=whole_scratch,
            )
            dtype = BF16
            samples, columns, mine, other = call_with_place(
                backward_kernel,
                (samples_shape, columns_shape, part_shape, part_shape),
                product,
                gram,
                *snp_others(wire),
                raw,
                matrix,
            )
        basis, projection = call_with_place(
            last_kernel,
            (samples_shape, columns_shape),
            *samp_sum(mine, other, dtype),
            samples,
            scratch=whole_scratch,
        )
        return (basis.T, projection.T, columns.T)

    in_specs = (
        P(samp_axes, "snp"),
        P("snp"),
        P(samp_axes, None),
        P(),
        P(("snp", *samp_axes), None),
        P("snp", None),
        P(),
        P(),
        P(),
    )
    out_specs = (P(samp_axes, None), P("snp", None), P("snp", None))
    return jax.shard_map(
        on_device, mesh=fine, in_specs=in_specs, out_specs=out_specs, check_vma=False
    )
```

```python
import math

import jax
import jax.numpy as jnp
from jax import lax
from jax.experimental import pallas as pl
from jax.experimental.pallas import tpu as pltpu
from jax.sharding import Mesh, PartitionSpec as P

BATCHES = 12
BLOCK = 256
ITERS = 2
BLOCKS = 16
LANES = 128
SUB = 8
GROUP = 32
SHIFTS = (2, 1, 3)
F32 = jnp.float32
BF16 = jnp.bfloat16
HIGH = lax.Precision.HIGHEST


def exact_dot(a, b, a_dim, b_dim):
    return lax.dot_general(
        a, b, (((a_dim,), (b_dim,)), ((), ())), precision=HIGH, preferred_element_type=F32
    )


def split_dot(values, matrix, dim):
    high = values.astype(BF16)
    low = (values - high.astype(F32)).astype(BF16)
    both = jnp.concatenate([high, low], axis=0)
    out = lax.dot_general(
        both, matrix, (((1,), (dim,)), ((), ())), preferred_element_type=F32
    )
    rows = values.shape[0]
    return out[:rows] + out[rows:]


def inverse_factor(gram, lower):
    size = gram.shape[0]
    across = lax.broadcasted_iota(jnp.int32, (size, size), 1)
    down = lax.broadcasted_iota(jnp.int32, (size, size), 0)
    wide = jnp.concatenate([gram, (across == down).astype(F32)], axis=1)
    count = size // SUB
    shape = (SUB, 2 * size)
    tiles = [wide[SUB * t : SUB * (t + 1)] for t in range(count)]
    sub = lax.broadcasted_iota(jnp.int32, shape, 0)
    step = 1 if lower else -1

    def spread_row(value, k):
        return jnp.broadcast_to(value[k : k + 1], shape)

    for a in range(count)[::step]:
        active = range(a, count) if lower else range(a + 1)
        cols = {
            t: [
                jnp.broadcast_to(tiles[t][:, SUB * a + k : SUB * a + k + 1], shape)
                for k in range(SUB)
            ]
            for t in active
        }
        scale = jnp.zeros(shape, F32)
        order = range(SUB)[::step]
        for p, q in zip(order[::2], order[1::2]):
            aa, bb = spread_row(cols[a][p], p), spread_row(cols[a][p], q)
            cc = spread_row(cols[a][q], q)
            det = aa * cc - bb * bb
            inverse, first = 1.0 / det, 1.0 / aa
            ia, ib, ic = cc * inverse, bb * inverse, aa * inverse
            scale = jnp.where(sub == p, aa, jnp.where(sub == q, det * first, scale))
            keep = (sub > q) if lower else (sub < q)
            rest = [j for j in order if (j > q if lower else j < q)]

            def solved(value):
                vp, vq = spread_row(value, p), spread_row(value, q)
                return ia * vp - ib * vq, ic * vq - ib * vp

            row_p = spread_row(tiles[a], p)
            up, uq = solved(tiles[a])
            heads = {j: solved(cols[a][j]) for j in rest}
            for t in active:
                cp, cq = cols[t][p], cols[t][q]
                for j in rest:
                    cols[t][j] = cols[t][j] - (cp * heads[j][0] + cq * heads[j][1])
                if t == a:
                    inner = jnp.where(sub == q, bb * first, 0.0) * row_p
                    cp, cq = jnp.where(keep, cp, 0.0), jnp.where(keep, cq, 0.0)
                    tiles[t] = tiles[t] - (cp * up + cq * uq) - inner
                else:
                    tiles[t] = tiles[t] - (cp * up + cq * uq)
        tiles[a] = tiles[a] * lax.rsqrt(scale)
    return jnp.concatenate(tiles, axis=0)[:, size:]


def shape_of(shape, dtype=F32):
    return jax.ShapeDtypeStruct(shape, dtype)


def write_send(columns, gram, core, mine, other):
    rows = columns.shape[0]
    blank = jnp.zeros((rows, LANES - gram.shape[1]), F32)
    value = jnp.concatenate([columns, gram, blank], axis=1)
    top, bottom = value[: rows // 2], value[rows // 2 :]
    mine[...] = jnp.where(core == 0, top, bottom)
    other[...] = jnp.where(core == 0, bottom, top)


def three_parts(value):
    high = value.astype(BF16)
    rest = value - high.astype(F32)
    middle = rest.astype(BF16)
    return [high, middle, (rest - middle.astype(F32)).astype(BF16)]


def solution(mesh):
    samp, snp = mesh.shape["samp"], mesh.shape["snp"]
    chips, ring = samp // 2, 4
    depth = chips // ring
    fine = Mesh(mesh.devices.reshape(depth, ring, 2, snp), ("z", "x", "core", "snp"))
    samp_axes = ("z", "x", "core")

    def swap(value):
        return lax.ppermute(value, "core", [(0, 1), (1, 0)])

    def snp_others(value):
        return [
            lax.ppermute(value, "snp", [(i, (i + k) % snp) for i in range(snp)])
            for k in SHIFTS
        ]

    def x_shift(value, k):
        return lax.ppermute(value, "x", [(i, (i + k) % ring) for i in range(ring)])

    def on_device(
        genotype,
        freqs,
        left_factors,
        singular,
        right_factors,
        sketch,
        batch_sizes,
        missing_batch,
        missing_block,
    ):
        row_count, col_width = genotype.shape
        rank = left_factors.shape[1]
        width = sketch.shape[1]
        sample_count = row_count * samp
        snp_count = col_width * snp
        place = lax.axis_index((*samp_axes, "snp")).reshape(1).astype(jnp.int32)
        local_blocks = col_width // BLOCK
        omega = sketch.T

        def core_of(place):
            return place[0] // snp % 2

        def x_of(place):
            return place[0] // (snp * 2) % ring

        def call_with_place(body, outs, *operands, scalars=(), scratch=()):
            smem = pl.BlockSpec(memory_space=pltpu.SMEM)
            specs = [smem] * (1 + len(scalars)) + [
                pl.BlockSpec(memory_space=pltpu.VMEM) for _ in operands
            ]
            return pl.pallas_call(
                body,
                out_shape=outs,
                in_specs=specs,
                scratch_shapes=scratch,
                compiler_params=pltpu.CompilerParams(vmem_limit_bytes=48 * 1024 * 1024),
            )(place, *scalars, *operands)

        def batch_ids(place, sizes, shape, axis):
            ids = lax.broadcasted_iota(jnp.int32, shape, axis) + place[0] // snp * row_count
            batch = jnp.zeros(shape, jnp.int32)
            end = jnp.int32(0)
            for b in range(BATCHES - 1):
                end = end + sizes[b]
                batch = batch + (ids >= end).astype(jnp.int32)
            return batch

        def gone_in(bits, batch):
            return ((jnp.broadcast_to(bits, batch.shape) >> batch) & 1) == 1

        chunk = LANES

        def observe_kernel(
            place, sizes_in, batch_in, block_in, geno_in, freq_in, om_in,
            obs, start, bits,
            sizes, tile_batch, tile_block, geno, freq, om, sems,
        ):
            copies = [
                pltpu.make_async_copy(source, target, sems.at[i])
                for i, (source, target) in enumerate(
                    [
                        (batch_in, tile_batch),
                        (block_in, tile_block),
                        (sizes_in, sizes),
                        (freq_in, freq),
                    ]
                    + [
                        (geno_in.at[pl.ds(low, chunk)], geno.at[pl.ds(low, chunk)])
                        for low in range(0, row_count, chunk)
                    ]
                    + [(om_in, om)]
                )
            ]
            for copy in copies:
                copy.start()
            for block in range(BLOCKS):
                bits[block] = 0
            copies[0].wait()
            copies[1].wait()
            for i in range(tile_batch.shape[0]):
                block = tile_block[i]
                bits[block] = bits[block] | (1 << tile_batch[i])
            copies[2].wait()
            copies[3].wait()
            batch = batch_ids(place, sizes, (row_count, LANES), 0)
            own_bits = [bits[place[0] % snp * local_blocks + j] for j in range(local_blocks)]
            for n, top in enumerate(range(0, row_count, chunk)):
                copies[4 + n].wait()
                rows = slice(top, top + chunk)
                for j in range(local_blocks):
                    gone = gone_in(own_bits[j], batch[rows])
                    for low in range(BLOCK * j, BLOCK * (j + 1), LANES):
                        at = slice(low, low + LANES)
                        values = geno[rows, at].astype(F32) - 2.0 * freq[:, at]
                        obs[rows, at] = jnp.where(gone, 0.0, values).astype(BF16)
            copies[-1].wait()
            start[...] = lax.dot_general(
                om[...], obs[...], (((1,), (1,)), ((), ())), preferred_element_type=F32
            )

        vmem = pl.BlockSpec(memory_space=pltpu.VMEM)
        smem = pl.BlockSpec(memory_space=pltpu.SMEM)
        tiles = missing_batch.shape
        observed, start, bits = pl.pallas_call(
            observe_kernel,
            out_shape=(
                shape_of((row_count, col_width), BF16),
                shape_of((width, row_count)),
                shape_of((BLOCKS,), jnp.int32),
            ),
            in_specs=[smem] + [pl.BlockSpec(memory_space=pltpu.HBM)] * 6,
            out_specs=(vmem, vmem, smem),
            scratch_shapes=[
                pltpu.SMEM(batch_sizes.shape, jnp.int32),
                pltpu.SMEM(tiles, jnp.int32),
                pltpu.SMEM(tiles, jnp.int32),
                pltpu.VMEM((row_count, col_width), jnp.int32),
                pltpu.VMEM((1, col_width), F32),
                pltpu.VMEM((width, col_width), BF16),
                pltpu.SemaphoreType.DMA((5 + row_count // chunk,)),
            ],
            compiler_params=pltpu.CompilerParams(vmem_limit_bytes=63 * 1024 * 1024),
        )(
            place,
            batch_sizes,
            missing_batch,
            missing_block,
            genotype,
            freqs.reshape(1, col_width),
            omega,
        )

        def pack_kernel(place, mine, other, spread):
            first = core_of(place) == 0
            low = jnp.where(first, mine[...], other[...])
            high = jnp.where(first, other[...], mine[...])
            fill = jnp.zeros((SUB, GROUP - rank), F32)
            pieces = []
            for part in (low, high):
                for top in range(0, part.shape[0], SUB):
                    pieces += [part[top : top + SUB], fill]
            tile = jnp.concatenate(pieces, axis=1)
            spread[...] = jnp.broadcast_to(tile[None], spread.shape)

        right_tiles = lax.all_to_all(
            call_with_place(
                pack_kernel,
                shape_of((chips, SUB, LANES)),
                right_factors,
                swap(right_factors),
            ),
            ("z", "x"),
            0,
            0,
        )
        start_others = snp_others(start)

        def right_rows(tiles):
            value = tiles[...]
            parts = [value[:, :, g : g + GROUP] for g in range(0, LANES, GROUP)]
            return jnp.stack(parts, axis=1).reshape(col_width, GROUP)

        def weight_rows(scale, left):
            rows = [left[r : r + 1, :] * scale[r] for r in range(rank)]
            return jnp.concatenate(
                [*rows, jnp.zeros((GROUP - rank, row_count), F32)], axis=0
            )

        def mix_kernel(place, tiles, om, mixed):
            right = right_rows(tiles)
            pieces = [
                exact_dot(
                    om[:, BLOCK * j : BLOCK * (j + 1)].astype(F32),
                    right[BLOCK * j : BLOCK * (j + 1)],
                    1,
                    0,
                )
                for j in range(local_blocks)
            ]
            mixed[...] = jnp.concatenate(pieces, axis=1)

        def build_kernel(place, sizes, bits, scale, obs, left, tiles, x_out):
            right = right_rows(tiles)
            weight = weight_rows(scale, left).T
            batch = batch_ids(place, sizes, (row_count, BLOCK), 0)
            for j in range(local_blocks):
                at = slice(BLOCK * j, BLOCK * (j + 1))
                lowrank = exact_dot(weight, right[at], 1, 1)
                gone = gone_in(bits[place[0] % snp * local_blocks + j], batch)
                x_out[:, at] = jnp.where(gone, lowrank, obs[:, at].astype(F32)).astype(BF16)

        mixed = call_with_place(
            mix_kernel,
            shape_of((width, local_blocks * GROUP)),
            right_tiles,
            omega,
        )
        mixed_others = snp_others(mixed)
        left_rows = left_factors.T
        matrix = call_with_place(
            build_kernel,
            shape_of((row_count, col_width), BF16),
            observed,
            left_rows,
            right_tiles,
            scalars=(batch_sizes, bits, singular),
        )

        packed = row_count + 3 * width
        sum_width = col_width + LANES
        part_shape = shape_of((width // 2, sum_width))
        tile_shape = shape_of((SUB, sum_width))

        def split_kernel(place, mine, got, own, *sends):
            for k, ref in enumerate((own, *sends)):
                rows = pl.ds(pl.multiple_of((x_of(place) + k) % ring * SUB, SUB), SUB)
                ref[...] = mine[rows, :] + got[rows, :]

        def spread_kernel(place, own, a, b, c, out):
            total = own[...] + a[...] + b[...] + c[...]
            if out.dtype == BF16:
                columns, gram = total[:, :col_width], total[:, col_width : col_width + width]
                total = jnp.concatenate(
                    [
                        columns.astype(BF16),
                        *three_parts(gram),
                        jnp.zeros((SUB, out.shape[2] - col_width - 3 * width), BF16),
                    ],
                    axis=1,
                )
            out[...] = jnp.broadcast_to(total[None], out.shape)

        def gather_kernel(place, parts, out):
            total = jnp.sum(parts[...].astype(F32), axis=0)
            if parts.dtype == BF16:
                grams = [
                    total[:, col_width + width * i : col_width + width * (i + 1)]
                    for i in range(3)
                ]
                total = jnp.concatenate(
                    [
                        total[:, :col_width],
                        grams[0] + (grams[1] + grams[2]),
                        jnp.zeros((SUB, LANES - width), F32),
                    ],
                    axis=1,
                )
            out[...] = total

        def samp_sum(mine, other, dtype):
            own, *sends = call_with_place(
                split_kernel, (tile_shape,) * ring, mine, swap(other)
            )
            gots = [x_shift(sends[k - 1], k) for k in ((1, 3, 2) if dtype == F32 else SHIFTS)]
            wide = sum_width if dtype == F32 else col_width + 2 * LANES
            spread = call_with_place(
                spread_kernel, shape_of((depth, SUB, wide), dtype), own, *gots
            )
            tile = call_with_place(
                gather_kernel, tile_shape, lax.all_to_all(spread, "z", 0, 0)
            )
            near = [tile] + [x_shift(tile, k) for k in SHIFTS]
            return (*near, *[swap(value) for value in near])

        def read_sum(place, tiles, whole):
            for n, ref in enumerate(tiles):
                side = core_of(place) if n < ring else 1 - core_of(place)
                back = ring - (0, *SHIFTS)[n % ring]
                tile = side * ring + (x_of(place) + back) % ring
                whole[pl.ds(pl.multiple_of(tile * SUB, SUB), SUB), :] = ref[...]
            return whole[:, :col_width], whole[:, col_width : col_width + width]

        whole_scratch = [pltpu.VMEM((width, sum_width), F32)]

        def first_kernel(
            place, sizes, bits, scale, own, a, b, c, q0, q1, q2, q3, left, x,
            samples_out, mine, other,
        ):
            samples = own[...] + a[...] + b[...] + c[...]
            batch = batch_ids(place, sizes, (1, row_count), 1)
            weight = weight_rows(scale, left)
            for k, q in zip((0, *SHIFTS), (q0, q1, q2, q3)):
                source = (place[0] + (snp - k)) % snp
                masked = [
                    jnp.where(gone_in(bits[source * local_blocks + j], batch), weight, 0.0)
                    for j in range(local_blocks)
                ]
                samples = samples + exact_dot(q[...], jnp.concatenate(masked, axis=0), 1, 0)
            samples_out[...] = samples
            write_send(
                split_dot(samples, x[...], 0),
                exact_dot(samples, samples, 1, 1),
                core_of(place),
                mine,
                other,
            )

        def forward_kernel(place, *refs):
            tiles, (x, raw_out, product_out, gram_out, wire, whole) = refs[: 2 * ring], refs[2 * ring :]
            columns, gram = read_sum(place, tiles, whole)
            raw = exact_dot(inverse_factor(gram / sample_count, True), columns, 1, 0)
            raw_out[...] = raw
            product = split_dot(raw, x[...], 1)
            own = exact_dot(raw, raw, 1, 1)
            product_out[...] = product
            gram_out[...] = own
            wire[...] = jnp.concatenate([product.astype(BF16), *three_parts(own)], axis=1)

        def backward_kernel(
            place, product, gram, a, b, c, raw, x, samples_out, columns_out, mine, other
        ):
            total, own = product[...], gram[...]
            for ref in (a, b, c):
                total = total + ref[:, :row_count].astype(F32)
                parts = [
                    ref[:, row_count + width * i : row_count + width * (i + 1)].astype(F32)
                    for i in range(3)
                ]
                own = own + (parts[0] + (parts[1] + parts[2]))
            factor = inverse_factor(own / snp_count, False)
            samples = exact_dot(factor, total, 1, 0)
            samples_out[...] = samples
            columns_out[...] = exact_dot(factor, raw[...], 1, 0)
            write_send(
                split_dot(samples, x[...], 0),
                exact_dot(samples, samples, 1, 1),
                core_of(place),
                mine,
                other,
            )

        def last_kernel(place, *refs):
            tiles, (samples, basis, projection, whole) = refs[: 2 * ring], refs[2 * ring :]
            columns, gram = read_sum(place, tiles, whole)
            factor = inverse_factor(gram / sample_count, True)
            basis[...] = exact_dot(factor, samples[...], 1, 0)
            projection[...] = exact_dot(factor / math.sqrt(sample_count), columns, 1, 0)

        samples_shape = shape_of((width, row_count))
        columns_shape = shape_of((width, col_width))
        samples, mine, other = call_with_place(
            first_kernel,
            (samples_shape, part_shape, part_shape),
            start,
            *start_others,
            mixed,
            *mixed_others,
            left_rows,
            matrix,
            scalars=(batch_sizes, bits, singular),
        )
        def sweep(index, carry):
            raw, product, gram, wire = call_with_place(
                forward_kernel,
                (
                    columns_shape,
                    samples_shape,
                    shape_of((width, width)),
                    shape_of((width, packed), BF16),
                ),
                *carry[0],
                matrix,
                scratch=whole_scratch,
            )
            samples, columns, mine, other = call_with_place(
                backward_kernel,
                (samples_shape, columns_shape, part_shape, part_shape),
                product,
                gram,
                *snp_others(wire),
                raw,
                matrix,
            )
            return samp_sum(mine, other, BF16), samples, columns

        tiles, samples, columns = lax.fori_loop(
            0,
            ITERS,
            sweep,
            (samp_sum(mine, other, F32), samples, jnp.zeros(columns_shape.shape, F32)),
        )
        basis, projection = call_with_place(
            last_kernel,
            (samples_shape, columns_shape),
            *tiles,
            samples,
            scratch=whole_scratch,
        )
        return (basis.T, projection.T, columns.T)

    in_specs = (
        P(samp_axes, "snp"),
        P("snp"),
        P(samp_axes, None),
        P(),
        P(("snp", *samp_axes), None),
        P("snp", None),
        P(),
        P(),
        P(),
    )
    out_specs = (P(samp_axes, None), P("snp", None), P("snp", None))
    return jax.shard_map(
        on_device, mesh=fine, in_specs=in_specs, out_specs=out_specs, check_vma=False
    )
```

```python
import math

import jax
import jax.numpy as jnp
from jax import lax
from jax.experimental import pallas as pl
from jax.experimental.pallas import tpu as pltpu
from jax.sharding import Mesh, PartitionSpec as P

BATCHES = 12
BLOCK = 256
ITERS = 2
BLOCKS = 16
LANES = 128
SUB = 8
GROUP = 32
SHIFTS = (2, 1, 3)
F32 = jnp.float32
BF16 = jnp.bfloat16
HIGH = lax.Precision.HIGHEST


def exact_dot(a, b, a_dim, b_dim):
    return lax.dot_general(
        a, b, (((a_dim,), (b_dim,)), ((), ())), precision=HIGH, preferred_element_type=F32
    )


def split_dot(values, matrix, dim):
    high = values.astype(BF16)
    low = (values - high.astype(F32)).astype(BF16)
    both = jnp.concatenate([high, low], axis=0)
    out = lax.dot_general(
        both, matrix, (((1,), (dim,)), ((), ())), preferred_element_type=F32
    )
    rows = values.shape[0]
    return out[:rows] + out[rows:]


def inverse_factor(gram, lower):
    size = gram.shape[0]
    across = lax.broadcasted_iota(jnp.int32, (size, size), 1)
    down = lax.broadcasted_iota(jnp.int32, (size, size), 0)
    wide = jnp.concatenate([gram, (across == down).astype(F32)], axis=1)
    count = size // SUB
    shape = (SUB, 2 * size)
    tiles = [wide[SUB * t : SUB * (t + 1)] for t in range(count)]
    sub = lax.broadcasted_iota(jnp.int32, shape, 0)
    step = 1 if lower else -1

    def spread_row(value, k):
        return jnp.broadcast_to(value[k : k + 1], shape)

    for a in range(count)[::step]:
        active = range(a, count) if lower else range(a + 1)
        cols = {
            t: [
                jnp.broadcast_to(tiles[t][:, SUB * a + k : SUB * a + k + 1], shape)
                for k in range(SUB)
            ]
            for t in active
        }
        scale = jnp.zeros(shape, F32)
        order = range(SUB)[::step]
        for p, q in zip(order[::2], order[1::2]):
            aa, bb = spread_row(cols[a][p], p), spread_row(cols[a][p], q)
            cc = spread_row(cols[a][q], q)
            det = aa * cc - bb * bb
            inverse, first = 1.0 / det, 1.0 / aa
            ia, ib, ic = cc * inverse, bb * inverse, aa * inverse
            scale = jnp.where(sub == p, aa, jnp.where(sub == q, det * first, scale))
            keep = (sub > q) if lower else (sub < q)
            rest = [j for j in order if (j > q if lower else j < q)]

            def solved(value):
                vp, vq = spread_row(value, p), spread_row(value, q)
                return ia * vp - ib * vq, ic * vq - ib * vp

            row_p = spread_row(tiles[a], p)
            up, uq = solved(tiles[a])
            heads = {j: solved(cols[a][j]) for j in rest}
            for t in active:
                cp, cq = cols[t][p], cols[t][q]
                for j in rest:
                    cols[t][j] = cols[t][j] - (cp * heads[j][0] + cq * heads[j][1])
                if t == a:
                    inner = jnp.where(sub == q, bb * first, 0.0) * row_p
                    cp, cq = jnp.where(keep, cp, 0.0), jnp.where(keep, cq, 0.0)
                    tiles[t] = tiles[t] - (cp * up + cq * uq) - inner
                else:
                    tiles[t] = tiles[t] - (cp * up + cq * uq)
        tiles[a] = tiles[a] * lax.rsqrt(scale)
    return jnp.concatenate(tiles, axis=0)[:, size:]


def shape_of(shape, dtype=F32):
    return jax.ShapeDtypeStruct(shape, dtype)


def write_send(columns, gram, core, mine, other):
    rows = columns.shape[0]
    blank = jnp.zeros((rows, LANES - gram.shape[1]), F32)
    value = jnp.concatenate([columns, gram, blank], axis=1)
    top, bottom = value[: rows // 2], value[rows // 2 :]
    mine[...] = jnp.where(core == 0, top, bottom)
    other[...] = jnp.where(core == 0, bottom, top)


def three_parts(value):
    high = value.astype(BF16)
    rest = value - high.astype(F32)
    middle = rest.astype(BF16)
    return [high, middle, (rest - middle.astype(F32)).astype(BF16)]


def solution(mesh):
    samp, snp = mesh.shape["samp"], mesh.shape["snp"]
    chips, ring = samp // 2, 4
    depth = chips // ring
    fine = Mesh(mesh.devices.reshape(depth, ring, 2, snp), ("z", "x", "core", "snp"))
    samp_axes = ("z", "x", "core")

    def swap(value):
        return lax.ppermute(value, "core", [(0, 1), (1, 0)])

    def snp_others(value):
        return [
            lax.ppermute(value, "snp", [(i, (i + k) % snp) for i in range(snp)])
            for k in SHIFTS
        ]

    def x_shift(value, k):
        return lax.ppermute(value, "x", [(i, (i + k) % ring) for i in range(ring)])

    def on_device(
        genotype,
        freqs,
        left_factors,
        singular,
        right_factors,
        sketch,
        batch_sizes,
        missing_batch,
        missing_block,
    ):
        row_count, col_width = genotype.shape
        rank = left_factors.shape[1]
        width = sketch.shape[1]
        sample_count = row_count * samp
        snp_count = col_width * snp
        place = lax.axis_index((*samp_axes, "snp")).reshape(1).astype(jnp.int32)
        local_blocks = col_width // BLOCK
        omega = sketch.T

        def core_of(place):
            return place[0] // snp % 2

        def x_of(place):
            return place[0] // (snp * 2) % ring

        def call_with_place(body, outs, *operands, scalars=(), scratch=()):
            smem = pl.BlockSpec(memory_space=pltpu.SMEM)
            specs = [smem] * (1 + len(scalars)) + [
                pl.BlockSpec(memory_space=pltpu.VMEM) for _ in operands
            ]
            return pl.pallas_call(
                body,
                out_shape=outs,
                in_specs=specs,
                scratch_shapes=scratch,
                compiler_params=pltpu.CompilerParams(vmem_limit_bytes=48 * 1024 * 1024),
            )(place, *scalars, *operands)

        def batch_ids(place, sizes, shape, axis):
            ids = lax.broadcasted_iota(jnp.int32, shape, axis) + place[0] // snp * row_count
            batch = jnp.zeros(shape, jnp.int32)
            end = jnp.int32(0)
            for b in range(BATCHES - 1):
                end = end + sizes[b]
                batch = batch + (ids >= end).astype(jnp.int32)
            return batch

        def gone_in(bits, batch):
            return ((jnp.broadcast_to(bits, batch.shape) >> batch) & 1) == 1

        chunk = LANES

        def observe_kernel(
            place, sizes_in, batch_in, block_in, geno_in, freq_in, om_in,
            obs, start, bits,
            sizes, tile_batch, tile_block, geno, freq, om, sems,
        ):
            copies = [
                pltpu.make_async_copy(source, target, sems.at[i])
                for i, (source, target) in enumerate(
                    [
                        (batch_in, tile_batch),
                        (block_in, tile_block),
                        (sizes_in, sizes),
                        (freq_in, freq),
                    ]
                    + [
                        (geno_in.at[pl.ds(low, chunk)], geno.at[pl.ds(low, chunk)])
                        for low in range(0, row_count, chunk)
                    ]
                    + [(om_in, om)]
                )
            ]
            for copy in copies:
                copy.start()
            for block in range(BLOCKS):
                bits[block] = 0
            copies[0].wait()
            copies[1].wait()
            for i in range(tile_batch.shape[0]):
                block = tile_block[i]
                bits[block] = bits[block] | (1 << tile_batch[i])
            copies[2].wait()
            copies[3].wait()
            batch = batch_ids(place, sizes, (row_count, LANES), 0)
            own_bits = [bits[place[0] % snp * local_blocks + j] for j in range(local_blocks)]
            for n, top in enumerate(range(0, row_count, chunk)):
                copies[4 + n].wait()
                rows = slice(top, top + chunk)
                for j in range(local_blocks):
                    gone = gone_in(own_bits[j], batch[rows])
                    for low in range(BLOCK * j, BLOCK * (j + 1), LANES):
                        at = slice(low, low + LANES)
                        values = geno[rows, at].astype(F32) - 2.0 * freq[:, at]
                        obs[rows, at] = jnp.where(gone, 0.0, values).astype(BF16)
            copies[-1].wait()
            start[...] = lax.dot_general(
                om[...], obs[...], (((1,), (1,)), ((), ())), preferred_element_type=F32
            )

        vmem = pl.BlockSpec(memory_space=pltpu.VMEM)
        smem = pl.BlockSpec(memory_space=pltpu.SMEM)
        tiles = missing_batch.shape
        observed, start, bits = pl.pallas_call(
            observe_kernel,
            out_shape=(
                shape_of((row_count, col_width), BF16),
                shape_of((width, row_count)),
                shape_of((BLOCKS,), jnp.int32),
            ),
            in_specs=[smem] + [pl.BlockSpec(memory_space=pltpu.HBM)] * 6,
            out_specs=(vmem, vmem, smem),
            scratch_shapes=[
                pltpu.SMEM(batch_sizes.shape, jnp.int32),
                pltpu.SMEM(tiles, jnp.int32),
                pltpu.SMEM(tiles, jnp.int32),
                pltpu.VMEM((row_count, col_width), jnp.int32),
                pltpu.VMEM((1, col_width), F32),
                pltpu.VMEM((width, col_width), BF16),
                pltpu.SemaphoreType.DMA((5 + row_count // chunk,)),
            ],
            compiler_params=pltpu.CompilerParams(vmem_limit_bytes=63 * 1024 * 1024),
        )(
            place,
            batch_sizes,
            missing_batch,
            missing_block,
            genotype,
            freqs.reshape(1, col_width),
            omega,
        )

        def pack_kernel(place, mine, other, spread):
            first = core_of(place) == 0
            low = jnp.where(first, mine[...], other[...])
            high = jnp.where(first, other[...], mine[...])
            fill = jnp.zeros((SUB, GROUP - rank), F32)
            pieces = []
            for part in (low, high):
                for top in range(0, part.shape[0], SUB):
                    pieces += [part[top : top + SUB], fill]
            tile = jnp.concatenate(pieces, axis=1)
            spread[...] = jnp.broadcast_to(tile[None], spread.shape)

        right_tiles = lax.all_to_all(
            call_with_place(
                pack_kernel,
                shape_of((chips, SUB, LANES)),
                right_factors,
                swap(right_factors),
            ),
            ("z", "x"),
            0,
            0,
        )

        def right_rows(tiles):
            value = tiles[...]
            parts = [value[:, :, g : g + GROUP] for g in range(0, LANES, GROUP)]
            return jnp.stack(parts, axis=1).reshape(col_width, GROUP)

        def weight_rows(scale, left):
            rows = [left[r : r + 1, :] * scale[r] for r in range(rank)]
            return jnp.concatenate(
                [*rows, jnp.zeros((GROUP - rank, row_count), F32)], axis=0
            )

        def mix_kernel(place, tiles, om, start, mixed):
            right = right_rows(tiles)
            pieces = [
                exact_dot(
                    om[:, BLOCK * j : BLOCK * (j + 1)].astype(F32),
                    right[BLOCK * j : BLOCK * (j + 1)],
                    1,
                    0,
                )
                for j in range(local_blocks)
            ]
            mixed[:, :row_count] = start[...]
            mixed[:, row_count:] = jnp.concatenate(pieces, axis=1)

        def build_kernel(place, sizes, bits, scale, obs, left, tiles, x_out):
            right = right_rows(tiles)
            weight = weight_rows(scale, left).T
            batch = batch_ids(place, sizes, (row_count, BLOCK), 0)
            for j in range(local_blocks):
                at = slice(BLOCK * j, BLOCK * (j + 1))
                lowrank = exact_dot(weight, right[at], 1, 1)
                gone = gone_in(bits[place[0] % snp * local_blocks + j], batch)
                x_out[:, at] = jnp.where(gone, lowrank, obs[:, at].astype(F32)).astype(BF16)

        mixed = call_with_place(
            mix_kernel,
            shape_of((width, row_count + local_blocks * GROUP)),
            right_tiles,
            omega,
            start,
        )
        mixed_others = snp_others(mixed)
        left_rows = left_factors.T
        matrix = call_with_place(
            build_kernel,
            shape_of((row_count, col_width), BF16),
            observed,
            left_rows,
            right_tiles,
            scalars=(batch_sizes, bits, singular),
        )

        packed = row_count + 3 * width
        sum_width = col_width + LANES
        part_shape = shape_of((width // 2, sum_width))
        tile_shape = shape_of((SUB, sum_width))

        def split_kernel(place, mine, got, own, *sends):
            for k, ref in enumerate((own, *sends)):
                rows = pl.ds(pl.multiple_of((x_of(place) + k) % ring * SUB, SUB), SUB)
                ref[...] = mine[rows, :] + got[rows, :]

        def spread_kernel(place, own, a, b, c, out):
            total = own[...] + a[...] + b[...] + c[...]
            if out.dtype == BF16:
                columns, gram = total[:, :col_width], total[:, col_width : col_width + width]
                total = jnp.concatenate(
                    [
                        columns.astype(BF16),
                        *three_parts(gram),
                        jnp.zeros((SUB, out.shape[2] - col_width - 3 * width), BF16),
                    ],
                    axis=1,
                )
            out[...] = jnp.broadcast_to(total[None], out.shape)

        def gather_kernel(place, parts, out):
            total = jnp.sum(parts[...].astype(F32), axis=0)
            if parts.dtype == BF16:
                grams = [
                    total[:, col_width + width * i : col_width + width * (i + 1)]
                    for i in range(3)
                ]
                total = jnp.concatenate(
                    [
                        total[:, :col_width],
                        grams[0] + (grams[1] + grams[2]),
                        jnp.zeros((SUB, LANES - width), F32),
                    ],
                    axis=1,
                )
            out[...] = total

        def samp_sum(mine, other, dtype):
            own, *sends = call_with_place(
                split_kernel, (tile_shape,) * ring, mine, swap(other)
            )
            gots = [x_shift(sends[k - 1], k) for k in ((1, 3, 2) if dtype == F32 else SHIFTS)]
            wide = sum_width if dtype == F32 else col_width + 2 * LANES
            spread = call_with_place(
                spread_kernel, shape_of((depth, SUB, wide), dtype), own, *gots
            )
            tile = call_with_place(
                gather_kernel, tile_shape, lax.all_to_all(spread, "z", 0, 0)
            )
            near = [tile] + [x_shift(tile, k) for k in SHIFTS]
            return (*near, *[swap(value) for value in near])

        def read_sum(place, tiles, whole):
            for n, ref in enumerate(tiles):
                side = core_of(place) if n < ring else 1 - core_of(place)
                back = ring - (0, *SHIFTS)[n % ring]
                tile = side * ring + (x_of(place) + back) % ring
                whole[pl.ds(pl.multiple_of(tile * SUB, SUB), SUB), :] = ref[...]
            return whole[:, :col_width], whole[:, col_width : col_width + width]

        whole_scratch = [pltpu.VMEM((width, sum_width), F32)]

        def first_kernel(
            place, sizes, bits, scale, w0, w1, w2, w3, left, x, samples_out, mine, other
        ):
            batch = batch_ids(place, sizes, (1, row_count), 1)
            weight = weight_rows(scale, left)
            samples = jnp.zeros((width, row_count), F32)
            for k, ref in zip((0, *SHIFTS), (w0, w1, w2, w3)):
                source = (place[0] + (snp - k)) % snp
                masked = [
                    jnp.where(gone_in(bits[source * local_blocks + j], batch), weight, 0.0)
                    for j in range(local_blocks)
                ]
                missed = exact_dot(ref[:, row_count:], jnp.concatenate(masked, axis=0), 1, 0)
                samples = samples + (ref[:, :row_count] + missed)
            samples_out[...] = samples
            write_send(
                split_dot(samples, x[...], 0),
                exact_dot(samples, samples, 1, 1),
                core_of(place),
                mine,
                other,
            )

        def forward_kernel(place, *refs):
            tiles, (x, raw_out, product_out, gram_out, wire, whole) = refs[: 2 * ring], refs[2 * ring :]
            columns, gram = read_sum(place, tiles, whole)
            raw = exact_dot(inverse_factor(gram / sample_count, True), columns, 1, 0)
            raw_out[...] = raw
            product = split_dot(raw, x[...], 1)
            own = exact_dot(raw, raw, 1, 1)
            product_out[...] = product
            gram_out[...] = own
            wire[...] = jnp.concatenate([product.astype(BF16), *three_parts(own)], axis=1)

        def backward_kernel(
            place, product, gram, a, b, c, x, samples_out, factor_out, mine, other
        ):
            total, own = product[...], gram[...]
            for ref in (a, b, c):
                total = total + ref[:, :row_count].astype(F32)
                parts = [
                    ref[:, row_count + width * i : row_count + width * (i + 1)].astype(F32)
                    for i in range(3)
                ]
                own = own + (parts[0] + (parts[1] + parts[2]))
            factor = inverse_factor(own / snp_count, False)
            samples = exact_dot(factor, total, 1, 0)
            samples_out[...] = samples
            factor_out[...] = factor
            write_send(
                split_dot(samples, x[...], 0),
                exact_dot(samples, samples, 1, 1),
                core_of(place),
                mine,
                other,
            )

        def columns_kernel(place, factor, raw, columns):
            columns[...] = exact_dot(factor[...], raw[...], 1, 0)

        def last_kernel(place, *refs):
            tiles, (samples, basis, projection, whole) = refs[: 2 * ring], refs[2 * ring :]
            columns, gram = read_sum(place, tiles, whole)
            factor = inverse_factor(gram / sample_count, True)
            basis[...] = exact_dot(factor, samples[...], 1, 0)
            projection[...] = exact_dot(factor / math.sqrt(sample_count), columns, 1, 0)

        samples_shape = shape_of((width, row_count))
        columns_shape = shape_of((width, col_width))
        samples, mine, other = call_with_place(
            first_kernel,
            (samples_shape, part_shape, part_shape),
            mixed,
            *mixed_others,
            left_rows,
            matrix,
            scalars=(batch_sizes, bits, singular),
        )
        def sweep(index, carry):
            raw, product, gram, wire = call_with_place(
                forward_kernel,
                (
                    columns_shape,
                    samples_shape,
                    shape_of((width, width)),
                    shape_of((width, packed), BF16),
                ),
                *carry[0],
                matrix,
                scratch=whole_scratch,
            )
            samples, factor, mine, other = call_with_place(
                backward_kernel,
                (samples_shape, shape_of((width, width)), part_shape, part_shape),
                product,
                gram,
                *snp_others(wire),
                matrix,
            )
            columns = call_with_place(columns_kernel, columns_shape, factor, raw)
            return samp_sum(mine, other, BF16), samples, columns

        tiles, samples, columns = lax.fori_loop(
            0,
            ITERS,
            sweep,
            (samp_sum(mine, other, F32), samples, jnp.zeros(columns_shape.shape, F32)),
        )
        basis, projection = call_with_place(
            last_kernel,
            (samples_shape, columns_shape),
            *tiles,
            samples,
            scratch=whole_scratch,
        )
        return (basis.T, projection.T, columns.T)

    in_specs = (
        P(samp_axes, "snp"),
        P("snp"),
        P(samp_axes, None),
        P(),
        P(("snp", *samp_axes), None),
        P("snp", None),
        P(),
        P(),
        P(),
    )
    out_specs = (P(samp_axes, None), P("snp", None), P("snp", None))
    return jax.shard_map(
        on_device, mesh=fine, in_specs=in_specs, out_specs=out_specs, check_vma=False
    )
```

```python
import math

import jax
import jax.numpy as jnp
from jax import lax
from jax.experimental import pallas as pl
from jax.experimental.pallas import tpu as pltpu
from jax.sharding import Mesh, PartitionSpec as P

BATCHES = 12
BLOCK = 256
ITERS = 2
BLOCKS = 16
LANES = 128
SUB = 8
GROUP = 32
SHIFTS = (2, 1, 3)
F32 = jnp.float32
BF16 = jnp.bfloat16
HIGH = lax.Precision.HIGHEST


def exact_dot(a, b, a_dim, b_dim):
    return lax.dot_general(
        a, b, (((a_dim,), (b_dim,)), ((), ())), precision=HIGH, preferred_element_type=F32
    )


def split_dot(values, matrix, dim):
    high = values.astype(BF16)
    low = (values - high.astype(F32)).astype(BF16)
    both = jnp.concatenate([high, low], axis=0)
    out = lax.dot_general(
        both, matrix, (((1,), (dim,)), ((), ())), preferred_element_type=F32
    )
    rows = values.shape[0]
    return out[:rows] + out[rows:]


def inverse_factor(gram, lower):
    size = gram.shape[0]
    across = lax.broadcasted_iota(jnp.int32, (size, size), 1)
    down = lax.broadcasted_iota(jnp.int32, (size, size), 0)
    wide = jnp.concatenate([gram, (across == down).astype(F32)], axis=1)
    count = size // SUB
    shape = (SUB, 2 * size)
    tiles = [wide[SUB * t : SUB * (t + 1)] for t in range(count)]
    sub = lax.broadcasted_iota(jnp.int32, shape, 0)
    step = 1 if lower else -1

    def spread_row(value, k):
        return jnp.broadcast_to(value[k : k + 1], shape)

    for a in range(count)[::step]:
        active = range(a, count) if lower else range(a + 1)
        cols = {
            t: [
                jnp.broadcast_to(tiles[t][:, SUB * a + k : SUB * a + k + 1], shape)
                for k in range(SUB)
            ]
            for t in active
        }
        scale = jnp.zeros(shape, F32)
        order = range(SUB)[::step]
        for p, q in zip(order[::2], order[1::2]):
            aa, bb = spread_row(cols[a][p], p), spread_row(cols[a][p], q)
            cc = spread_row(cols[a][q], q)
            det = aa * cc - bb * bb
            inverse, first = 1.0 / det, 1.0 / aa
            ia, ib, ic = cc * inverse, bb * inverse, aa * inverse
            scale = jnp.where(sub == p, aa, jnp.where(sub == q, det * first, scale))
            keep = (sub > q) if lower else (sub < q)
            rest = [j for j in order if (j > q if lower else j < q)]

            def solved(value):
                vp, vq = spread_row(value, p), spread_row(value, q)
                return ia * vp - ib * vq, ic * vq - ib * vp

            row_p = spread_row(tiles[a], p)
            up, uq = solved(tiles[a])
            heads = {j: solved(cols[a][j]) for j in rest}
            for t in active:
                cp, cq = cols[t][p], cols[t][q]
                for j in rest:
                    cols[t][j] = cols[t][j] - (cp * heads[j][0] + cq * heads[j][1])
                if t == a:
                    inner = jnp.where(sub == q, bb * first, 0.0) * row_p
                    cp, cq = jnp.where(keep, cp, 0.0), jnp.where(keep, cq, 0.0)
                    tiles[t] = tiles[t] - (cp * up + cq * uq) - inner
                else:
                    tiles[t] = tiles[t] - (cp * up + cq * uq)
        tiles[a] = tiles[a] * lax.rsqrt(scale)
    return jnp.concatenate(tiles, axis=0)[:, size:]


def shape_of(shape, dtype=F32):
    return jax.ShapeDtypeStruct(shape, dtype)


def write_send(columns, gram, core, mine, other):
    rows = columns.shape[0]
    blank = jnp.zeros((rows, LANES - gram.shape[1]), F32)
    value = jnp.concatenate([columns, gram, blank], axis=1)
    top, bottom = value[: rows // 2], value[rows // 2 :]
    mine[...] = jnp.where(core == 0, top, bottom)
    other[...] = jnp.where(core == 0, bottom, top)


def three_parts(value):
    high = value.astype(BF16)
    rest = value - high.astype(F32)
    middle = rest.astype(BF16)
    return [high, middle, (rest - middle.astype(F32)).astype(BF16)]


def solution(mesh):
    samp, snp = mesh.shape["samp"], mesh.shape["snp"]
    chips, ring = samp // 2, 4
    depth = chips // ring
    fine = Mesh(mesh.devices.reshape(depth, ring, 2, snp), ("z", "x", "core", "snp"))
    samp_axes = ("z", "x", "core")

    def swap(value):
        return lax.ppermute(value, "core", [(0, 1), (1, 0)])

    def snp_others(value):
        return [
            lax.ppermute(value, "snp", [(i, (i + k) % snp) for i in range(snp)])
            for k in SHIFTS
        ]

    def x_shift(value, k):
        return lax.ppermute(value, "x", [(i, (i + k) % ring) for i in range(ring)])

    def on_device(
        genotype,
        freqs,
        left_factors,
        singular,
        right_factors,
        sketch,
        batch_sizes,
        missing_batch,
        missing_block,
    ):
        row_count, col_width = genotype.shape
        rank = left_factors.shape[1]
        width = sketch.shape[1]
        sample_count = row_count * samp
        snp_count = col_width * snp
        place = lax.axis_index((*samp_axes, "snp")).reshape(1).astype(jnp.int32)
        local_blocks = col_width // BLOCK
        omega = sketch.T

        def core_of(place):
            return place[0] // snp % 2

        def x_of(place):
            return place[0] // (snp * 2) % ring

        def call_with_place(body, outs, *operands, scalars=(), scratch=()):
            smem = pl.BlockSpec(memory_space=pltpu.SMEM)
            specs = [smem] * (1 + len(scalars)) + [
                pl.BlockSpec(memory_space=pltpu.VMEM) for _ in operands
            ]
            return pl.pallas_call(
                body,
                out_shape=outs,
                in_specs=specs,
                scratch_shapes=scratch,
                compiler_params=pltpu.CompilerParams(vmem_limit_bytes=48 * 1024 * 1024),
            )(place, *scalars, *operands)

        def batch_ids(place, sizes, shape, axis):
            ids = lax.broadcasted_iota(jnp.int32, shape, axis) + place[0] // snp * row_count
            batch = jnp.zeros(shape, jnp.int32)
            end = jnp.int32(0)
            for b in range(BATCHES - 1):
                end = end + sizes[b]
                batch = batch + (ids >= end).astype(jnp.int32)
            return batch

        def gone_in(bits, batch):
            return ((jnp.broadcast_to(bits, batch.shape) >> batch) & 1) == 1

        chunk = LANES

        def observe_kernel(
            place, sizes_in, batch_in, block_in, geno_in, freq_in, om_in,
            obs, start, bits,
            sizes, tile_batch, tile_block, geno, freq, om, sems,
        ):
            copies = [
                pltpu.make_async_copy(source, target, sems.at[i])
                for i, (source, target) in enumerate(
                    [
                        (batch_in, tile_batch),
                        (block_in, tile_block),
                        (sizes_in, sizes),
                        (freq_in, freq),
                    ]
                    + [
                        (geno_in.at[pl.ds(low, chunk)], geno.at[pl.ds(low, chunk)])
                        for low in range(0, row_count, chunk)
                    ]
                    + [(om_in, om)]
                )
            ]
            for copy in copies:
                copy.start()
            for block in range(BLOCKS):
                bits[block] = 0
            copies[0].wait()
            copies[1].wait()
            for i in range(tile_batch.shape[0]):
                block = tile_block[i]
                bits[block] = bits[block] | (1 << tile_batch[i])
            copies[2].wait()
            copies[3].wait()
            batch = batch_ids(place, sizes, (row_count, LANES), 0)
            own_bits = [bits[place[0] % snp * local_blocks + j] for j in range(local_blocks)]
            for n, top in enumerate(range(0, row_count, chunk)):
                copies[4 + n].wait()
                rows = slice(top, top + chunk)
                for j in range(local_blocks):
                    gone = gone_in(own_bits[j], batch[rows])
                    for low in range(BLOCK * j, BLOCK * (j + 1), LANES):
                        at = slice(low, low + LANES)
                        values = geno[rows, at].astype(F32) - 2.0 * freq[:, at]
                        obs[rows, at] = jnp.where(gone, 0.0, values).astype(BF16)
            copies[-1].wait()
            start[...] = lax.dot_general(
                om[...], obs[...], (((1,), (1,)), ((), ())), preferred_element_type=F32
            )

        vmem = pl.BlockSpec(memory_space=pltpu.VMEM)
        smem = pl.BlockSpec(memory_space=pltpu.SMEM)
        tiles = missing_batch.shape
        observed, start, bits = pl.pallas_call(
            observe_kernel,
            out_shape=(
                shape_of((row_count, col_width), BF16),
                shape_of((width, row_count)),
                shape_of((BLOCKS,), jnp.int32),
            ),
            in_specs=[smem] + [pl.BlockSpec(memory_space=pltpu.HBM)] * 6,
            out_specs=(vmem, vmem, smem),
            scratch_shapes=[
                pltpu.SMEM(batch_sizes.shape, jnp.int32),
                pltpu.SMEM(tiles, jnp.int32),
                pltpu.SMEM(tiles, jnp.int32),
                pltpu.VMEM((row_count, col_width), jnp.int32),
                pltpu.VMEM((1, col_width), F32),
                pltpu.VMEM((width, col_width), BF16),
                pltpu.SemaphoreType.DMA((5 + row_count // chunk,)),
            ],
            compiler_params=pltpu.CompilerParams(vmem_limit_bytes=48 * 1024 * 1024),
        )(
            place,
            batch_sizes,
            missing_batch,
            missing_block,
            genotype,
            freqs.reshape(1, col_width),
            omega,
        )

        def pack_kernel(place, mine, other, spread):
            first = core_of(place) == 0
            low = jnp.where(first, mine[...], other[...])
            high = jnp.where(first, other[...], mine[...])
            fill = jnp.zeros((SUB, GROUP - rank), F32)
            pieces = []
            for part in (low, high):
                for top in range(0, part.shape[0], SUB):
                    pieces += [part[top : top + SUB], fill]
            tile = jnp.concatenate(pieces, axis=1)
            spread[...] = jnp.broadcast_to(tile[None], spread.shape)

        right_tiles = lax.all_to_all(
            call_with_place(
                pack_kernel,
                shape_of((chips, SUB, LANES)),
                right_factors,
                swap(right_factors),
            ),
            ("z", "x"),
            0,
            0,
        )

        def right_rows(tiles):
            value = tiles[...]
            parts = [value[:, :, g : g + GROUP] for g in range(0, LANES, GROUP)]
            return jnp.stack(parts, axis=1).reshape(col_width, GROUP)

        def weight_rows(scale, left):
            rows = [left[r : r + 1, :] * scale[r] for r in range(rank)]
            return jnp.concatenate(
                [*rows, jnp.zeros((GROUP - rank, row_count), F32)], axis=0
            )

        def mix_kernel(place, tiles, om, start, mixed):
            right = right_rows(tiles)
            pieces = [
                exact_dot(
                    om[:, BLOCK * j : BLOCK * (j + 1)].astype(F32),
                    right[BLOCK * j : BLOCK * (j + 1)],
                    1,
                    0,
                )
                for j in range(local_blocks)
            ]
            mixed[:, :row_count] = start[...]
            mixed[:, row_count:] = jnp.concatenate(pieces, axis=1)

        def build_kernel(place, sizes, bits, scale, obs, left, tiles, x_out):
            right = right_rows(tiles)
            weight = weight_rows(scale, left).T
            batch = batch_ids(place, sizes, (row_count, BLOCK), 0)
            for j in range(local_blocks):
                at = slice(BLOCK * j, BLOCK * (j + 1))
                lowrank = exact_dot(weight, right[at], 1, 1)
                gone = gone_in(bits[place[0] % snp * local_blocks + j], batch)
                x_out[:, at] = jnp.where(gone, lowrank, obs[:, at].astype(F32)).astype(BF16)

        mixed = call_with_place(
            mix_kernel,
            shape_of((width, row_count + local_blocks * GROUP)),
            right_tiles,
            omega,
            start,
        )
        mixed_others = snp_others(mixed)
        left_rows = left_factors.T
        matrix = call_with_place(
            build_kernel,
            shape_of((row_count, col_width), BF16),
            observed,
            left_rows,
            right_tiles,
            scalars=(batch_sizes, bits, singular),
        )

        packed = row_count + 3 * width
        sum_width = col_width + LANES
        part_shape = shape_of((width // 2, sum_width))
        tile_shape = shape_of((SUB, sum_width))

        def split_kernel(place, mine, got, own, *sends):
            for k, ref in enumerate((own, *sends)):
                rows = pl.ds(pl.multiple_of((x_of(place) + k) % ring * SUB, SUB), SUB)
                ref[...] = mine[rows, :] + got[rows, :]

        def spread_kernel(place, own, a, b, c, out):
            total = own[...] + a[...] + b[...] + c[...]
            if out.dtype == BF16:
                columns, gram = total[:, :col_width], total[:, col_width : col_width + width]
                total = jnp.concatenate(
                    [
                        columns.astype(BF16),
                        *three_parts(gram),
                        jnp.zeros((SUB, out.shape[2] - col_width - 3 * width), BF16),
                    ],
                    axis=1,
                )
            out[...] = jnp.broadcast_to(total[None], out.shape)

        def gather_kernel(place, parts, out):
            total = jnp.sum(parts[...].astype(F32), axis=0)
            if parts.dtype == BF16:
                grams = [
                    total[:, col_width + width * i : col_width + width * (i + 1)]
                    for i in range(3)
                ]
                total = jnp.concatenate(
                    [
                        total[:, :col_width],
                        grams[0] + (grams[1] + grams[2]),
                        jnp.zeros((SUB, LANES - width), F32),
                    ],
                    axis=1,
                )
            out[...] = total

        def samp_sum(mine, other, dtype):
            own, *sends = call_with_place(
                split_kernel, (tile_shape,) * ring, mine, swap(other)
            )
            gots = [x_shift(sends[k - 1], k) for k in ((1, 3, 2) if dtype == F32 else SHIFTS)]
            wide = sum_width if dtype == F32 else col_width + 2 * LANES
            spread = call_with_place(
                spread_kernel, shape_of((depth, SUB, wide), dtype), own, *gots
            )
            tile = call_with_place(
                gather_kernel, tile_shape, lax.all_to_all(spread, "z", 0, 0)
            )
            near = [tile] + [x_shift(tile, k) for k in SHIFTS]
            return (*near, *[swap(value) for value in near])

        def read_sum(place, tiles, whole):
            for n, ref in enumerate(tiles):
                side = core_of(place) if n < ring else 1 - core_of(place)
                back = ring - (0, *SHIFTS)[n % ring]
                tile = side * ring + (x_of(place) + back) % ring
                whole[pl.ds(pl.multiple_of(tile * SUB, SUB), SUB), :] = ref[...]
            return whole[:, :col_width], whole[:, col_width : col_width + width]

        whole_scratch = [pltpu.VMEM((width, sum_width), F32)]

        def first_kernel(
            place, sizes, bits, scale, w0, w1, w2, w3, left, x, samples_out, mine, other
        ):
            batch = batch_ids(place, sizes, (1, row_count), 1)
            weight = weight_rows(scale, left)
            samples = jnp.zeros((width, row_count), F32)
            for k, ref in zip((0, *SHIFTS), (w0, w1, w2, w3)):
                source = (place[0] + (snp - k)) % snp
                masked = [
                    jnp.where(gone_in(bits[source * local_blocks + j], batch), weight, 0.0)
                    for j in range(local_blocks)
                ]
                missed = exact_dot(ref[:, row_count:], jnp.concatenate(masked, axis=0), 1, 0)
                samples = samples + (ref[:, :row_count] + missed)
            samples_out[...] = samples
            write_send(
                split_dot(samples, x[...], 0),
                exact_dot(samples, samples, 1, 1),
                core_of(place),
                mine,
                other,
            )

        def forward_kernel(place, *refs):
            tiles, (x, raw_out, product_out, gram_out, wire, whole) = refs[: 2 * ring], refs[2 * ring :]
            columns, gram = read_sum(place, tiles, whole)
            raw = exact_dot(inverse_factor(gram / sample_count, True), columns, 1, 0)
            raw_out[...] = raw
            product = split_dot(raw, x[...], 1)
            own = exact_dot(raw, raw, 1, 1)
            product_out[...] = product
            gram_out[...] = own
            wire[...] = jnp.concatenate([product.astype(BF16), *three_parts(own)], axis=1)

        def backward_kernel(
            place, product, gram, a, b, c, x, samples_out, factor_out, mine, other
        ):
            total, own = product[...], gram[...]
            for ref in (a, b, c):
                total = total + ref[:, :row_count].astype(F32)
                parts = [
                    ref[:, row_count + width * i : row_count + width * (i + 1)].astype(F32)
                    for i in range(3)
                ]
                own = own + (parts[0] + (parts[1] + parts[2]))
            factor = inverse_factor(own / snp_count, False)
            samples = exact_dot(factor, total, 1, 0)
            samples_out[...] = samples
            factor_out[...] = factor
            write_send(
                split_dot(samples, x[...], 0),
                exact_dot(samples, samples, 1, 1),
                core_of(place),
                mine,
                other,
            )

        def last_kernel(place, *refs):
            tiles, rest = refs[: 2 * ring], refs[2 * ring :]
            samples, upper, raw, basis, projection, snp_basis, whole = rest
            snp_basis[...] = exact_dot(upper[...], raw[...], 1, 0)
            columns, gram = read_sum(place, tiles, whole)
            factor = inverse_factor(gram / sample_count, True)
            basis[...] = exact_dot(factor, samples[...], 1, 0)
            projection[...] = exact_dot(factor / math.sqrt(sample_count), columns, 1, 0)

        samples_shape = shape_of((width, row_count))
        columns_shape = shape_of((width, col_width))
        samples, mine, other = call_with_place(
            first_kernel,
            (samples_shape, part_shape, part_shape),
            mixed,
            *mixed_others,
            left_rows,
            matrix,
            scalars=(batch_sizes, bits, singular),
        )
        def sweep(index, carry):
            raw, product, gram, wire = call_with_place(
                forward_kernel,
                (
                    columns_shape,
                    samples_shape,
                    shape_of((width, width)),
                    shape_of((width, packed), BF16),
                ),
                *carry[0],
                matrix,
                scratch=whole_scratch,
            )
            samples, factor, mine, other = call_with_place(
                backward_kernel,
                (samples_shape, shape_of((width, width)), part_shape, part_shape),
                product,
                gram,
                *snp_others(wire),
                matrix,
            )
            return samp_sum(mine, other, BF16), samples, factor, raw

        tiles, samples, factor, raw = lax.fori_loop(
            0,
            ITERS,
            sweep,
            (
                samp_sum(mine, other, F32),
                samples,
                jnp.zeros((width, width), F32),
                jnp.zeros(columns_shape.shape, F32),
            ),
        )
        basis, projection, columns = call_with_place(
            last_kernel,
            (samples_shape, columns_shape, columns_shape),
            *tiles,
            samples,
            factor,
            raw,
            scratch=whole_scratch,
        )
        return (basis.T, projection.T, columns.T)

    in_specs = (
        P(samp_axes, "snp"),
        P("snp"),
        P(samp_axes, None),
        P(),
        P(("snp", *samp_axes), None),
        P("snp", None),
        P(),
        P(),
        P(),
    )
    out_specs = (P(samp_axes, None), P("snp", None), P("snp", None))
    return jax.shard_map(
        on_device, mesh=fine, in_specs=in_specs, out_specs=out_specs, check_vma=False
    )
```

```python
import math

import jax
import jax.numpy as jnp
from jax import lax
from jax.experimental import pallas as pl
from jax.experimental.pallas import tpu as pltpu
from jax.sharding import Mesh, PartitionSpec as P

BATCHES = 12
BLOCK = 256
ITERS = 2
BLOCKS = 16
LANES = 128
SUB = 8
GROUP = 32
SHIFTS = (2, 1, 3)
F32 = jnp.float32
BF16 = jnp.bfloat16
HIGH = lax.Precision.HIGHEST


def exact_dot(a, b, a_dim, b_dim):
    return lax.dot_general(
        a, b, (((a_dim,), (b_dim,)), ((), ())), precision=HIGH, preferred_element_type=F32
    )


def split_dot(values, matrix, dim):
    high = values.astype(BF16)
    low = (values - high.astype(F32)).astype(BF16)
    both = jnp.concatenate([high, low], axis=0)
    out = lax.dot_general(
        both, matrix, (((1,), (dim,)), ((), ())), preferred_element_type=F32
    )
    rows = values.shape[0]
    return out[:rows] + out[rows:]


def inverse_factor(gram, lower):
    size = gram.shape[0]
    across = lax.broadcasted_iota(jnp.int32, (size, size), 1)
    down = lax.broadcasted_iota(jnp.int32, (size, size), 0)
    wide = jnp.concatenate([gram, (across == down).astype(F32)], axis=1)
    count = size // SUB
    shape = (SUB, 2 * size)
    tiles = [wide[SUB * t : SUB * (t + 1)] for t in range(count)]
    sub = lax.broadcasted_iota(jnp.int32, shape, 0)
    step = 1 if lower else -1

    def spread_row(value, k):
        return jnp.broadcast_to(value[k : k + 1], shape)

    for a in range(count)[::step]:
        active = range(a, count) if lower else range(a + 1)
        cols = {
            t: [
                jnp.broadcast_to(tiles[t][:, SUB * a + k : SUB * a + k + 1], shape)
                for k in range(SUB)
            ]
            for t in active
        }
        scale = jnp.zeros(shape, F32)
        order = range(SUB)[::step]
        for p, q in zip(order[::2], order[1::2]):
            aa, bb = spread_row(cols[a][p], p), spread_row(cols[a][p], q)
            cc = spread_row(cols[a][q], q)
            det = aa * cc - bb * bb
            inverse, first = 1.0 / det, 1.0 / aa
            ia, ib, ic = cc * inverse, bb * inverse, aa * inverse
            scale = jnp.where(sub == p, aa, jnp.where(sub == q, det * first, scale))
            keep = (sub > q) if lower else (sub < q)
            rest = [j for j in order if (j > q if lower else j < q)]

            def solved(value):
                vp, vq = spread_row(value, p), spread_row(value, q)
                return ia * vp - ib * vq, ic * vq - ib * vp

            row_p = spread_row(tiles[a], p)
            up, uq = solved(tiles[a])
            heads = {j: solved(cols[a][j]) for j in rest}
            for t in active:
                cp, cq = cols[t][p], cols[t][q]
                for j in rest:
                    cols[t][j] = cols[t][j] - (cp * heads[j][0] + cq * heads[j][1])
                if t == a:
                    inner = jnp.where(sub == q, bb * first, 0.0) * row_p
                    cp, cq = jnp.where(keep, cp, 0.0), jnp.where(keep, cq, 0.0)
                    tiles[t] = tiles[t] - (cp * up + cq * uq) - inner
                else:
                    tiles[t] = tiles[t] - (cp * up + cq * uq)
        tiles[a] = tiles[a] * lax.rsqrt(scale)
    return jnp.concatenate(tiles, axis=0)[:, size:]


def shape_of(shape, dtype=F32):
    return jax.ShapeDtypeStruct(shape, dtype)


def write_send(columns, gram, core, mine, other):
    rows = columns.shape[0]
    blank = jnp.zeros((rows, LANES - gram.shape[1]), F32)
    value = jnp.concatenate([columns, gram, blank], axis=1)
    top, bottom = value[: rows // 2], value[rows // 2 :]
    mine[...] = jnp.where(core == 0, top, bottom)
    other[...] = jnp.where(core == 0, bottom, top)


def three_parts(value):
    high = value.astype(BF16)
    rest = value - high.astype(F32)
    middle = rest.astype(BF16)
    return [high, middle, (rest - middle.astype(F32)).astype(BF16)]


def solution(mesh):
    samp, snp = mesh.shape["samp"], mesh.shape["snp"]
    chips, ring = samp // 2, 4
    depth = chips // ring
    fine = Mesh(mesh.devices.reshape(depth, ring, 2, snp), ("z", "x", "core", "snp"))
    samp_axes = ("z", "x", "core")

    def swap(value):
        return lax.ppermute(value, "core", [(0, 1), (1, 0)])

    def snp_others(value):
        return [
            lax.ppermute(value, "snp", [(i, (i + k) % snp) for i in range(snp)])
            for k in SHIFTS
        ]

    def x_shift(value, k):
        return lax.ppermute(value, "x", [(i, (i + k) % ring) for i in range(ring)])

    def on_device(
        genotype,
        freqs,
        left_factors,
        singular,
        right_factors,
        sketch,
        batch_sizes,
        missing_batch,
        missing_block,
    ):
        row_count, col_width = genotype.shape
        rank = left_factors.shape[1]
        width = sketch.shape[1]
        sample_count = row_count * samp
        snp_count = col_width * snp
        place = lax.axis_index((*samp_axes, "snp")).reshape(1).astype(jnp.int32)
        local_blocks = col_width // BLOCK
        omega = sketch.T

        def core_of(place):
            return place[0] // snp % 2

        def x_of(place):
            return place[0] // (snp * 2) % ring

        def call_with_place(body, outs, *operands, scalars=(), scratch=(), out_specs=None):
            smem = pl.BlockSpec(memory_space=pltpu.SMEM)
            specs = [smem] * (1 + len(scalars)) + [
                pl.BlockSpec(memory_space=pltpu.VMEM) for _ in operands
            ]
            return pl.pallas_call(
                body,
                out_shape=outs,
                in_specs=specs,
                scratch_shapes=scratch,
                **({} if out_specs is None else {"out_specs": out_specs}),
                compiler_params=pltpu.CompilerParams(vmem_limit_bytes=48 * 1024 * 1024),
            )(place, *scalars, *operands)

        def batch_ids(place, sizes, shape, axis):
            ids = lax.broadcasted_iota(jnp.int32, shape, axis) + place[0] // snp * row_count
            batch = jnp.zeros(shape, jnp.int32)
            end = jnp.int32(0)
            for b in range(BATCHES - 1):
                end = end + sizes[b]
                batch = batch + (ids >= end).astype(jnp.int32)
            return batch

        def gone_in(bits, batch):
            return ((jnp.broadcast_to(bits, batch.shape) >> batch) & 1) == 1

        chunk = LANES

        def observe_kernel(
            place, sizes_in, batch_in, block_in, geno_in, freq_in, om_in,
            obs, start, bits,
            sizes, tile_batch, tile_block, geno, freq, om, sems,
        ):
            copies = [
                pltpu.make_async_copy(source, target, sems.at[i])
                for i, (source, target) in enumerate(
                    [
                        (batch_in, tile_batch),
                        (block_in, tile_block),
                        (sizes_in, sizes),
                        (freq_in, freq),
                    ]
                    + [
                        (geno_in.at[pl.ds(low, chunk)], geno.at[pl.ds(low, chunk)])
                        for low in range(0, row_count, chunk)
                    ]
                    + [(om_in, om)]
                )
            ]
            for copy in copies:
                copy.start()
            for block in range(BLOCKS):
                bits[block] = 0
            copies[0].wait()
            copies[1].wait()
            for i in range(tile_batch.shape[0]):
                block = tile_block[i]
                bits[block] = bits[block] | (1 << tile_batch[i])
            copies[2].wait()
            copies[3].wait()
            batch = batch_ids(place, sizes, (row_count, LANES), 0)
            own_bits = [bits[place[0] % snp * local_blocks + j] for j in range(local_blocks)]
            for n, top in enumerate(range(0, row_count, chunk)):
                copies[4 + n].wait()
                rows = slice(top, top + chunk)
                for j in range(local_blocks):
                    gone = gone_in(own_bits[j], batch[rows])
                    for low in range(BLOCK * j, BLOCK * (j + 1), LANES):
                        at = slice(low, low + LANES)
                        values = geno[rows, at].astype(F32) - 2.0 * freq[:, at]
                        obs[rows, at] = jnp.where(gone, 0.0, values).astype(BF16)
            copies[-1].wait()
            start[...] = lax.dot_general(
                om[...], obs[...], (((1,), (1,)), ((), ())), preferred_element_type=F32
            )

        vmem = pl.BlockSpec(memory_space=pltpu.VMEM)
        smem = pl.BlockSpec(memory_space=pltpu.SMEM)
        tiles = missing_batch.shape
        observed, start, bits = pl.pallas_call(
            observe_kernel,
            out_shape=(
                shape_of((row_count, col_width), BF16),
                shape_of((width, row_count)),
                shape_of((BLOCKS,), jnp.int32),
            ),
            in_specs=[smem] + [pl.BlockSpec(memory_space=pltpu.HBM)] * 6,
            out_specs=(vmem, vmem, smem),
            scratch_shapes=[
                pltpu.SMEM(batch_sizes.shape, jnp.int32),
                pltpu.SMEM(tiles, jnp.int32),
                pltpu.SMEM(tiles, jnp.int32),
                pltpu.VMEM((row_count, col_width), jnp.int32),
                pltpu.VMEM((1, col_width), F32),
                pltpu.VMEM((width, col_width), BF16),
                pltpu.SemaphoreType.DMA((5 + row_count // chunk,)),
            ],
            compiler_params=pltpu.CompilerParams(vmem_limit_bytes=48 * 1024 * 1024),
        )(
            place,
            batch_sizes,
            missing_batch,
            missing_block,
            genotype,
            freqs.reshape(1, col_width),
            omega,
        )

        def pack_kernel(place, mine, other, spread):
            first = core_of(place) == 0
            low = jnp.where(first, mine[...], other[...])
            high = jnp.where(first, other[...], mine[...])
            fill = jnp.zeros((SUB, GROUP - rank), F32)
            pieces = []
            for part in (low, high):
                for top in range(0, part.shape[0], SUB):
                    pieces += [part[top : top + SUB], fill]
            tile = jnp.concatenate(pieces, axis=1)
            spread[...] = jnp.broadcast_to(tile[None], spread.shape)

        right_tiles = lax.all_to_all(
            call_with_place(
                pack_kernel,
                shape_of((chips, SUB, LANES)),
                right_factors,
                swap(right_factors),
            ),
            ("z", "x"),
            0,
            0,
        )

        def right_rows(tiles):
            value = tiles[...]
            parts = [value[:, :, g : g + GROUP] for g in range(0, LANES, GROUP)]
            return jnp.stack(parts, axis=1).reshape(col_width, GROUP)

        def weight_rows(scale, left):
            rows = [left[r : r + 1, :] * scale[r] for r in range(rank)]
            return jnp.concatenate(
                [*rows, jnp.zeros((GROUP - rank, row_count), F32)], axis=0
            )

        def mix_kernel(place, tiles, om, start, mixed):
            right = right_rows(tiles)
            pieces = [
                exact_dot(
                    om[:, BLOCK * j : BLOCK * (j + 1)].astype(F32),
                    right[BLOCK * j : BLOCK * (j + 1)],
                    1,
                    0,
                )
                for j in range(local_blocks)
            ]
            mixed[:, :row_count] = start[...]
            mixed[:, row_count:] = jnp.concatenate(pieces, axis=1)

        def build_kernel(place, sizes, bits, scale, obs, left, tiles, x_out):
            right = right_rows(tiles)
            weight = weight_rows(scale, left).T
            batch = batch_ids(place, sizes, (row_count, BLOCK), 0)
            for j in range(local_blocks):
                at = slice(BLOCK * j, BLOCK * (j + 1))
                lowrank = exact_dot(weight, right[at], 1, 1)
                gone = gone_in(bits[place[0] % snp * local_blocks + j], batch)
                x_out[:, at] = jnp.where(gone, lowrank, obs[:, at].astype(F32)).astype(BF16)

        mixed = call_with_place(
            mix_kernel,
            shape_of((width, row_count + local_blocks * GROUP)),
            right_tiles,
            omega,
            start,
        )
        mixed_others = snp_others(mixed)
        left_rows = left_factors.T
        matrix = call_with_place(
            build_kernel,
            shape_of((row_count, col_width), BF16),
            observed,
            left_rows,
            right_tiles,
            scalars=(batch_sizes, bits, singular),
        )

        packed = row_count + 3 * width
        sum_width = col_width + LANES
        part_shape = shape_of((width // 2, sum_width))
        tile_shape = shape_of((SUB, sum_width))

        def split_kernel(place, mine, got, own, *sends):
            for k, ref in enumerate((own, *sends)):
                rows = pl.ds(pl.multiple_of((x_of(place) + k) % ring * SUB, SUB), SUB)
                ref[...] = mine[rows, :] + got[rows, :]

        def spread_kernel(place, own, a, b, c, out):
            total = own[...] + a[...] + b[...] + c[...]
            if out.dtype == BF16:
                columns, gram = total[:, :col_width], total[:, col_width : col_width + width]
                total = jnp.concatenate(
                    [
                        columns.astype(BF16),
                        *three_parts(gram),
                        jnp.zeros((SUB, out.shape[2] - col_width - 3 * width), BF16),
                    ],
                    axis=1,
                )
            out[...] = jnp.broadcast_to(total[None], out.shape)

        def gather_kernel(place, parts, out):
            total = jnp.sum(parts[...].astype(F32), axis=0)
            if parts.dtype == BF16:
                grams = [
                    total[:, col_width + width * i : col_width + width * (i + 1)]
                    for i in range(3)
                ]
                total = jnp.concatenate(
                    [
                        total[:, :col_width],
                        grams[0] + (grams[1] + grams[2]),
                        jnp.zeros((SUB, LANES - width), F32),
                    ],
                    axis=1,
                )
            out[...] = total

        def samp_sum(mine, other, dtype):
            own, *sends = call_with_place(
                split_kernel, (tile_shape,) * ring, mine, swap(other)
            )
            gots = [x_shift(sends[k - 1], k) for k in ((1, 3, 2) if dtype == F32 else SHIFTS)]
            wide = sum_width if dtype == F32 else col_width + 2 * LANES
            spread = call_with_place(
                spread_kernel, shape_of((depth, SUB, wide), dtype), own, *gots
            )
            tile = call_with_place(
                gather_kernel, tile_shape, lax.all_to_all(spread, "z", 0, 0)
            )
            near = [tile] + [x_shift(tile, k) for k in SHIFTS]
            return (*near, *[swap(value) for value in near])

        def read_sum(place, tiles, whole):
            for n, ref in enumerate(tiles):
                side = core_of(place) if n < ring else 1 - core_of(place)
                back = ring - (0, *SHIFTS)[n % ring]
                tile = side * ring + (x_of(place) + back) % ring
                whole[pl.ds(pl.multiple_of(tile * SUB, SUB), SUB), :] = ref[...]
            return whole[:, :col_width], whole[:, col_width : col_width + width]

        whole_scratch = [pltpu.VMEM((width, sum_width), F32)]

        def first_kernel(
            place, sizes, bits, scale, w0, w1, w2, w3, left, x, samples_out, mine, other
        ):
            batch = batch_ids(place, sizes, (1, row_count), 1)
            weight = weight_rows(scale, left)
            samples = jnp.zeros((width, row_count), F32)
            for k, ref in zip((0, *SHIFTS), (w0, w1, w2, w3)):
                source = (place[0] + (snp - k)) % snp
                masked = [
                    jnp.where(gone_in(bits[source * local_blocks + j], batch), weight, 0.0)
                    for j in range(local_blocks)
                ]
                missed = exact_dot(ref[:, row_count:], jnp.concatenate(masked, axis=0), 1, 0)
                samples = samples + (ref[:, :row_count] + missed)
            samples_out[...] = samples
            write_send(
                split_dot(samples, x[...], 0),
                exact_dot(samples, samples, 1, 1),
                core_of(place),
                mine,
                other,
            )

        def forward_kernel(place, *refs):
            tiles, (x, raw_out, product_out, gram_out, wire, whole) = refs[: 2 * ring], refs[2 * ring :]
            columns, gram = read_sum(place, tiles, whole)
            raw = exact_dot(inverse_factor(gram / sample_count, True), columns, 1, 0)
            raw_out[...] = raw
            product = split_dot(raw, x[...], 1)
            own = exact_dot(raw, raw, 1, 1)
            product_out[...] = product
            gram_out[...] = own
            wire[...] = jnp.concatenate([product.astype(BF16), *three_parts(own)], axis=1)

        def backward_kernel(
            place, product, gram, a, b, c, x, samples_out, factor_out, mine, other
        ):
            total, own = product[...], gram[...]
            for ref in (a, b, c):
                total = total + ref[:, :row_count].astype(F32)
                parts = [
                    ref[:, row_count + width * i : row_count + width * (i + 1)].astype(F32)
                    for i in range(3)
                ]
                own = own + (parts[0] + (parts[1] + parts[2]))
            factor = inverse_factor(own / snp_count, False)
            samples = exact_dot(factor, total, 1, 0)
            samples_out[...] = samples
            factor_out[...] = factor
            write_send(
                split_dot(samples, x[...], 0),
                exact_dot(samples, samples, 1, 1),
                core_of(place),
                mine,
                other,
            )

        def last_kernel(place, *refs):
            tiles, rest = refs[: 2 * ring], refs[2 * ring :]
            samples, upper, raw, *outs = rest[:6]
            whole, *holds, sems = rest[6:]
            copies = [
                pltpu.make_async_copy(hold, out, sems.at[n])
                for n, (hold, out) in enumerate(zip(holds, outs))
            ]
            holds[2][...] = exact_dot(upper[...], raw[...], 1, 0)
            copies[2].start()
            columns, gram = read_sum(place, tiles, whole)
            factor = inverse_factor(gram / sample_count, True)
            holds[1][...] = exact_dot(factor / math.sqrt(sample_count), columns, 1, 0)
            copies[1].start()
            holds[0][...] = exact_dot(factor, samples[...], 1, 0)
            copies[0].start()
            for copy in copies:
                copy.wait()

        samples_shape = shape_of((width, row_count))
        columns_shape = shape_of((width, col_width))
        samples, mine, other = call_with_place(
            first_kernel,
            (samples_shape, part_shape, part_shape),
            mixed,
            *mixed_others,
            left_rows,
            matrix,
            scalars=(batch_sizes, bits, singular),
        )
        def sweep(index, carry):
            raw, product, gram, wire = call_with_place(
                forward_kernel,
                (
                    columns_shape,
                    samples_shape,
                    shape_of((width, width)),
                    shape_of((width, packed), BF16),
                ),
                *carry[0],
                matrix,
                scratch=whole_scratch,
            )
            samples, factor, mine, other = call_with_place(
                backward_kernel,
                (samples_shape, shape_of((width, width)), part_shape, part_shape),
                product,
                gram,
                *snp_others(wire),
                matrix,
            )
            return samp_sum(mine, other, BF16), samples, factor, raw

        tiles, samples, factor, raw = lax.fori_loop(
            0,
            ITERS,
            sweep,
            (
                samp_sum(mine, other, F32),
                samples,
                jnp.zeros((width, width), F32),
                jnp.zeros(columns_shape.shape, F32),
            ),
        )
        basis, projection, columns = call_with_place(
            last_kernel,
            (samples_shape, columns_shape, columns_shape),
            *tiles,
            samples,
            factor,
            raw,
            scratch=[
                *whole_scratch,
                pltpu.VMEM((width, row_count), F32),
                pltpu.VMEM((width, col_width), F32),
                pltpu.VMEM((width, col_width), F32),
                pltpu.SemaphoreType.DMA((3,)),
            ],
            out_specs=(pl.BlockSpec(memory_space=pltpu.HBM),) * 3,
        )
        return (basis.T, projection.T, columns.T)

    in_specs = (
        P(samp_axes, "snp"),
        P("snp"),
        P(samp_axes, None),
        P(),
        P(("snp", *samp_axes), None),
        P("snp", None),
        P(),
        P(),
        P(),
    )
    out_specs = (P(samp_axes, None), P("snp", None), P("snp", None))
    return jax.shard_map(
        on_device, mesh=fine, in_specs=in_specs, out_specs=out_specs, check_vma=False
    )
```
